32 devices in a mesh: ctx: 8 (over z, y), fsdp: 4 (over x, core).
Axes of the slice: x: 2, y: 2, z: 4, core: 2. Of those that a mesh axis runs over, the one named last changes fastest.
Arguments:
- tokens: bfloat16 [4, 4096, 1024], P('fsdp', 'ctx'), may hold values from -6 to 6
- block_pos: int32 [4, 16], P('fsdp'), may hold values from 0 to 15, each once within a row
- gain_attn: bfloat16 [1024], P('fsdp'), may hold values from 0.25 to 1.75
- w_query: bfloat16 [1024, 256], P('fsdp'), may hold values from -0.1875 to 0.1875
- w_key: bfloat16 [1024, 256], P('fsdp'), may hold values from -0.1875 to 0.1875
- w_value: bfloat16 [1024, 1024], P('fsdp'), may hold values from -0.1875 to 0.1875
- w_out: bfloat16 [1024, 1024], P('fsdp'), may hold values from -2 to 2
- gain_ffn: bfloat16 [1024], P('fsdp'), may hold values from 0.25 to 1.75
- w_gate: bfloat16 [1024, 2752], P('fsdp'), may hold values from -0.1875 to 0.1875
- w_up: bfloat16 [1024, 2752], P('fsdp'), may hold values from -0.1875 to 0.1875
- w_down: bfloat16 [2752, 1024], P('fsdp'), may hold values from -0.109375 to 0.109375
- cotangent: bfloat16 [4, 4096, 1024], P('fsdp', 'ctx'), may hold values from -6 to 6
Outputs:
- output: bfloat16 [4, 4096, 1024], P('fsdp', 'ctx')
- grad_tokens: float32 [4, 4096, 1024], P('fsdp', 'ctx')
- grad_gain_attn: float32 [1024], P('fsdp')
- grad_query: float32 [1024, 256], P('fsdp')
- grad_key: float32 [1024, 256], P('fsdp')
- grad_value: float32 [1024, 1024], P('fsdp')
- grad_out: float32 [1024, 1024], P('fsdp')
- grad_gain_ffn: float32 [1024], P('fsdp')
- grad_gate: float32 [1024, 2752], P('fsdp')
- grad_up: float32 [1024, 2752], P('fsdp')
- grad_down: float32 [2752, 1024], P('fsdp')
The draws below stay inside these ranges and needn't reach their ends.
Inputs may be any that keep to these rules, and one draw needn't show every extreme that they name: `block_pos`: each row is a permutation of the 16 position blocks of one sequence.
All inputs are finite; a program needn't handle non-finite values.
Results may differ from the reference program's by a relative error of at most 0.015.
Values may be sent and summed in bfloat16 or wider, within the bound.
A program may use at most 512 MiB of HBM per device.

```python
import jax
import jax.numpy as jnp
from jax import lax

D = 1024
FF = 2752
HEADS = 16
FDIM = 16
VDIM = 64
BLOCK = 256
LEN = 4096
SEQS = 4
NB = 16


def steps_of(own_key, shape, pieces, smallest, largest):
    def one(dim, shards_of):
        draws = jax.random.uniform(jax.random.fold_in(jax.random.fold_in(own_key, 6), dim), (shards_of,), jnp.float32, smallest / len(pieces), largest / len(pieces))
        return jnp.repeat(jnp.exp(draws), shape[dim] // shards_of).reshape((-1,) + (1,) * (len(shape) - dim - 1))

    gain = one(*pieces[0])
    for cut in pieces[1:]:
        gain = gain * one(*cut)
    return gain


def noise(key, extent, scale, most, pieces=(), dtype=jnp.bfloat16):
    entries = scale * jax.random.normal(key, extent, jnp.float32)
    if pieces:
        entries = entries * steps_of(key, extent, pieces, -0.22, 0.18)
    return jnp.clip(entries, -most, most).astype(dtype)


def setup_inputs(seed: int = 0) -> dict:
    key_list = jax.random.split(jax.random.key(seed), 13)
    return {
        "tokens": noise(key_list[0], (SEQS, LEN, D), 1.0, 6.0, ((0, 4), (1, 8))),
        "block_pos": jax.vmap(lambda own: jax.random.permutation(own, NB))(jax.random.split(key_list[1], SEQS)).reshape((SEQS, NB)).astype(jnp.int32),
        "gain_attn": jnp.clip(1.0 + 0.15 * jax.random.normal(key_list[2], (D,), jnp.float32), 0.25, 1.75).astype(jnp.bfloat16),
        "w_query": noise(key_list[3], (D, HEADS * FDIM), D ** -0.5, 0.1875, ((0, 4),)),
        "w_key": noise(key_list[4], (D, HEADS * FDIM), D ** -0.5, 0.1875, ((0, 4),)),
        "w_value": noise(key_list[5], (D, HEADS * VDIM), D ** -0.5, 0.1875, ((0, 4),)),
        "w_out": noise(key_list[6], (HEADS * VDIM, D), (max(1, HEADS * VDIM * 32 // LEN)) ** -0.5, 2.0, ((0, 4),)),
        "gain_ffn": jnp.clip(1.0 + 0.15 * jax.random.normal(key_list[7], (D,), jnp.float32), 0.25, 1.75).astype(jnp.bfloat16),
        "w_gate": noise(key_list[8], (D, FF), D ** -0.5, 0.1875, ((0, 4),)),
        "w_up": noise(key_list[9], (D, FF), D ** -0.5, 0.1875, ((0, 4),)),
        "w_down": noise(key_list[10], (FF, D), FF ** -0.5, 0.109375, ((0, 4),)),
        "cotangent": noise(key_list[11], (SEQS, LEN, D), 1.0, 6.0, ((0, 4), (1, 8))),
    }


@jax.custom_vjp
def low(v):
    return lax.optimization_barrier(v.astype(jnp.bfloat16)).astype(jnp.float32)

@jax.custom_vjp
def low_back(v):
    return v

def low_keep(v):
    return (low(v), None)

def low_pass(kept, grad):
    return (grad,)

def back_keep(v):
    return (v, None)

def back_low(kept, grad):
    return (low(grad),)
low.defvjp(low_keep, low_pass)
low_back.defvjp(back_keep, back_low)
highest = lax.Precision.HIGHEST
eps_norm = 1e-05
root_half = 0.7071067811865476

def features(scaled):
    outer_prod = scaled[..., :, None] * scaled[..., None, :]
    flattened = outer_prod.reshape(scaled.shape[:-1] + (scaled.shape[-1] * scaled.shape[-1],)) * root_half
    constant = jnp.ones(scaled.shape[:-1] + (1,), jnp.float32)
    return jnp.concatenate([constant, scaled, flattened], axis=-1)

def rms_scale(values, gain_vector):
    return values * lax.rsqrt(lax.optimization_barrier(jnp.mean(values * values, axis=-1, keepdims=True)) + eps_norm) * gain_vector

def mix_sequence(residual, positions, weights):
    gain_attn, w_query, w_key, w_value, w_out, gain_ffn, w_gate, w_up, w_down = weights
    block_total = LEN // BLOCK
    normed_one = low(rms_scale(residual, gain_attn))
    queries = low_back(low(jnp.dot(normed_one, w_query, precision=highest)))
    keys_all = low_back(low(jnp.dot(normed_one, w_key, precision=highest)))
    values_all = low_back(low(jnp.dot(normed_one, w_value, precision=highest)))
    query_scaled = queries.reshape(block_total, BLOCK, HEADS, FDIM) * 0.5
    key_scaled = keys_all.reshape(block_total, BLOCK, HEADS, FDIM) * 0.5
    value_blocks = values_all.reshape(block_total, BLOCK, HEADS, VDIM)
    phi_query = low(features(query_scaled))
    phi_key = low(features(key_scaled))
    block_states = jnp.einsum('nthf,nthv->nhfv', phi_key, value_blocks, precision=highest)
    block_norms = lax.optimization_barrier(jnp.sum(phi_key, axis=1))
    earlier = (positions[None, :] < positions[:, None]).astype(jnp.float32)
    prefix = jnp.einsum('ib,bhfv->ihfv', earlier, block_states, precision=highest)
    prefix_norm = jnp.einsum('ib,bhf->ihf', earlier, block_norms, precision=highest)
    scores = low_back(jnp.einsum('nshf,nthf->nhst', query_scaled, key_scaled, precision=highest))
    kernel = 1.0 + scores + 0.5 * scores * scores
    numerator = low_back(jnp.einsum('nhst,nthv->nshv', low(kernel), value_blocks, precision=highest) + jnp.einsum('nshf,nhfv->nshv', phi_query, prefix, precision=highest))
    denominator = low_back(jnp.transpose(lax.optimization_barrier(jnp.sum(kernel, axis=-1)), (0, 2, 1)) + jnp.einsum('nshf,nhf->nsh', phi_query, prefix_norm, precision=highest))
    attention = low((numerator / denominator[..., None]).reshape(LEN, HEADS * VDIM))
    middle = residual + low_back(jnp.dot(attention, w_out, precision=highest))
    normed_two = low(rms_scale(middle, gain_ffn))
    gate_pre = low_back(jnp.dot(normed_two, w_gate, precision=highest))
    up_pre = low_back(jnp.dot(normed_two, w_up, precision=highest))
    hidden = low(jax.nn.silu(gate_pre) * up_pre)
    return middle + jnp.dot(hidden, w_down, precision=highest)

def reference(tokens, block_pos, gain_attn, w_query, w_key, w_value, w_out, gain_ffn, w_gate, w_up, w_down, cotangent):
    weights = tuple((weight_arg.astype(jnp.float32) for weight_arg in (gain_attn, w_query, w_key, w_value, w_out, gain_ffn, w_gate, w_up, w_down)))
    inputs = tokens.astype(jnp.float32)

    def forward(inputs_now, weights_now):

        def per_sequence(sequence_args):
            return jax.checkpoint(mix_sequence)(sequence_args[0], sequence_args[1], weights_now)
        return lax.map(per_sequence, (inputs_now, block_pos))
    result, pullback = jax.vjp(forward, inputs, weights)
    grad_inputs, grad_weights = pullback(cotangent.astype(jnp.float32))
    return (result.astype(jnp.bfloat16), grad_inputs, grad_weights[0], grad_weights[1], grad_weights[2], grad_weights[3], grad_weights[4], grad_weights[5], grad_weights[6], grad_weights[7], grad_weights[8])
```

```python
import jax
import jax.numpy as jnp
from jax import lax
from jax.experimental import pallas as pl
from jax.experimental.pallas import tpu as pltpu
from jax.sharding import PartitionSpec as P

HEADS = 16
FDIM = 16
VDIM = 64
BLOCK = 256
GROUP = 8
FEAT = 160
STATE = GROUP // 2 * FEAT + 2 * GROUP
EPS = 1e-05
ROOT_HALF = 0.7071067811865476

f32 = jnp.float32
bf16 = jnp.bfloat16


def dims(lhs, rhs):
    return (((lhs,), (rhs,)), ((), ()))


def dot(lhs, rhs, contract):
    return lax.dot_general(lhs, rhs, dims(*contract), preferred_element_type=f32)


def turned(u, shift):
    return pltpu.roll(u, FDIM - shift, 0)


def features(u, pair_weight):
    rows = [u, u * u * ROOT_HALF]
    for shift in range(1, 8):
        rows.append(u * turned(u, shift) * ROOT_HALF)
    rows.append(u[:8] * u[8:] * ROOT_HALF)
    one = (lax.broadcasted_iota(jnp.int32, (8, u.shape[1]), 0) == 0).astype(f32)
    linear = jnp.concatenate(rows[:2], axis=0).astype(bf16)
    pairs = jnp.concatenate(rows[2:], axis=0).astype(bf16) * pair_weight
    del rows
    return jnp.concatenate([linear.astype(f32), pairs.astype(f32), one], axis=0).astype(bf16)


def features_back(u, g):
    total = g[:16] + (2.0 * ROOT_HALF) * (g[16:32] * u)
    for shift in range(1, 8):
        here = (2.0 * ROOT_HALF) * g[16 + 16 * shift : 32 + 16 * shift]
        total = total + here * turned(u, shift) + pltpu.roll(here * u, shift, 0)
    here = (2.0 * ROOT_HALF) * g[144:152]
    return total + jnp.concatenate([here * u[8:], here * u[:8]], axis=0)


def halved(ref, head):
    return ref[head * FDIM : (head + 1) * FDIM, :].astype(f32) * 0.5


def write_states(out_ref, feat, value_pair, weight_row, head):
    pair = head // 2
    product = dot(feat, value_pair, (1, 1))
    half = slice(0, 64) if head % 2 == 0 else slice(64, 128)
    out_ref[0, 0, pair * FEAT : (pair + 1) * FEAT, half] = product[:, half].astype(bf16)
    norm = dot(weight_row, feat, (1, 1))
    base = GROUP // 2 * FEAT + 2 * head
    out_ref[0, 0, base : base + 1, :] = norm[:1, :128].astype(bf16)
    out_ref[0, 0, base + 1 : base + 2, :] = jnp.concatenate([norm[:1, 128:], jnp.zeros((1, 96), f32)], axis=1).astype(bf16)


def norm_row(state_ref, head):
    base = GROUP // 2 * FEAT + 2 * head
    return state_ref[0, 0, base : base + 1, :], state_ref[0, 0, base + 1 : base + 2, :32]


def head_state(state_ref, head):
    pair = head // 2
    return state_ref[0, 0, pair * FEAT : (pair + 1) * FEAT, 64 * (head % 2) : 64 * (head % 2) + 64]


def states_kernel(key_ref, value_ref, out_ref):
    ones = jnp.ones((8, BLOCK), bf16)
    for head in range(GROUP):
        feat = features(halved(key_ref, head), 1.0)
        pair = head // 2
        write_states(out_ref, feat, value_ref[pair * 128 : (pair + 1) * 128, :], ones, head)


def intra_kernel(query_ref, key_ref, value_ref, numer_ref, denom_ref):
    for head in range(GROUP):
        rows = slice(head * FDIM, (head + 1) * FDIM)
        wide = slice(head * VDIM, (head + 1) * VDIM)
        scores = dot(key_ref[rows, :], query_ref[rows, :], (0, 0)) * 0.25
        kernel = 1.0 + scores + 0.5 * scores * scores
        denom_ref[head : head + 1, :] = jnp.sum(kernel, axis=0, keepdims=True)
        numer_ref[wide, :] = dot(value_ref[wide, :], kernel.astype(bf16), (1, 0))


def inter_kernel(query_ref, prefix_ref, numer_ref, denom_in_ref, atten_ref, denom_ref):
    for head in range(GROUP):
        wide = slice(head * VDIM, (head + 1) * VDIM)
        feat = features(halved(query_ref, head), 2.0)
        numer = numer_ref[wide, :] + dot(head_state(prefix_ref, head), feat, (0, 0))
        first, second = norm_row(prefix_ref, head)
        denom = denom_in_ref[head : head + 1, :] + dot(first, feat[:128], (1, 0)) + dot(second, feat[128:], (1, 0))
        denom_ref[head : head + 1, :] = denom
        atten_ref[wide, :] = (numer / denom).astype(bf16)


def grad_states_kernel(query_ref, atten_ref, denom_ref, grad_ref, gnumer_ref, gdenom_ref, out_ref):
    for pair in range(GROUP // 2):
        for head in (2 * pair, 2 * pair + 1):
            wide = slice(head * VDIM, (head + 1) * VDIM)
            denom = denom_ref[head : head + 1, :]
            grad = grad_ref[wide, :]
            gnumer_ref[wide, :] = (grad / denom).astype(bf16)
            gdenom = -jnp.sum(grad * atten_ref[wide, :].astype(f32), axis=0, keepdims=True) / denom
            gdenom_ref[head : head + 1, :] = gdenom.astype(bf16).astype(f32)
        for head in (2 * pair, 2 * pair + 1):
            feat = features(halved(query_ref, head), 1.0)
            weights = jnp.broadcast_to(gdenom_ref[head : head + 1, :], (8, BLOCK)).astype(bf16)
            write_states(out_ref, feat, gnumer_ref[pair * 128 : (pair + 1) * 128, :], weights, head)


def intra_back_kernel(
    query_ref, key_ref, value_ref, gnumer_ref, gdenom_ref, prefix_ref, gquery_ref, gkey_ref, gvalue_ref
):
    for head in range(GROUP):
        rows = slice(head * FDIM, (head + 1) * FDIM)
        wide = slice(head * VDIM, (head + 1) * VDIM)
        query, key = query_ref[rows, :], key_ref[rows, :]
        gnumer = gnumer_ref[wide, :]
        gdenom = gdenom_ref[head : head + 1, :]
        scores = dot(key, query, (0, 0)) * 0.25
        kernel = (1.0 + scores + 0.5 * scores * scores).astype(bf16)
        gkernel = dot(value_ref[wide, :], gnumer, (0, 0)) + gdenom
        gscores = ((1.0 + scores) * gkernel).astype(bf16)
        gvalue_ref[wide, :] = dot(gnumer, kernel, (1, 1))
        gkey_ref[rows, :] = dot(query, gscores, (1, 1)) * 0.25
        first, second = norm_row(prefix_ref, head)
        gdenom_low = gdenom.astype(bf16)
        outer_prod = jnp.concatenate([dot(first, gdenom_low, (0, 0)), dot(second, gdenom_low, (0, 0))], axis=0)
        gfeat = dot(head_state(prefix_ref, head), gnumer, (1, 0)) + outer_prod
        gquery = dot(key, gscores, (1, 0)) * 0.25 + 0.5 * features_back(halved(query_ref, head), gfeat)
        gquery_ref[rows, :] = gquery.astype(bf16)


def inter_back_kernel(key_ref, value_ref, later_ref, gkey_in_ref, gvalue_in_ref, gkey_ref, gvalue_ref):
    ones = jnp.ones((1, BLOCK), bf16)
    for head in range(GROUP):
        rows = slice(head * FDIM, (head + 1) * FDIM)
        wide = slice(head * VDIM, (head + 1) * VDIM)
        u = halved(key_ref, head)
        state = head_state(later_ref, head)
        first, second = norm_row(later_ref, head)
        outer_prod = jnp.concatenate([dot(first, ones, (0, 0)), dot(second, ones, (0, 0))], axis=0)
        gfeat = dot(state, value_ref[wide, :], (1, 0)) + outer_prod
        gkey_ref[rows, :] = (gkey_in_ref[rows, :] + 0.5 * features_back(u, gfeat)).astype(bf16)
        feat = features(u, 2.0)
        gvalue_ref[wide, :] = (gvalue_in_ref[wide, :] + dot(state, feat, (0, 0))).astype(bf16)


def attention_call(kernel, ins, outs, tokens, flops):
    blocks = tokens // BLOCK
    groups = HEADS // GROUP
    forms = {
        "narrow": ((GROUP * FDIM, BLOCK), lambda b, g: (g, b), (HEADS * FDIM, tokens)),
        "wide": ((GROUP * VDIM, BLOCK), lambda b, g: (g, b), (HEADS * VDIM, tokens)),
        "head": ((GROUP, BLOCK), lambda b, g: (g, b), (HEADS, tokens)),
        "state": ((1, 1, STATE, 128), lambda b, g: (b, g, 0, 0), (blocks, groups, STATE, 128)),
    }

    def spec(name):
        return pl.BlockSpec(forms[name][0], forms[name][1])

    def call(*arrays):
        moved = sum(a.size * a.dtype.itemsize for a in arrays)
        return pl.pallas_call(
            kernel,
            out_shape=[jax.ShapeDtypeStruct(forms[name][2], dtype) for name, dtype in outs],
            grid=(blocks, groups),
            in_specs=[spec(name) for name in ins],
            out_specs=[spec(name) for name, _ in outs],
            compiler_params=pltpu.CompilerParams(vmem_limit_bytes=40 << 20),
            cost_estimate=pl.CostEstimate(flops=flops, bytes_accessed=2 * moved, transcendentals=0),
        )(*arrays)

    return call


ORDER = (0, 2, 1, 3)


def place(step):
    return (step % 2) * 2 + step // 2


def ffn_kernel(me_ref, middle_ref, gain_ref, cot_ref, *refs):
    gates, ups, downs = refs[:4], refs[4:8], refs[8:12]
    output_ref, gmiddle_ref, branch_ref, ggain_ref = refs[12:16]
    gate_keep, gate_send, up_keep, up_send, down_keep, down_send = refs[16:22]
    normed, x_own, x_turned, cot_turned, down, total, gnormed = refs[22:]
    step = pl.program_id(0)
    me = me_ref[0]
    width = gates[0].shape[1]

    def columns(r):
        return pl.ds(pl.multiple_of((me ^ r) * width, width), width)

    def inverse():
        middle = middle_ref[...]
        return lax.rsqrt(jnp.mean(middle * middle, axis=-1, keepdims=True) + EPS)

    @pl.when(step == 0)
    def _():
        normed[...] = (middle_ref[...] * inverse() * gain_ref[...]).astype(bf16)
        for r in range(4):
            part = normed[:, columns(r)]
            x_own[:, r * width : (r + 1) * width] = part
            x_turned[r * width : (r + 1) * width, :] = part.T
        cot_turned[...] = cot_ref[...].T
        total[...] = jnp.zeros_like(total)
        gnormed[...] = jnp.zeros_like(gnormed)

    for at in range(4):

        @pl.when(step == at)
        def _(at=at):
            down[...] = downs[ORDER[at]][...]

    gate = dot(gates[0][...], x_turned[:width, :], (1, 0))
    up = dot(ups[0][...], x_turned[:width, :], (1, 0))
    for r in range(1, 4):
        x_part = x_turned[r * width : (r + 1) * width, :]
        gate = gate + dot(gates[r][...], x_part, (1, 0))
        up = up + dot(ups[r][...], x_part, (1, 0))
    ghidden = dot(down[...], cot_turned[...], (1, 0))
    sigmoid = jax.nn.sigmoid(gate)
    silu = gate * sigmoid
    hidden = (silu * up).astype(bf16)
    ggate = (ghidden * up * (sigmoid * (1.0 + gate * (1.0 - sigmoid)))).astype(bf16)
    gup = (ghidden * silu).astype(bf16)
    total[...] += dot(hidden, down[...], (0, 0))
    gdown = dot(hidden, cot_ref[...], (1, 0)).astype(bf16)

    @pl.when(step < 2)
    def _():
        down_keep[0] = gdown

    @pl.when(step >= 2)
    def _():
        down_send[0] = gdown

    for r in range(4):
        part = slice(r * width, (r + 1) * width)
        gnormed[:, part] += dot(ggate, gates[r][...], (0, 0)) + dot(gup, ups[r][...], (0, 0))
        x_part = x_own[:, part]
        (gate_send if r % 2 else gate_keep)[r // 2] = dot(ggate, x_part, (1, 0)).astype(bf16)
        (up_send if r % 2 else up_keep)[r // 2] = dot(gup, x_part, (1, 0)).astype(bf16)

    @pl.when(step == 3)
    def _():
        for r in range(4):
            gmiddle_ref[:, columns(r)] = gnormed[:, r * width : (r + 1) * width]
        middle, inv, cot = middle_ref[...], inverse(), cot_ref[...].astype(f32)
        grad = gmiddle_ref[...]
        output_ref[...] = (middle + total[...]).astype(bf16)
        ggain_ref[...] = jnp.broadcast_to(jnp.sum(grad * middle * inv, axis=0, keepdims=True), ggain_ref.shape)
        weighted = grad * gain_ref[...]
        slope = jnp.mean(weighted * middle, axis=-1, keepdims=True)
        gmiddle = cot + inv * weighted - middle * (inv * inv * inv) * slope
        gmiddle_ref[...] = gmiddle
        branch_ref[...] = gmiddle.astype(bf16)


def ffn_call(me, middle, gain, cot, gates, ups, downs):
    rows, model = middle.shape
    hidden, width = gates[0].shape
    tile = downs[0].shape[0]
    once = pl.Buffered(1)

    def whole(shape, **kw):
        return pl.BlockSpec(shape, lambda s, me: (0,) * len(shape), **kw)

    piece = pl.BlockSpec((tile, width), lambda s, me: (me[0] ^ place(s), 0))
    pair = pl.BlockSpec((2, tile, width), lambda s, me: (0, me[0] ^ place(s), 0))
    pair_shape = jax.ShapeDtypeStruct((2, hidden, width), bf16)
    down_shape = jax.ShapeDtypeStruct((2, tile, model), bf16)
    return pl.pallas_call(
        ffn_kernel,
        out_shape=[
            jax.ShapeDtypeStruct((rows, model), bf16),
            jax.ShapeDtypeStruct((rows, model), f32),
            jax.ShapeDtypeStruct((rows, model), bf16),
            jax.ShapeDtypeStruct((8, model), f32),
            pair_shape,
            pair_shape,
            pair_shape,
            pair_shape,
            down_shape,
            down_shape,
        ],
        grid_spec=pltpu.PrefetchScalarGridSpec(
            num_scalar_prefetch=1,
            grid=(4,),
            in_specs=[whole((rows, model), pipeline_mode=once), whole((1, model)), whole((rows, model), pipeline_mode=once)]
            + [piece] * 8
            + [whole((tile, model), pipeline_mode=once)] * 4,
            out_specs=[
                whole((rows, model), pipeline_mode=once),
                whole((rows, model), pipeline_mode=once),
                whole((rows, model), pipeline_mode=once),
                whole((8, model)),
                pair,
                pair,
                pair,
                pair,
                pl.BlockSpec((1, tile, model), lambda s, me: (jnp.minimum(s, 1), 0, 0)),
                pl.BlockSpec((1, tile, model), lambda s, me: (jnp.maximum(s - 2, 0), 0, 0)),
            ],
            scratch_shapes=[
                pltpu.VMEM((rows, model), bf16),
                pltpu.VMEM((rows, model), bf16),
                pltpu.VMEM((model, rows), bf16),
                pltpu.VMEM((model, rows), bf16),
                pltpu.VMEM((tile, model), bf16),
                pltpu.VMEM((rows, model), f32),
                pltpu.VMEM((rows, model), f32),
            ],
        ),
        compiler_params=pltpu.CompilerParams(vmem_limit_bytes=58 << 20),
        cost_estimate=pl.CostEstimate(
            flops=18 * rows * model * hidden, bytes_accessed=14 * hidden * model, transcendentals=0
        ),
    )(me, middle, gain, cot, *gates, *ups, *downs)


def out_grad_kernel(me_ref, atten_ref, branch_ref, keep_ref, send_ref):
    grad = dot(atten_ref[...], branch_ref[...], (1, 0)).astype(bf16)

    @pl.when(pl.program_id(0) < 2)
    def _():
        keep_ref[0] = grad

    @pl.when(pl.program_id(0) >= 2)
    def _():
        send_ref[0] = grad


def in_grad_kernel(me_ref, normed_ref, query_ref, key_ref, value_ref, gain_ref, keep_ref, send_ref):
    x = normed_ref[...].T
    parts = [dot(x, ref[...], (1, 1)) for ref in (query_ref, key_ref, value_ref)]
    grad = jnp.concatenate(parts + [gain_ref[...]], axis=1).astype(bf16)

    @pl.when(pl.program_id(0) < 2)
    def _():
        keep_ref[0] = grad

    @pl.when(pl.program_id(0) >= 2)
    def _():
        send_ref[0] = grad


def shard_grads(kernel, me, moving, moving_axis, fixed, also, width):
    size = moving.shape[moving_axis] // 4
    block = list(moving.shape)
    block[moving_axis] = size
    if moving_axis == 0:
        spec = pl.BlockSpec(tuple(block), lambda s, me: (me[0] ^ place(s), 0))
    else:
        spec = pl.BlockSpec(tuple(block), lambda s, me: (0, me[0] ^ place(s)))
    extra = [pl.BlockSpec((size, a.shape[1]), lambda s, me: (me[0] ^ place(s), 0)) for a in also]
    steady = [pl.BlockSpec(a.shape, lambda s, me: (0, 0)) for a in fixed]
    shape = jax.ShapeDtypeStruct((2, size, width), bf16)
    tokens = moving.shape[1 - moving_axis]
    return pl.pallas_call(
        kernel,
        out_shape=[shape, shape],
        grid_spec=pltpu.PrefetchScalarGridSpec(
            num_scalar_prefetch=1,
            grid=(4,),
            in_specs=[spec] + steady + extra,
            out_specs=[
                pl.BlockSpec((1, size, width), lambda s, me: (jnp.minimum(s, 1), 0, 0)),
                pl.BlockSpec((1, size, width), lambda s, me: (jnp.maximum(s - 2, 0), 0, 0)),
            ],
        ),
        compiler_params=pltpu.CompilerParams(vmem_limit_bytes=40 << 20),
        cost_estimate=pl.CostEstimate(
            flops=8 * tokens * size * width, bytes_accessed=16 * size * width, transcendentals=0
        ),
    )(me, moving, *fixed, *also)


CORE = [(0, 1), (1, 0), (2, 3), (3, 2)]
CHIP = [(0, 2), (2, 0), (1, 3), (3, 1)]


def pieces(shard, after=None):
    crossing = shard if after is None else lax.optimization_barrier((shard, after))[0]
    far = lax.ppermute(crossing, "fsdp", CHIP)
    return shard, lax.ppermute(shard, "fsdp", CORE), far, lax.ppermute(far, "fsdp", CORE)


def ordered(parts, place_bits):
    for bit in (1, 2):
        swap = (place_bits & bit) != 0
        parts = [jnp.where(swap, parts[j ^ bit], parts[j]) for j in range(4)]
    return parts


def summed(keep, send, own, count, axis):
    got = lax.ppermute(send, "fsdp", CORE)
    cross = (keep[1].astype(f32) + got[1].astype(f32)).astype(bf16)
    got_cross = lax.ppermute(cross, "fsdp", CHIP)
    total = keep[0].astype(f32) + got[0].astype(f32) + got_cross.astype(f32)
    if count != 8:
        return lax.psum(total.astype(bf16), "ctx").astype(f32)
    size = total.shape[axis]
    y, z = own % 2, own // 2

    def cut(array, index, parts):
        part = array.shape[axis] // parts
        return lax.dynamic_slice_in_dim(array, index * part, part, axis)

    def trade(array, bits):
        return lax.ppermute(array, "ctx", [(i, i ^ bits) for i in range(count)])

    got_half = trade(cut(total, 1 - y, 2).astype(bf16), 1)
    half = cut(total, y, 2) + got_half.astype(f32)
    mine = cut(half, z, 4)
    for k in (1, 2, 3):
        mine = mine + trade(cut(half, z ^ k, 4).astype(bf16), 2 * k).astype(f32)
    mine = mine.astype(bf16)
    near = [mine] + [trade(mine, 2 * k) for k in (1, 2, 3)]
    far = trade(jnp.concatenate(near, axis=axis), 1)
    far = [cut(far, k, 4) for k in range(4)]
    low = [jnp.where(y == 0, a, b) for a, b in zip(near, far)]
    high = [jnp.where(y == 0, b, a) for a, b in zip(near, far)]
    return jnp.concatenate(ordered(low, z) + ordered(high, z), axis=axis).astype(f32)


def masked_sums(pieces, masks, dtype):
    total = None
    for index, piece in enumerate(pieces):
        for block in range(piece.shape[0]):
            term = masks[:, index, block][:, None, None, None] * piece[block].astype(f32)[None]
            total = term if total is None else total + term
    return total.astype(dtype)


def exchange(own_states, positions, own, count, later):
    local = own_states.shape[0]
    table = positions.reshape(count, local)

    def mask(target, sources):
        there = table[target][:, None, None]
        here = table[jnp.stack(sources)][None]
        return ((here > there) if later else (here < there)).astype(f32)

    pieces, sources = [own_states], [own]
    for step in range(1, count // 2):
        pieces.append(lax.ppermute(pieces[-1], "ctx", [(i, (i + 2) % count) for i in range(count)]))
        sources.append((own - 2 * step) % count)
    partner = own ^ 1
    for_partner = masked_sums(pieces, mask(partner, sources), bf16)
    received = lax.ppermute(for_partner, "ctx", [(i, i ^ 1) for i in range(count)])
    return (masked_sums(pieces, mask(own, sources), f32) + received.astype(f32)).astype(bf16)


def body(count):
    def layer(
        tokens, block_pos, gain_attn, w_query, w_key, w_value, w_out, gain_ffn, w_gate, w_up, w_down, cotangent
    ):
        gather = lambda a: lax.all_gather(a, "fsdp", axis=0, tiled=True)
        own = lax.axis_index("ctx")
        me = lax.axis_index("fsdp").astype(jnp.int32).reshape(1)
        positions = block_pos[0]
        gains = gather(jnp.stack([gain_attn, gain_ffn], axis=1)).astype(f32)
        gain_one, gain_two = gains[:, 0], gains[:, 1]
        in_full = gather(jnp.concatenate([w_query, w_key, w_value], axis=1))
        gates = pieces(w_gate.T, in_full)
        ups = pieces(w_up.T, in_full)
        downs = pieces(w_down, gates[2])
        out_full = gather(w_out)
        residual = tokens[0].astype(f32)
        rows = residual.shape[0]
        inv_one = lax.rsqrt(jnp.mean(residual * residual, axis=-1, keepdims=True) + EPS)
        normed_one = (residual * inv_one * gain_one).astype(bf16)
        narrow = HEADS * FDIM
        projected = dot(in_full, normed_one, (0, 1)).astype(bf16)
        query, key, value = projected[:narrow], projected[narrow : 2 * narrow], projected[2 * narrow :]

        unit = 2 * rows * BLOCK * HEADS
        (own_states,) = attention_call(
            states_kernel, ("narrow", "wide"), (("state", bf16),), rows, unit * FEAT
        )(key, value)
        numer, denom = attention_call(
            intra_kernel, ("narrow", "narrow", "wide"), (("wide", f32), ("head", f32)), rows, unit * 256
        )(query, key, value)
        prefix = exchange(own_states, positions, own, count, False)
        atten, denom = attention_call(
            inter_kernel, ("narrow", "state", "wide", "head"), (("wide", bf16), ("head", f32)), rows, unit * FEAT
        )(query, prefix, numer, denom)

        middle = residual + dot(atten, out_full, (0, 0))
        results = ffn_call(me, middle, gain_two.reshape(1, -1), cotangent[0], gates, ups, downs)
        output, grad_middle, branch, grad_gain_two = results[:4]
        gate_keep, gate_send, up_keep, up_send, down_keep, down_send = results[4:]
        grad_atten = dot(out_full, branch, (1, 1))

        gnumer, gdenom, grad_states = attention_call(
            grad_states_kernel,
            ("narrow", "wide", "head", "wide"),
            (("wide", bf16), ("head", f32), ("state", bf16)),
            rows,
            unit * FEAT,
        )(query, atten, denom, grad_atten)
        gquery, gkey, gvalue = attention_call(
            intra_back_kernel,
            ("narrow", "narrow", "wide", "wide", "head", "state"),
            (("narrow", bf16), ("narrow", f32), ("wide", f32)),
            rows,
            unit * 512,
        )(query, key, value, gnumer, gdenom, prefix)
        later = exchange(grad_states, positions, own, count, True)
        gkey, gvalue = attention_call(
            inter_back_kernel,
            ("narrow", "wide", "state", "narrow", "wide"),
            (("narrow", bf16), ("wide", bf16)),
            rows,
            unit * 256,
        )(key, value, later, gkey, gvalue)
        gprojected = jnp.concatenate([gquery, gkey, gvalue], axis=0)
        gnormed_one = dot(gprojected, in_full, (0, 1))
        weighted_one = gnormed_one * gain_one
        grad_gain_one = jnp.sum(gnormed_one * residual * inv_one, axis=0)
        grad_tokens = (
            grad_middle
            + inv_one * weighted_one
            - residual * (inv_one * inv_one * inv_one) * jnp.mean(weighted_one * residual, axis=-1, keepdims=True)
        )[None]
        grad_gains = jnp.pad(jnp.stack([grad_gain_one, grad_gain_two[0]], axis=1), ((0, 0), (0, 126)))

        width = in_full.shape[1]
        out_keep, out_send = shard_grads(out_grad_kernel, me, atten, 0, [branch], [], branch.shape[1])
        in_keep, in_send = shard_grads(
            in_grad_kernel, me, normed_one, 1, [gquery, gkey, gvalue], [grad_gains], width + 128
        )
        down_grad = summed(down_keep, down_send, own, count, 1)
        gate_grad = summed(gate_keep, gate_send, own, count, 0).T
        up_grad = summed(up_keep, up_send, own, count, 0).T
        out_grad = summed(out_keep, out_send, own, count, 0)
        in_grad = summed(in_keep, in_send, own, count, 0)
        return (
            output[None],
            grad_tokens,
            in_grad[:, width],
            in_grad[:, :narrow],
            in_grad[:, narrow : 2 * narrow],
            in_grad[:, 2 * narrow : width],
            out_grad,
            in_grad[:, width + 1],
            gate_grad,
            up_grad,
            down_grad,
        )

    return layer


def solution(mesh):
    rows = P("fsdp", None)
    seqs = P("fsdp", "ctx", None)
    vec = P("fsdp")
    in_specs = (seqs, rows, vec, rows, rows, rows, rows, vec, rows, rows, rows, seqs)
    out_specs = (seqs, seqs, vec, rows, rows, rows, rows, vec, rows, rows, rows)
    return jax.shard_map(
        body(mesh.shape["ctx"]), mesh=mesh, in_specs=in_specs, out_specs=out_specs, check_vma=False
    )
```

```python
import jax
import jax.numpy as jnp
from jax import lax
from jax.experimental import pallas as pl
from jax.experimental.pallas import tpu as pltpu
from jax.sharding import PartitionSpec as P

HEADS = 16
FDIM = 16
VDIM = 64
BLOCK = 256
GROUP = 8
FEAT = 160
STATE = GROUP // 2 * FEAT + 2 * GROUP
EPS = 1e-05
ROOT_HALF = 0.7071067811865476

f32 = jnp.float32
bf16 = jnp.bfloat16


def dims(lhs, rhs):
    return (((lhs,), (rhs,)), ((), ()))


def dot(lhs, rhs, contract):
    return lax.dot_general(lhs, rhs, dims(*contract), preferred_element_type=f32)


def turned(u, shift):
    return pltpu.roll(u, FDIM - shift, 0)


def features(u, pair_weight):
    rows = [u, u * u * ROOT_HALF]
    for shift in range(1, 8):
        rows.append(u * turned(u, shift) * ROOT_HALF)
    rows.append(u[:8] * u[8:] * ROOT_HALF)
    one = (lax.broadcasted_iota(jnp.int32, (8, u.shape[1]), 0) == 0).astype(f32)
    linear = jnp.concatenate(rows[:2], axis=0).astype(bf16)
    pairs = jnp.concatenate(rows[2:], axis=0).astype(bf16) * pair_weight
    del rows
    return jnp.concatenate([linear.astype(f32), pairs.astype(f32), one], axis=0).astype(bf16)


def features_back(u, g):
    total = g[:16] + (2.0 * ROOT_HALF) * (g[16:32] * u)
    for shift in range(1, 8):
        here = (2.0 * ROOT_HALF) * g[16 + 16 * shift : 32 + 16 * shift]
        total = total + here * turned(u, shift) + pltpu.roll(here * u, shift, 0)
    here = (2.0 * ROOT_HALF) * g[144:152]
    return total + jnp.concatenate([here * u[8:], here * u[:8]], axis=0)


def halved(ref, head):
    return ref[head * FDIM : (head + 1) * FDIM, :].astype(f32) * 0.5


def write_states(out_ref, feat, value_pair, weight_row, head):
    pair = head // 2
    product = dot(feat, value_pair, (1, 1))
    half = slice(0, 64) if head % 2 == 0 else slice(64, 128)
    out_ref[0, 0, pair * FEAT : (pair + 1) * FEAT, half] = product[:, half].astype(bf16)
    norm = dot(weight_row, feat, (1, 1))
    base = GROUP // 2 * FEAT + 2 * head
    out_ref[0, 0, base : base + 1, :] = norm[:1, :128].astype(bf16)
    out_ref[0, 0, base + 1 : base + 2, :] = jnp.concatenate([norm[:1, 128:], jnp.zeros((1, 96), f32)], axis=1).astype(bf16)


def norm_row(state_ref, head):
    base = GROUP // 2 * FEAT + 2 * head
    return state_ref[0, 0, base : base + 1, :], state_ref[0, 0, base + 1 : base + 2, :32]


def head_state(state_ref, head):
    pair = head // 2
    return state_ref[0, 0, pair * FEAT : (pair + 1) * FEAT, 64 * (head % 2) : 64 * (head % 2) + 64]


def states_kernel(key_ref, value_ref, out_ref):
    ones = jnp.ones((8, BLOCK), bf16)
    for head in range(GROUP):
        feat = features(halved(key_ref, head), 1.0)
        pair = head // 2
        write_states(out_ref, feat, value_ref[pair * 128 : (pair + 1) * 128, :], ones, head)


def intra_kernel(query_ref, key_ref, value_ref, numer_ref, denom_ref):
    for head in range(GROUP):
        rows = slice(head * FDIM, (head + 1) * FDIM)
        wide = slice(head * VDIM, (head + 1) * VDIM)
        scores = dot(key_ref[rows, :], query_ref[rows, :], (0, 0)) * 0.25
        kernel = 1.0 + scores + 0.5 * scores * scores
        denom_ref[head : head + 1, :] = jnp.sum(kernel, axis=0, keepdims=True)
        numer_ref[wide, :] = dot(value_ref[wide, :], kernel.astype(bf16), (1, 0))


def inter_kernel(query_ref, prefix_ref, numer_ref, denom_in_ref, atten_ref, denom_ref):
    for head in range(GROUP):
        wide = slice(head * VDIM, (head + 1) * VDIM)
        feat = features(halved(query_ref, head), 2.0)
        numer = numer_ref[wide, :] + dot(head_state(prefix_ref, head), feat, (0, 0))
        first, second = norm_row(prefix_ref, head)
        denom = denom_in_ref[head : head + 1, :] + dot(first, feat[:128], (1, 0)) + dot(second, feat[128:], (1, 0))
        denom_ref[head : head + 1, :] = denom
        atten_ref[wide, :] = (numer / denom).astype(bf16)


def grad_states_kernel(query_ref, atten_ref, denom_ref, grad_ref, gnumer_ref, gdenom_ref, out_ref):
    for pair in range(GROUP // 2):
        for head in (2 * pair, 2 * pair + 1):
            wide = slice(head * VDIM, (head + 1) * VDIM)
            denom = denom_ref[head : head + 1, :]
            grad = grad_ref[wide, :]
            gnumer_ref[wide, :] = (grad / denom).astype(bf16)
            gdenom = -jnp.sum(grad * atten_ref[wide, :].astype(f32), axis=0, keepdims=True) / denom
            gdenom_ref[head : head + 1, :] = gdenom.astype(bf16).astype(f32)
        for head in (2 * pair, 2 * pair + 1):
            feat = features(halved(query_ref, head), 1.0)
            weights = jnp.broadcast_to(gdenom_ref[head : head + 1, :], (8, BLOCK)).astype(bf16)
            write_states(out_ref, feat, gnumer_ref[pair * 128 : (pair + 1) * 128, :], weights, head)


def intra_back_kernel(
    query_ref, key_ref, value_ref, gnumer_ref, gdenom_ref, prefix_ref, gquery_ref, gkey_ref, gvalue_ref
):
    for head in range(GROUP):
        rows = slice(head * FDIM, (head + 1) * FDIM)
        wide = slice(head * VDIM, (head + 1) * VDIM)
        query, key = query_ref[rows, :], key_ref[rows, :]
        gnumer = gnumer_ref[wide, :]
        gdenom = gdenom_ref[head : head + 1, :]
        scores = dot(key, query, (0, 0)) * 0.25
        kernel = (1.0 + scores + 0.5 * scores * scores).astype(bf16)
        gkernel = dot(value_ref[wide, :], gnumer, (0, 0)) + gdenom
        gscores = ((1.0 + scores) * gkernel).astype(bf16)
        gvalue_ref[wide, :] = dot(gnumer, kernel, (1, 1))
        gkey_ref[rows, :] = dot(query, gscores, (1, 1)) * 0.25
        first, second = norm_row(prefix_ref, head)
        gdenom_low = gdenom.astype(bf16)
        outer_prod = jnp.concatenate([dot(first, gdenom_low, (0, 0)), dot(second, gdenom_low, (0, 0))], axis=0)
        gfeat = dot(head_state(prefix_ref, head), gnumer, (1, 0)) + outer_prod
        gquery = dot(key, gscores, (1, 0)) * 0.25 + 0.5 * features_back(halved(query_ref, head), gfeat)
        gquery_ref[rows, :] = gquery.astype(bf16)


def inter_back_kernel(key_ref, value_ref, later_ref, gkey_in_ref, gvalue_in_ref, gkey_ref, gvalue_ref):
    ones = jnp.ones((1, BLOCK), bf16)
    for head in range(GROUP):
        rows = slice(head * FDIM, (head + 1) * FDIM)
        wide = slice(head * VDIM, (head + 1) * VDIM)
        u = halved(key_ref, head)
        state = head_state(later_ref, head)
        first, second = norm_row(later_ref, head)
        outer_prod = jnp.concatenate([dot(first, ones, (0, 0)), dot(second, ones, (0, 0))], axis=0)
        gfeat = dot(state, value_ref[wide, :], (1, 0)) + outer_prod
        gkey_ref[rows, :] = (gkey_in_ref[rows, :] + 0.5 * features_back(u, gfeat)).astype(bf16)
        feat = features(u, 2.0)
        gvalue_ref[wide, :] = (gvalue_in_ref[wide, :] + dot(state, feat, (0, 0))).astype(bf16)


def attention_call(kernel, ins, outs, tokens, flops):
    blocks = tokens // BLOCK
    groups = HEADS // GROUP
    forms = {
        "narrow": ((GROUP * FDIM, BLOCK), lambda b, g: (g, b), (HEADS * FDIM, tokens)),
        "wide": ((GROUP * VDIM, BLOCK), lambda b, g: (g, b), (HEADS * VDIM, tokens)),
        "head": ((GROUP, BLOCK), lambda b, g: (g, b), (HEADS, tokens)),
        "state": ((1, 1, STATE, 128), lambda b, g: (b, g, 0, 0), (blocks, groups, STATE, 128)),
    }

    def spec(name):
        return pl.BlockSpec(forms[name][0], forms[name][1])

    def call(*arrays):
        moved = sum(a.size * a.dtype.itemsize for a in arrays)
        return pl.pallas_call(
            kernel,
            out_shape=[jax.ShapeDtypeStruct(forms[name][2], dtype) for name, dtype in outs],
            grid=(blocks, groups),
            in_specs=[spec(name) for name in ins],
            out_specs=[spec(name) for name, _ in outs],
            compiler_params=pltpu.CompilerParams(vmem_limit_bytes=40 << 20),
            cost_estimate=pl.CostEstimate(flops=flops, bytes_accessed=2 * moved, transcendentals=0),
        )(*arrays)

    return call


ORDER = (0, 2, 1, 3)


def place(step):
    return (step % 2) * 2 + step // 2


def ffn_kernel(me_ref, middle_ref, gain_ref, cot_ref, gates, ups, downs, *refs):
    output_ref, gmiddle_ref, branch_ref, ggain_ref = refs[:4]
    gate_keep, gate_send, up_keep, up_send, down_keep, down_send = refs[4:10]
    normed, x_own, x_turned, cot_turned, total, gnormed = refs[10:]
    step = pl.program_id(0)
    me = me_ref[0]
    width = gates.shape[2]

    def inverse():
        middle = middle_ref[...]
        return lax.rsqrt(jnp.mean(middle * middle, axis=-1, keepdims=True) + EPS)

    @pl.when(step == 0)
    def _():
        normed[...] = (middle_ref[...] * inverse() * gain_ref[...]).astype(bf16)
        for r in range(4):
            x_own[r] = normed[:, pl.ds(pl.multiple_of((me ^ r) * width, width), width)]
        x_turned[...] = normed[...].T
        cot_turned[...] = cot_ref[...].T
        total[...] = jnp.zeros_like(total)
        gnormed[...] = jnp.zeros_like(gnormed)

    x_part = x_turned[:width, :]
    gate = dot(gates[0], x_part, (1, 0))
    up = dot(ups[0], x_part, (1, 0))
    for r in range(1, 4):
        x_part = x_turned[r * width : (r + 1) * width, :]
        gate = gate + dot(gates[r], x_part, (1, 0))
        up = up + dot(ups[r], x_part, (1, 0))
    down = downs[0]
    ghidden = dot(down, cot_turned[...], (1, 0))
    sigmoid = jax.nn.sigmoid(gate)
    silu = gate * sigmoid
    hidden = (silu * up).astype(bf16)
    ggate = (ghidden * up * (sigmoid * (1.0 + gate * (1.0 - sigmoid)))).astype(bf16)
    gup = (ghidden * silu).astype(bf16)
    total[...] += dot(hidden, down, (0, 0))
    gdown = dot(hidden, cot_ref[...], (1, 0)).astype(bf16)

    @pl.when(step < 2)
    def _():
        down_keep[0] = gdown

    @pl.when(step >= 2)
    def _():
        down_send[0] = gdown

    for r in range(4):
        part = slice(r * width, (r + 1) * width)
        gnormed[:, part] += dot(ggate, gates[r], (0, 0)) + dot(gup, ups[r], (0, 0))
        (gate_send if r % 2 else gate_keep)[r // 2] = dot(ggate, x_own[r], (1, 0)).astype(bf16)
        (up_send if r % 2 else up_keep)[r // 2] = dot(gup, x_own[r], (1, 0)).astype(bf16)

    @pl.when(step == 3)
    def _():
        middle, inv, cot = middle_ref[...], inverse(), cot_ref[...].astype(f32)
        grad = gnormed[...]
        output_ref[...] = (middle + total[...]).astype(bf16)
        ggain_ref[...] = jnp.broadcast_to(jnp.sum(grad * middle * inv, axis=0, keepdims=True), ggain_ref.shape)
        weighted = grad * gain_ref[...]
        slope = jnp.mean(weighted * middle, axis=-1, keepdims=True)
        gmiddle = cot + inv * weighted - middle * (inv * inv * inv) * slope
        gmiddle_ref[...] = gmiddle
        branch_ref[...] = gmiddle.astype(bf16)


def ffn_call(me, middle, gain, cot, gates, ups, downs):
    rows, model = middle.shape
    _, hidden, width = gates.shape
    tile = downs.shape[1]
    once = pl.Buffered(1)

    def whole(shape, **kw):
        return pl.BlockSpec(shape, lambda s, me: (0,) * len(shape), **kw)

    columns = pl.BlockSpec((4, tile, width), lambda s, me: (0, me[0] ^ place(s), 0))
    pair = pl.BlockSpec((2, tile, width), lambda s, me: (0, me[0] ^ place(s), 0))
    pair_shape = jax.ShapeDtypeStruct((2, hidden, width), bf16)
    down_shape = jax.ShapeDtypeStruct((2, tile, model), bf16)
    return pl.pallas_call(
        ffn_kernel,
        out_shape=[
            jax.ShapeDtypeStruct((rows, model), bf16),
            jax.ShapeDtypeStruct((rows, model), f32),
            jax.ShapeDtypeStruct((rows, model), bf16),
            jax.ShapeDtypeStruct((8, model), f32),
            pair_shape,
            pair_shape,
            pair_shape,
            pair_shape,
            down_shape,
            down_shape,
        ],
        grid_spec=pltpu.PrefetchScalarGridSpec(
            num_scalar_prefetch=1,
            grid=(4,),
            in_specs=[
                whole((rows, model), pipeline_mode=once),
                whole((1, model)),
                whole((rows, model), pipeline_mode=once),
                columns,
                columns,
                pl.BlockSpec((1, tile, model), lambda s, me: (me[0] ^ place(s), 0, 0)),
            ],
            out_specs=[
                whole((rows, model), pipeline_mode=once),
                whole((rows, model), pipeline_mode=once),
                whole((rows, model), pipeline_mode=once),
                whole((8, model)),
                pair,
                pair,
                pair,
                pair,
                pl.BlockSpec((1, tile, model), lambda s, me: (jnp.minimum(s, 1), 0, 0)),
                pl.BlockSpec((1, tile, model), lambda s, me: (jnp.maximum(s - 2, 0), 0, 0)),
            ],
            scratch_shapes=[
                pltpu.VMEM((rows, model), bf16),
                pltpu.VMEM((4, rows, width), bf16),
                pltpu.VMEM((model, rows), bf16),
                pltpu.VMEM((model, rows), bf16),
                pltpu.VMEM((rows, model), f32),
                pltpu.VMEM((rows, model), f32),
            ],
        ),
        compiler_params=pltpu.CompilerParams(vmem_limit_bytes=58 << 20),
        cost_estimate=pl.CostEstimate(
            flops=18 * rows * model * hidden, bytes_accessed=14 * hidden * model, transcendentals=0
        ),
    )(me, middle, gain, cot, gates, ups, downs)


def out_grad_kernel(me_ref, atten_ref, branch_ref, keep_ref, send_ref):
    grad = dot(atten_ref[...], branch_ref[...], (1, 0)).astype(bf16)

    @pl.when(pl.program_id(0) < 2)
    def _():
        keep_ref[0] = grad

    @pl.when(pl.program_id(0) >= 2)
    def _():
        send_ref[0] = grad


def in_grad_kernel(me_ref, normed_ref, query_ref, key_ref, value_ref, gain_ref, keep_ref, send_ref):
    x = normed_ref[...].T
    parts = [dot(x, ref[...], (1, 1)) for ref in (query_ref, key_ref, value_ref)]
    grad = jnp.concatenate(parts + [gain_ref[...]], axis=1).astype(bf16)

    @pl.when(pl.program_id(0) < 2)
    def _():
        keep_ref[0] = grad

    @pl.when(pl.program_id(0) >= 2)
    def _():
        send_ref[0] = grad


def shard_grads(kernel, me, moving, moving_axis, fixed, also, width):
    size = moving.shape[moving_axis] // 4
    block = list(moving.shape)
    block[moving_axis] = size
    if moving_axis == 0:
        spec = pl.BlockSpec(tuple(block), lambda s, me: (me[0] ^ place(s), 0))
    else:
        spec = pl.BlockSpec(tuple(block), lambda s, me: (0, me[0] ^ place(s)))
    extra = [pl.BlockSpec((size, a.shape[1]), lambda s, me: (me[0] ^ place(s), 0)) for a in also]
    steady = [pl.BlockSpec(a.shape, lambda s, me: (0, 0)) for a in fixed]
    shape = jax.ShapeDtypeStruct((2, size, width), bf16)
    tokens = moving.shape[1 - moving_axis]
    return pl.pallas_call(
        kernel,
        out_shape=[shape, shape],
        grid_spec=pltpu.PrefetchScalarGridSpec(
            num_scalar_prefetch=1,
            grid=(4,),
            in_specs=[spec] + steady + extra,
            out_specs=[
                pl.BlockSpec((1, size, width), lambda s, me: (jnp.minimum(s, 1), 0, 0)),
                pl.BlockSpec((1, size, width), lambda s, me: (jnp.maximum(s - 2, 0), 0, 0)),
            ],
        ),
        compiler_params=pltpu.CompilerParams(vmem_limit_bytes=40 << 20),
        cost_estimate=pl.CostEstimate(
            flops=8 * tokens * size * width, bytes_accessed=16 * size * width, transcendentals=0
        ),
    )(me, moving, *fixed, *also)


CORE = [(0, 1), (1, 0), (2, 3), (3, 2)]
CHIP = [(0, 2), (2, 0), (1, 3), (3, 1)]


class Links:
    def __init__(self):
        self.last = ()

    def round(self, sends, beside=()):
        arrays = [send[0] for send in sends]
        if self.last:
            arrays = lax.optimization_barrier((*arrays, *self.last))[: len(arrays)]
        results = [lax.ppermute(a, axis, perm) for a, (_, axis, perm) in zip(arrays, sends)]
        self.last = (*results, *beside)
        return results


def trade(array, bits, count):
    return array, "ctx", [(i, i ^ bits) for i in range(count)]


def ordered(parts, place_bits):
    for bit in (1, 2):
        swap = (place_bits & bit) != 0
        parts = [jnp.where(swap, parts[j ^ bit], parts[j]) for j in range(4)]
    return parts


def cut(array, index, parts, axis):
    part = array.shape[axis] // parts
    return lax.dynamic_slice_in_dim(array, index * part, part, axis)


MESH = pl.DeviceIdType.MESH


class Spot:
    def __init__(self):
        self.me = lax.axis_index("fsdp")
        self.own = lax.axis_index("ctx")
        self.core = {"fsdp": self.me + 1 - 2 * (self.me % 2)}
        self.across = (self.me + 2) % 4
        self.chip = {"fsdp": self.across}
        self.y = self.own % 2
        self.z = self.own // 2
        self.side = {"ctx": self.own + 1 - 2 * self.y}
        self.ahead = [None] + [{"ctx": (self.own + 2 * k) % 8} for k in (1, 2, 3)]

    def greet(self, neighbours):
        barrier = pltpu.get_barrier_semaphore()
        for neighbour in neighbours:
            pl.semaphore_signal(barrier, inc=1, device_id=neighbour, device_id_type=MESH)
        pl.semaphore_wait(barrier, len(neighbours))


class Wire:
    def __init__(self, send_sems, recv_sems, local_sems):
        self.send_sems, self.recv_sems, self.local_sems = send_sems, recv_sems, local_sems
        self.sent, self.local = [], []

    def send(self, source, target, device):
        k = len(self.sent)
        copy = pltpu.make_async_remote_copy(
            src_ref=source,
            dst_ref=target,
            send_sem=self.send_sems.at[k],
            recv_sem=self.recv_sems.at[k],
            device_id=device,
            device_id_type=MESH,
        )
        copy.start()
        self.sent.append(copy)
        return copy

    def keep(self, source, target):
        copy = pltpu.make_async_copy(source, target, self.local_sems.at[len(self.local)])
        copy.start()
        self.local.append(copy)
        return copy

    def end(self):
        for copy in self.sent:
            copy.wait_send()


class Gather:
    def __init__(self, wire, spot, shard, full, axis):
        self.wire, self.spot, self.full, self.axis = wire, spot, full, axis
        me = spot.me
        self.own = wire.keep(shard, full.at[me])
        self.cross = wire.send(self.half(shard, spot.y), self.half(full.at[me], spot.y), spot.chip)
        self.near = wire.send(shard, full.at[me], spot.core)

    def half(self, ref, y):
        size = ref.shape[self.axis] // 2
        index = [slice(None)] * 2
        index[self.axis] = pl.ds(pl.multiple_of(y * size, size), size)
        return ref.at[tuple(index)]

    def relay(self):
        self.cross.wait_recv()
        part = self.half(self.full.at[self.spot.across], self.spot.y)
        self.side = self.wire.send(part, part, self.spot.side)
        self.far = [self.wire.send(part, part, self.spot.core)]

    def relay_other(self):
        self.side.wait_recv()
        part = self.half(self.full.at[self.spot.across], 1 - self.spot.y)
        self.far.append(self.wire.send(part, part, self.spot.core))

    def end(self):
        self.own.wait()
        self.near.wait_recv()
        for copy in self.far:
            copy.wait_recv()


def gather_kernel(gain_ref, in_ref, gain_full, in_full, send_sems, recv_sems, local_sems):
    spot = Spot()
    wire = Wire(send_sems, recv_sems, local_sems)
    spot.greet([spot.core, spot.chip, spot.side])
    own = wire.keep(gain_ref, gain_full.at[spot.me])
    near = wire.send(gain_ref, gain_full.at[spot.me], spot.core)
    cross = wire.send(gain_ref, gain_full.at[spot.me], spot.chip)
    weight = Gather(wire, spot, in_ref, in_full, 0)
    cross.wait_recv()
    far = wire.send(gain_full.at[spot.across], gain_full.at[spot.across], spot.core)
    weight.relay()
    weight.relay_other()
    own.wait()
    near.wait_recv()
    far.wait_recv()
    weight.end()
    wire.end()


def add_masked(total, piece, mask_ref, source, block, first):
    for group in range(piece.shape[0]):
        states = piece[group].astype(f32)
        for target in range(4):
            term = states * mask_ref[target, 2 * source + block]
            if first:
                total[target, group] = term
            else:
                total[target, group] += term


def forward_kernel(
    mask_ref, states_ref, query_ref, key_ref, value_ref, *refs
):
    weights, (prefix_ref, numer_ref, denom_ref), fulls = refs[:4], refs[4:7], refs[7:11]
    ring, total, outgoing, incoming, send_sems, recv_sems, local_sems = refs[11:]
    spot = Spot()
    wire = Wire(send_sems, recv_sems, local_sems)
    spot.greet([spot.core, spot.chip, spot.side, spot.ahead[1], spot.ahead[3]])
    hops = [[wire.send(states_ref.at[b], ring.at[0, b], spot.ahead[1]) for b in range(2)]]
    gathers = [Gather(wire, spot, w, full, axis) for w, full, axis in zip(weights, fulls, (0, 0, 0, 1))]
    for block in range(2):
        for group in range(HEADS // GROUP):
            narrow = (slice(group * GROUP * FDIM, (group + 1) * GROUP * FDIM), slice(block * BLOCK, (block + 1) * BLOCK))
            wide = (slice(group * GROUP * VDIM, (group + 1) * GROUP * VDIM), narrow[1])
            heads = (slice(group * GROUP, (group + 1) * GROUP), narrow[1])
            intra_kernel(
                query_ref.at[narrow], key_ref.at[narrow], value_ref.at[wide], numer_ref.at[wide], denom_ref.at[heads]
            )
            if group == 1:
                hops[0][block].wait_recv()
                hops.append([]) if block == 0 else None
                hops[1].append(wire.send(ring.at[0, block], ring.at[1, block], spot.ahead[1]))
            if (block, group) == (1, 0):
                gathers[0].relay()
    for block in range(2):
        add_masked(total, states_ref.at[block], mask_ref, 0, block, block == 0)
        add_masked(total, ring.at[0, block], mask_ref, 1, block, False)
    gathers[1].relay()
    gathers[0].relay_other()
    hops.append([])
    for block in range(2):
        hops[1][block].wait_recv()
        hops[2].append(wire.send(ring.at[1, block], ring.at[2, block], spot.ahead[1]))
        add_masked(total, ring.at[1, block], mask_ref, 2, block, False)
    gathers[2].relay()
    gathers[1].relay_other()
    for block in range(2):
        hops[2][block].wait_recv()
        add_masked(total, ring.at[2, block], mask_ref, 3, block, False)
    outgoing[...] = total[2:].astype(bf16)
    partner = wire.send(outgoing, incoming, spot.side)
    gathers[3].relay()
    gathers[2].relay_other()
    partner.wait_recv()
    prefix_ref[...] = (total[:2] + incoming[...].astype(f32)).astype(bf16)
    gathers[3].relay_other()
    for one in gathers:
        one.end()
    wire.end()


HBM = pl.BlockSpec(memory_space=pltpu.HBM)
VMEM = pl.BlockSpec(memory_space=pltpu.VMEM)
SMEM = pl.BlockSpec(memory_space=pltpu.SMEM)


def sems(count):
    return pltpu.SemaphoreType.DMA((count,))


def gather_call(gains, in_shard):
    return pl.pallas_call(
        gather_kernel,
        out_shape=[jax.ShapeDtypeStruct((4, *a.shape), a.dtype) for a in (gains, in_shard)],
        in_specs=[HBM, HBM],
        out_specs=[HBM, HBM],
        scratch_shapes=[sems(8), sems(8), sems(2)],
        compiler_params=pltpu.CompilerParams(collective_id=0, has_side_effects=True, vmem_limit_bytes=16 << 20),
    )(gains, in_shard)


def forward_call(masks, states, query, key, value, weights):
    state = states.shape
    rows = query.shape[1]
    return pl.pallas_call(
        forward_kernel,
        out_shape=[
            jax.ShapeDtypeStruct(state, bf16),
            jax.ShapeDtypeStruct((HEADS * VDIM, rows), f32),
            jax.ShapeDtypeStruct((HEADS, rows), f32),
        ]
        + [jax.ShapeDtypeStruct((4, *w.shape), bf16) for w in weights],
        in_specs=[SMEM, VMEM, VMEM, VMEM, VMEM] + [HBM] * 4,
        out_specs=[VMEM, VMEM, VMEM] + [HBM] * 4,
        scratch_shapes=[
            pltpu.VMEM((3, *state), bf16),
            pltpu.VMEM((4, *state[1:]), f32),
            pltpu.VMEM(state, bf16),
            pltpu.VMEM(state, bf16),
            sems(28),
            sems(28),
            sems(4),
        ],
        compiler_params=pltpu.CompilerParams(collective_id=1, has_side_effects=True, vmem_limit_bytes=40 << 20),
    )(masks, states, query, key, value, *weights)


class Shard:
    def __init__(self, keep, send, own, rows, y_axis, z_axis):
        self.keep, self.whole_send, self.rows = keep, send, rows
        self.y, self.z, self.y_axis, self.z_axis = own % 2, own // 2, y_axis, z_axis

    def cross(self, got):
        start, stop = self.rows
        self.got = got
        return (self.keep[1, start:stop].astype(f32) + got[1, start:stop].astype(f32)).astype(bf16), "fsdp", CHIP

    def chip_sum(self, got_cross):
        start, stop = self.rows
        return self.keep[0, start:stop].astype(f32) + self.got[0, start:stop].astype(f32) + got_cross.astype(f32)

    def y_scatter(self, got_cross):
        self.total = self.chip_sum(got_cross)
        return [trade(cut(self.total, 1 - self.y, 2, self.y_axis).astype(bf16), 1, 8)]

    def z_scatter(self, got):
        self.half = cut(self.total, self.y, 2, self.y_axis) + got[0].astype(f32)
        return [trade(cut(self.half, self.z ^ k, 4, self.z_axis).astype(bf16), 2 * k, 8) for k in (1, 2, 3)]

    def z_gather(self, got):
        mine = cut(self.half, self.z, 4, self.z_axis)
        for part in got:
            mine = mine + part.astype(f32)
        self.mine = mine.astype(bf16)
        return [trade(self.mine, 2 * k, 8) for k in (1, 2, 3)]

    def y_gather(self, got):
        self.parts = [self.mine, *got]
        return [trade(jnp.concatenate(self.parts, axis=self.z_axis), 1, 8)]

    def result(self, got):
        far = [cut(got[0], k, 4, self.z_axis) for k in range(4)]
        low = [jnp.where(self.y == 0, a, b) for a, b in zip(self.parts, far)]
        high = [jnp.where(self.y == 0, b, a) for a, b in zip(self.parts, far)]
        sides = [jnp.concatenate(ordered(side, self.z), axis=self.z_axis) for side in (low, high)]
        return jnp.concatenate(sides, axis=self.y_axis).astype(f32)


def masked_sums(pieces, masks, dtype):
    total = None
    for index, piece in enumerate(pieces):
        for block in range(piece.shape[0]):
            term = masks[:, index, block][:, None, None, None] * piece[block].astype(f32)[None]
            total = term if total is None else total + term
    return total.astype(dtype)


class Exchange:
    def __init__(self, states, positions, own, count, later):
        self.pieces, self.sources, self.own, self.count, self.later = [states], [own], own, count, later
        self.table = positions.reshape(count, states.shape[0])

    def mask(self, target):
        there = self.table[target][:, None, None]
        here = self.table[jnp.stack(self.sources)][None]
        return ((here > there) if self.later else (here < there)).astype(f32)

    def ring(self):
        return self.pieces[-1], "ctx", [(i, (i + 2) % self.count) for i in range(self.count)]

    def masks(self):
        self.sources = [(self.own - 2 * k) % self.count for k in range(self.count // 2)]
        both = jnp.concatenate([self.mask(self.own), self.mask(self.own ^ 1)], axis=0)
        return both.reshape(both.shape[0], -1)

    def passed(self, piece):
        self.sources.append((self.own - 2 * len(self.pieces)) % self.count)
        self.pieces.append(piece)

    def partner(self):
        return trade(masked_sums(self.pieces, self.mask(self.own ^ 1), bf16), 1, self.count)

    def total(self, received):
        return (masked_sums(self.pieces, self.mask(self.own), f32) + received.astype(f32)).astype(bf16)


def body(count):
    def layer(
        tokens, block_pos, gain_attn, w_query, w_key, w_value, w_out, gain_ffn, w_gate, w_up, w_down, cotangent
    ):
        own = lax.axis_index("ctx")
        me = lax.axis_index("fsdp").astype(jnp.int32).reshape(1)
        positions = block_pos[0]
        in_shard = jnp.concatenate([w_query, w_key, w_value], axis=1)
        gains = jnp.stack([gain_attn, gain_ffn])
        if count == 8:
            gains, in_full = gather_call(gains, in_shard)
        else:
            gains, in_full = (lax.all_gather(a, "fsdp") for a in (gains, in_shard))
        gain_one, gain_two = (gains[:, k].reshape(-1).astype(f32) for k in (0, 1))
        in_full = in_full.reshape(-1, in_shard.shape[1])
        residual = tokens[0].astype(f32)
        rows = residual.shape[0]
        inv_one = lax.rsqrt(jnp.mean(residual * residual, axis=-1, keepdims=True) + EPS)
        normed_one = (residual * inv_one * gain_one).astype(bf16)
        narrow = HEADS * FDIM
        projected = dot(in_full, normed_one, (0, 1)).astype(bf16)
        query, key, value = projected[:narrow], projected[narrow : 2 * narrow], projected[2 * narrow :]

        unit = 2 * rows * BLOCK * HEADS
        (own_states,) = attention_call(
            states_kernel, ("narrow", "wide"), (("state", bf16),), rows, unit * FEAT
        )(key, value)
        weights = (w_out, w_gate.T, w_up.T, w_down)
        states = Exchange(own_states, positions, own, count, False)
        if count == 8:
            prefix, numer, denom, out_full, gates, ups, downs = forward_call(
                states.masks(), own_states, query, key, value, weights
            )
        else:
            numer, denom = attention_call(
                intra_kernel, ("narrow", "narrow", "wide"), (("wide", f32), ("head", f32)), rows, unit * 256
            )(query, key, value)
            links = Links()
            for _ in range(1, count // 2):
                states.passed(links.round([states.ring()])[0])
            prefix = states.total(links.round([states.partner()])[0])
            out_full, gates, ups, downs = (lax.all_gather(w, "fsdp") for w in weights)
        out_full = out_full.reshape(-1, w_out.shape[1])
        atten, denom = attention_call(
            inter_kernel, ("narrow", "state", "wide", "head"), (("wide", bf16), ("head", f32)), rows, unit * FEAT
        )(query, prefix, numer, denom)

        middle = residual + dot(atten, out_full, (0, 0))
        results = ffn_call(me, middle, gain_two.reshape(1, -1), cotangent[0], gates, ups, downs)
        output, grad_middle, branch, grad_gain_two = results[:4]
        gate_keep, gate_send, up_keep, up_send, down_keep, down_send = results[4:]
        grad_atten = dot(out_full, branch, (1, 1))

        gnumer, gdenom, grad_states = attention_call(
            grad_states_kernel,
            ("narrow", "wide", "head", "wide"),
            (("wide", bf16), ("head", f32), ("state", bf16)),
            rows,
            unit * FEAT,
        )(query, atten, denom, grad_atten)
        gquery, gkey, gvalue = attention_call(
            intra_back_kernel,
            ("narrow", "narrow", "wide", "wide", "head", "state"),
            (("narrow", bf16), ("narrow", f32), ("wide", f32)),
            rows,
            unit * 512,
        )(query, key, value, gnumer, gdenom, prefix)
        width = in_full.shape[1]
        out_keep, out_send = shard_grads(out_grad_kernel, me, atten, 0, [branch], [], branch.shape[1])

        def core(send):
            return send, "fsdp", CORE

        def ending(later, gkey, gvalue):
            gkey, gvalue = attention_call(
                inter_back_kernel,
                ("narrow", "wide", "state", "narrow", "wide"),
                (("narrow", bf16), ("wide", bf16)),
                rows,
                unit * 256,
            )(key, value, later, gkey, gvalue)
            gprojected = jnp.concatenate([gquery, gkey, gvalue], axis=0)
            gnormed_one = dot(gprojected, in_full, (0, 1))
            weighted_one = gnormed_one * gain_one
            grad_gain_one = jnp.sum(gnormed_one * residual * inv_one, axis=0)
            grad_tokens = (
                grad_middle
                + inv_one * weighted_one
                - residual
                * (inv_one * inv_one * inv_one)
                * jnp.mean(weighted_one * residual, axis=-1, keepdims=True)
            )[None]
            grad_gains = jnp.pad(jnp.stack([grad_gain_one, grad_gain_two[0]], axis=1), ((0, 0), (0, 126)))
            return grad_tokens, *shard_grads(
                in_grad_kernel, me, normed_one, 1, [gquery, gkey, gvalue], [grad_gains], width + 128
            )

        backward = Exchange(grad_states, positions, own, count, True)
        tall, wide = gate_keep.shape[1], down_keep.shape[1]
        model = branch.shape[1]
        links = Links()
        if count == 8:
            da, db = (Shard(down_keep, down_send, own, r, 1, 1) for r in ((0, wide // 2), (wide // 2, wide)))
            ga, gb = (Shard(gate_keep, gate_send, own, r, 1, 0) for r in ((0, tall // 2), (tall // 2, tall)))
            ua, ub = (Shard(up_keep, up_send, own, r, 1, 0) for r in ((0, tall // 2), (tall // 2, tall)))
            o = Shard(out_keep, out_send, own, (0, model // 4), 1, 0)
            (d_core,) = links.round([core(down_send)], (grad_states,))
            piece, da_x, g_core = links.round(
                [backward.ring(), da.cross(d_core), core(gate_send)], (gquery, gkey, gvalue)
            )
            backward.passed(piece)
            piece, db_x, u_core, *da_y = links.round(
                [backward.ring(), db.cross(d_core), core(up_send), *da.y_scatter(da_x)], (out_keep, out_send)
            )
            backward.passed(piece)
            piece, ga_x, o_core, *db_y = links.round(
                [backward.ring(), ga.cross(g_core), core(out_send), *db.y_scatter(db_x)]
            )
            backward.passed(piece)
            got = links.round([backward.partner(), gb.cross(g_core), *da.z_scatter(da_y), *db.z_scatter(db_y)])
            received, gb_x, da_z, db_z = got[0], got[1], got[2:5], got[5:8]
            grad_tokens, in_keep, in_send = ending(backward.total(received), gkey, gvalue)
            i = Shard(in_keep, in_send, own, (0, model // 4), 0, 0)
            got = links.round(
                [ua.cross(u_core), *ga.y_scatter(ga_x), *gb.y_scatter(gb_x), *da.z_gather(da_z), *db.z_gather(db_z)],
                (in_keep, in_send),
            )
            ua_x, ga_y, gb_y, da_w, db_w = got[0], got[1:2], got[2:3], got[3:6], got[6:9]
            got = links.round(
                [
                    ub.cross(u_core),
                    core(in_send),
                    *da.y_gather(da_w),
                    *db.y_gather(db_w),
                    *ga.z_scatter(ga_y),
                    *gb.z_scatter(gb_y),
                ]
            )
            ub_x, i_core, da_v, db_v, ga_z, gb_z = got[0], got[1], got[2:3], got[3:4], got[4:7], got[7:10]
            got = links.round(
                [i.cross(i_core), *ua.y_scatter(ua_x), *ub.y_scatter(ub_x), *ga.z_gather(ga_z), *gb.z_gather(gb_z)]
            )
            i_x, ua_y, ub_y, ga_w, gb_w = got[0], got[1:2], got[2:3], got[3:6], got[6:9]
            got = links.round([o.cross(o_core), *i.y_scatter(i_x), *ua.z_scatter(ua_y), *ub.z_scatter(ub_y)])
            o_x, i_y, ua_z, ub_z = got[0], got[1:2], got[2:5], got[5:8]
            got = links.round(
                [
                    *o.y_scatter(o_x),
                    *i.z_scatter(i_y),
                    *ga.y_gather(ga_w),
                    *gb.y_gather(gb_w),
                    *ua.z_gather(ua_z),
                    *ub.z_gather(ub_z),
                ]
            )
            o_y, i_z, ga_v, gb_v, ua_w, ub_w = got[0:1], got[1:4], got[4:5], got[5:6], got[6:9], got[9:12]
            got = links.round(
                [*o.z_scatter(o_y), *i.z_gather(i_z), *ua.y_gather(ua_w), *ub.y_gather(ub_w)]
            )
            o_z, i_w, ua_v, ub_v = got[0:3], got[3:6], got[6:7], got[7:8]
            got = links.round([*o.z_gather(o_z), *i.y_gather(i_w)])
            o_w, i_v = got[0:3], got[3:4]
            o_v = links.round(o.y_gather(o_w))
            down_grad = jnp.concatenate([da.result(da_v), db.result(db_v)], axis=0)
            gate_grad = jnp.concatenate([ga.result(ga_v), gb.result(gb_v)], axis=0).T
            up_grad = jnp.concatenate([ua.result(ua_v), ub.result(ub_v)], axis=0).T
            out_grad, in_grad = o.result(o_v), i.result(i_v)
        else:
            for _ in range(1, count // 2):
                backward.passed(links.round([backward.ring()])[0])
            grad_tokens, in_keep, in_send = ending(
                backward.total(links.round([backward.partner()])[0]), gkey, gvalue
            )

            def summed(keep, send):
                shard = Shard(keep, send, own, (0, keep.shape[1]), 0, 0)
                (got,) = links.round([core(send)])
                (got_cross,) = links.round([shard.cross(got)])
                return lax.psum(shard.chip_sum(got_cross).astype(bf16), "ctx").astype(f32)

            down_grad, gate_grad, up_grad = summed(down_keep, down_send), summed(gate_keep, gate_send).T, summed(up_keep, up_send).T
            out_grad, in_grad = summed(out_keep, out_send), summed(in_keep, in_send)
        return (
            output[None],
            grad_tokens,
            in_grad[:, width],
            in_grad[:, :narrow],
            in_grad[:, narrow : 2 * narrow],
            in_grad[:, 2 * narrow : width],
            out_grad,
            in_grad[:, width + 1],
            gate_grad,
            up_grad,
            down_grad,
        )

    return layer


def solution(mesh):
    rows = P("fsdp", None)
    seqs = P("fsdp", "ctx", None)
    vec = P("fsdp")
    in_specs = (seqs, rows, vec, rows, rows, rows, rows, vec, rows, rows, rows, seqs)
    out_specs = (seqs, seqs, vec, rows, rows, rows, rows, vec, rows, rows, rows)
    return jax.shard_map(
        body(mesh.shape["ctx"]), mesh=mesh, in_specs=in_specs, out_specs=out_specs, check_vma=False
    )
```

```python
import functools
from types import SimpleNamespace

import jax
import jax.numpy as jnp
from jax import lax
from jax.experimental import pallas as pl
from jax.experimental.pallas import tpu as pltpu
from jax.sharding import PartitionSpec as P

HEADS = 16
FDIM = 16
VDIM = 64
BLOCK = 256
GROUP = 8
FEAT = 160
STATE = GROUP // 2 * FEAT + 2 * GROUP
EPS = 1e-05
ROOT_HALF = 0.7071067811865476

f32 = jnp.float32
bf16 = jnp.bfloat16


def dims(lhs, rhs):
    return (((lhs,), (rhs,)), ((), ()))


def dot(lhs, rhs, contract):
    return lax.dot_general(lhs, rhs, dims(*contract), preferred_element_type=f32)


def turned(u, shift):
    return pltpu.roll(u, FDIM - shift, 0)


def features(u, pair_weight):
    rows = [u, u * u * ROOT_HALF]
    for shift in range(1, 8):
        rows.append(u * turned(u, shift) * ROOT_HALF)
    rows.append(u[:8] * u[8:] * ROOT_HALF)
    one = (lax.broadcasted_iota(jnp.int32, (8, u.shape[1]), 0) == 0).astype(f32)
    linear = jnp.concatenate(rows[:2], axis=0).astype(bf16)
    pairs = jnp.concatenate(rows[2:], axis=0).astype(bf16) * pair_weight
    del rows
    return jnp.concatenate([linear.astype(f32), pairs.astype(f32), one], axis=0).astype(bf16)


def features_back(u, g):
    total = g[:16] + (2.0 * ROOT_HALF) * (g[16:32] * u)
    for shift in range(1, 8):
        here = (2.0 * ROOT_HALF) * g[16 + 16 * shift : 32 + 16 * shift]
        total = total + here * turned(u, shift) + pltpu.roll(here * u, shift, 0)
    here = (2.0 * ROOT_HALF) * g[144:152]
    return total + jnp.concatenate([here * u[8:], here * u[:8]], axis=0)


def halved(ref, head):
    return ref[head * FDIM : (head + 1) * FDIM, :].astype(f32) * 0.5


def write_states(out_ref, feat, value_pair, weight_row, head):
    pair = head // 2
    product = dot(feat, value_pair, (1, 1))
    half = slice(0, 64) if head % 2 == 0 else slice(64, 128)
    out_ref[0, 0, pair * FEAT : (pair + 1) * FEAT, half] = product[:, half].astype(bf16)
    norm = dot(weight_row, feat, (1, 1))
    base = GROUP // 2 * FEAT + 2 * head
    out_ref[0, 0, base : base + 1, :] = norm[:1, :128].astype(bf16)
    out_ref[0, 0, base + 1 : base + 2, :] = jnp.concatenate([norm[:1, 128:], jnp.zeros((1, 96), f32)], axis=1).astype(bf16)


def norm_row(state_ref, head):
    base = GROUP // 2 * FEAT + 2 * head
    return state_ref[0, 0, base : base + 1, :], state_ref[0, 0, base + 1 : base + 2, :32]


def head_state(state_ref, head):
    pair = head // 2
    return state_ref[0, 0, pair * FEAT : (pair + 1) * FEAT, 64 * (head % 2) : 64 * (head % 2) + 64]


def states_kernel(key_ref, value_ref, out_ref):
    ones = jnp.ones((8, BLOCK), bf16)
    for head in range(GROUP):
        feat = features(halved(key_ref, head), 1.0)
        pair = head // 2
        write_states(out_ref, feat, value_ref[pair * 128 : (pair + 1) * 128, :], ones, head)


def intra_kernel(query_ref, key_ref, value_ref, numer_ref, denom_ref):
    for head in range(GROUP):
        rows = slice(head * FDIM, (head + 1) * FDIM)
        wide = slice(head * VDIM, (head + 1) * VDIM)
        scores = dot(key_ref[rows, :], query_ref[rows, :], (0, 0)) * 0.25
        kernel = 1.0 + scores + 0.5 * scores * scores
        denom_ref[head : head + 1, :] = jnp.sum(kernel, axis=0, keepdims=True)
        numer_ref[wide, :] = dot(value_ref[wide, :], kernel.astype(bf16), (1, 0))


def inter_kernel(query_ref, prefix_ref, numer_ref, denom_in_ref, atten_ref, denom_ref):
    for head in range(GROUP):
        wide = slice(head * VDIM, (head + 1) * VDIM)
        feat = features(halved(query_ref, head), 2.0)
        numer = numer_ref[wide, :] + dot(head_state(prefix_ref, head), feat, (0, 0))
        first, second = norm_row(prefix_ref, head)
        denom = denom_in_ref[head : head + 1, :] + dot(first, feat[:128], (1, 0)) + dot(second, feat[128:], (1, 0))
        denom_ref[head : head + 1, :] = denom
        atten_ref[wide, :] = (numer / denom).astype(bf16)


def grad_states_kernel(query_ref, atten_ref, denom_ref, grad_ref, gnumer_ref, gdenom_ref, out_ref):
    for pair in range(GROUP // 2):
        for head in (2 * pair, 2 * pair + 1):
            wide = slice(head * VDIM, (head + 1) * VDIM)
            denom = denom_ref[head : head + 1, :]
            grad = grad_ref[wide, :]
            gnumer_ref[wide, :] = (grad / denom).astype(bf16)
            gdenom = -jnp.sum(grad * atten_ref[wide, :].astype(f32), axis=0, keepdims=True) / denom
            gdenom_ref[head : head + 1, :] = gdenom.astype(bf16).astype(f32)
        for head in (2 * pair, 2 * pair + 1):
            feat = features(halved(query_ref, head), 1.0)
            weights = jnp.broadcast_to(gdenom_ref[head : head + 1, :], (8, BLOCK)).astype(bf16)
            write_states(out_ref, feat, gnumer_ref[pair * 128 : (pair + 1) * 128, :], weights, head)


def intra_back_kernel(
    query_ref, key_ref, value_ref, gnumer_ref, gdenom_ref, prefix_ref, gquery_ref, gkey_ref, gvalue_ref
):
    for head in range(GROUP):
        rows = slice(head * FDIM, (head + 1) * FDIM)
        wide = slice(head * VDIM, (head + 1) * VDIM)
        query, key = query_ref[rows, :], key_ref[rows, :]
        gnumer = gnumer_ref[wide, :]
        gdenom = gdenom_ref[head : head + 1, :]
        scores = dot(key, query, (0, 0)) * 0.25
        kernel = (1.0 + scores + 0.5 * scores * scores).astype(bf16)
        gkernel = dot(value_ref[wide, :], gnumer, (0, 0)) + gdenom
        gscores = ((1.0 + scores) * gkernel).astype(bf16)
        gvalue_ref[wide, :] = dot(gnumer, kernel, (1, 1))
        gkey_ref[rows, :] = dot(query, gscores, (1, 1)) * 0.25
        first, second = norm_row(prefix_ref, head)
        gdenom_low = gdenom.astype(bf16)
        outer_prod = jnp.concatenate([dot(first, gdenom_low, (0, 0)), dot(second, gdenom_low, (0, 0))], axis=0)
        gfeat = dot(head_state(prefix_ref, head), gnumer, (1, 0)) + outer_prod
        gquery = dot(key, gscores, (1, 0)) * 0.25 + 0.5 * features_back(halved(query_ref, head), gfeat)
        gquery_ref[rows, :] = gquery.astype(bf16)


def inter_back_kernel(key_ref, value_ref, later_ref, gkey_in_ref, gvalue_in_ref, gkey_ref, gvalue_ref):
    ones = jnp.ones((1, BLOCK), bf16)
    for head in range(GROUP):
        rows = slice(head * FDIM, (head + 1) * FDIM)
        wide = slice(head * VDIM, (head + 1) * VDIM)
        u = halved(key_ref, head)
        state = head_state(later_ref, head)
        first, second = norm_row(later_ref, head)
        outer_prod = jnp.concatenate([dot(first, ones, (0, 0)), dot(second, ones, (0, 0))], axis=0)
        gfeat = dot(state, value_ref[wide, :], (1, 0)) + outer_prod
        gkey_ref[rows, :] = (gkey_in_ref[rows, :] + 0.5 * features_back(u, gfeat)).astype(bf16)
        feat = features(u, 2.0)
        gvalue_ref[wide, :] = (gvalue_in_ref[wide, :] + dot(state, feat, (0, 0))).astype(bf16)


def attention_call(kernel, ins, outs, tokens, flops):
    blocks = tokens // BLOCK
    groups = HEADS // GROUP
    forms = {
        "narrow": ((GROUP * FDIM, BLOCK), lambda b, g: (g, b), (HEADS * FDIM, tokens)),
        "wide": ((GROUP * VDIM, BLOCK), lambda b, g: (g, b), (HEADS * VDIM, tokens)),
        "head": ((GROUP, BLOCK), lambda b, g: (g, b), (HEADS, tokens)),
        "state": ((1, 1, STATE, 128), lambda b, g: (b, g, 0, 0), (blocks, groups, STATE, 128)),
    }

    def spec(name):
        return pl.BlockSpec(forms[name][0], forms[name][1])

    def call(*arrays):
        moved = sum(a.size * a.dtype.itemsize for a in arrays)
        return pl.pallas_call(
            kernel,
            out_shape=[jax.ShapeDtypeStruct(forms[name][2], dtype) for name, dtype in outs],
            grid=(blocks, groups),
            in_specs=[spec(name) for name in ins],
            out_specs=[spec(name) for name, _ in outs],
            compiler_params=pltpu.CompilerParams(vmem_limit_bytes=40 << 20),
            cost_estimate=pl.CostEstimate(flops=flops, bytes_accessed=2 * moved, transcendentals=0),
        )(*arrays)

    return call


ORDER = (0, 2, 1, 3)


def place(step):
    return (step % 2) * 2 + step // 2


def ffn_kernel(me_ref, middle_ref, gain_ref, cot_ref, gates, ups, downs, *refs):
    output_ref, gmiddle_ref, branch_ref, ggain_ref = refs[:4]
    gate_keep, gate_send, up_keep, up_send, down_keep, down_send = refs[4:10]
    normed, x_own, x_turned, cot_turned, total, gnormed = refs[10:]
    step = pl.program_id(0)
    me = me_ref[0]
    width = gates.shape[2]

    def inverse():
        middle = middle_ref[...]
        return lax.rsqrt(jnp.mean(middle * middle, axis=-1, keepdims=True) + EPS)

    @pl.when(step == 0)
    def _():
        normed[...] = (middle_ref[...] * inverse() * gain_ref[...]).astype(bf16)
        for r in range(4):
            x_own[r] = normed[:, pl.ds(pl.multiple_of((me ^ r) * width, width), width)]
        x_turned[...] = normed[...].T
        cot_turned[...] = cot_ref[...].T
        total[...] = jnp.zeros_like(total)
        gnormed[...] = jnp.zeros_like(gnormed)

    x_part = x_turned[:width, :]
    gate = dot(gates[0], x_part, (1, 0))
    up = dot(ups[0], x_part, (1, 0))
    for r in range(1, 4):
        x_part = x_turned[r * width : (r + 1) * width, :]
        gate = gate + dot(gates[r], x_part, (1, 0))
        up = up + dot(ups[r], x_part, (1, 0))
    down = downs[0]
    ghidden = dot(down, cot_turned[...], (1, 0))
    sigmoid = jax.nn.sigmoid(gate)
    silu = gate * sigmoid
    hidden = (silu * up).astype(bf16)
    ggate = (ghidden * up * (sigmoid * (1.0 + gate * (1.0 - sigmoid)))).astype(bf16)
    gup = (ghidden * silu).astype(bf16)
    total[...] += dot(hidden, down, (0, 0))
    gdown = dot(hidden, cot_ref[...], (1, 0))
    tall, broad = down_keep.shape[3:]

    def store(ref, slot, grad):
        for half in range(2):
            for eighth in range(8):
                ref[half, slot, eighth] = grad[
                    half * tall : (half + 1) * tall, eighth * broad : (eighth + 1) * broad
                ].astype(bf16)

    @pl.when(step < 2)
    def _():
        store(down_keep, 0, gdown)

    @pl.when(step >= 2)
    def _():
        store(down_send, 0, gdown)

    def store_turned(keep, send, r, grad):
        ref = send if r % 2 else keep
        for half in range(2):
            for eighth in range(2):
                ref[half, r // 2, eighth] = grad[
                    eighth * tall : (eighth + 1) * tall, half * broad : (half + 1) * broad
                ].astype(bf16)

    for r in range(4):
        part = slice(r * width, (r + 1) * width)
        gnormed[:, part] += dot(ggate, gates[r], (0, 0)) + dot(gup, ups[r], (0, 0))
        store_turned(gate_keep, gate_send, r, dot(ggate, x_own[r], (1, 0)))
        store_turned(up_keep, up_send, r, dot(gup, x_own[r], (1, 0)))

    @pl.when(step == 3)
    def _():
        middle, inv, cot = middle_ref[...], inverse(), cot_ref[...].astype(f32)
        grad = gnormed[...]
        output_ref[...] = (middle + total[...]).astype(bf16)
        ggain_ref[...] = jnp.broadcast_to(jnp.sum(grad * middle * inv, axis=0, keepdims=True), ggain_ref.shape)
        weighted = grad * gain_ref[...]
        slope = jnp.mean(weighted * middle, axis=-1, keepdims=True)
        gmiddle = cot + inv * weighted - middle * (inv * inv * inv) * slope
        gmiddle_ref[...] = gmiddle
        branch_ref[...] = gmiddle.astype(bf16)


def ffn_call(me, middle, gain, cot, gates, ups, downs):
    rows, model = middle.shape
    _, hidden, width = gates.shape
    tile = downs.shape[1]
    once = pl.Buffered(1)

    def whole(shape, **kw):
        return pl.BlockSpec(shape, lambda s, me: (0,) * len(shape), **kw)

    columns = pl.BlockSpec((4, tile, width), lambda s, me: (0, me[0] ^ place(s), 0))
    block = (tile // 2, model // 8)
    pair = pl.BlockSpec((2, 2, 2, *block), lambda s, me: (0, 0, me[0] ^ place(s), 0, 0))
    grads = jax.ShapeDtypeStruct((2, 2, 8, *block), bf16)
    return pl.pallas_call(
        ffn_kernel,
        out_shape=[
            jax.ShapeDtypeStruct((rows, model), bf16),
            jax.ShapeDtypeStruct((rows, model), f32),
            jax.ShapeDtypeStruct((rows, model), bf16),
            jax.ShapeDtypeStruct((8, model), f32),
            grads,
            grads,
            grads,
            grads,
            grads,
            grads,
        ],
        grid_spec=pltpu.PrefetchScalarGridSpec(
            num_scalar_prefetch=1,
            grid=(4,),
            in_specs=[
                whole((rows, model), pipeline_mode=once),
                whole((1, model)),
                whole((rows, model), pipeline_mode=once),
                columns,
                columns,
                pl.BlockSpec((1, tile, model), lambda s, me: (me[0] ^ place(s), 0, 0)),
            ],
            out_specs=[
                whole((rows, model), pipeline_mode=once),
                whole((rows, model), pipeline_mode=once),
                whole((rows, model), pipeline_mode=once),
                whole((8, model)),
                pair,
                pair,
                pair,
                pair,
                pl.BlockSpec((2, 1, 8, *block), lambda s, me: (0, jnp.minimum(s, 1), 0, 0, 0)),
                pl.BlockSpec((2, 1, 8, *block), lambda s, me: (0, jnp.maximum(s - 2, 0), 0, 0, 0)),
            ],
            scratch_shapes=[
                pltpu.VMEM((rows, model), bf16),
                pltpu.VMEM((4, rows, width), bf16),
                pltpu.VMEM((model, rows), bf16),
                pltpu.VMEM((model, rows), bf16),
                pltpu.VMEM((rows, model), f32),
                pltpu.VMEM((rows, model), f32),
            ],
        ),
        compiler_params=pltpu.CompilerParams(vmem_limit_bytes=58 << 20),
        cost_estimate=pl.CostEstimate(
            flops=18 * rows * model * hidden, bytes_accessed=14 * hidden * model, transcendentals=0
        ),
    )(me, middle, gain, cot, gates, ups, downs)


CORE = [(0, 1), (1, 0), (2, 3), (3, 2)]
CHIP = [(0, 2), (2, 0), (1, 3), (3, 1)]


class Links:
    def __init__(self):
        self.last = ()

    def round(self, sends, beside=()):
        arrays = [send[0] for send in sends]
        if self.last:
            arrays = lax.optimization_barrier((*arrays, *self.last))[: len(arrays)]
        results = [lax.ppermute(a, axis, perm) for a, (_, axis, perm) in zip(arrays, sends)]
        self.last = (*results, *beside)
        return results


def trade(array, bits, count):
    return array, "ctx", [(i, i ^ bits) for i in range(count)]


MESH = pl.DeviceIdType.MESH


class Spot:
    def __init__(self):
        self.me = lax.axis_index("fsdp")
        self.own = lax.axis_index("ctx")
        self.core = {"fsdp": self.me + 1 - 2 * (self.me % 2)}
        self.across = (self.me + 2) % 4
        self.chip = {"fsdp": self.across}
        self.y = self.own % 2
        self.z = self.own // 2
        self.side = {"ctx": self.own + 1 - 2 * self.y}
        self.next = {"ctx": self.own + 2 - 4 * (self.z % 2)}
        self.ahead = [None] + [{"ctx": (self.own + 2 * k) % 8} for k in (1, 2, 3)]

    def greet(self, neighbours):
        barrier = pltpu.get_barrier_semaphore()
        for neighbour in neighbours:
            pl.semaphore_signal(barrier, inc=1, device_id=neighbour, device_id_type=MESH)
        pl.semaphore_wait(barrier, len(neighbours))


class Wire:
    def __init__(self, send_sems, recv_sems, local_sems):
        self.send_sems, self.recv_sems, self.local_sems = send_sems, recv_sems, local_sems
        self.sent, self.local, self.count = [], [], 0

    def send(self, source, target, device):
        k = self.count
        self.count += 1
        copy = pltpu.make_async_remote_copy(
            src_ref=source,
            dst_ref=target,
            send_sem=self.send_sems.at[k],
            recv_sem=self.recv_sems.at[k],
            device_id=device,
            device_id_type=MESH,
        )
        copy.start()
        self.sent.append(copy)
        return copy

    def keep(self, source, target):
        copy = pltpu.make_async_copy(source, target, self.local_sems.at[len(self.local)])
        copy.start()
        self.local.append(copy)
        return copy

    def left(self, copy):
        copy.wait_send()
        self.sent = [other for other in self.sent if other is not copy]

    def end(self):
        for copy in self.sent:
            copy.wait_send()


class Gather:
    def __init__(self, wire, spot, shard, full, held, axis, split, chunks):
        self.wire, self.spot, self.full, self.axis, self.split = wire, spot, full, axis, split
        self.part = shard.shape[axis] // (2 if split else 1)
        self.size = self.part // chunks
        me = spot.me
        self.held, self.loaded = held, wire.keep(shard, held)
        here = [self.view(shard, c, spot.y) for c in range(chunks)]
        there = [self.view(full.at[me], c, spot.y) for c in range(chunks)]
        self.cross = [wire.send(a, b, spot.chip) for a, b in zip(here, there)]
        self.near = wire.send(shard, full.at[me], spot.core)
        self.side, self.far = {}, []

    def write(self):
        self.loaded.wait()
        self.own = self.wire.keep(self.held, self.full.at[self.spot.me])

    def view(self, ref, chunk, y):
        start = chunk * self.size + (y * self.part if self.split else 0)
        index = [slice(None)] * 2
        index[self.axis] = pl.ds(pl.multiple_of(start, self.size), self.size)
        return ref.at[tuple(index)]

    def relay(self, chunk):
        self.cross[chunk].wait_recv()
        part = self.view(self.full.at[self.spot.across], chunk, self.spot.y)
        if self.split:
            self.side[chunk] = self.wire.send(part, part, self.spot.side)
        self.far.append(self.wire.send(part, part, self.spot.core))

    def relay_other(self, chunk):
        self.side[chunk].wait_recv()
        part = self.view(self.full.at[self.spot.across], chunk, 1 - self.spot.y)
        self.far.append(self.wire.send(part, part, self.spot.core))

    def end(self):
        self.own.wait()
        self.near.wait_recv()
        for copy in self.far:
            copy.wait_recv()


def gather_kernel(gain_ref, in_ref, gain_full, in_full, held, gain_held, send_sems, recv_sems, local_sems):
    spot = Spot()
    wire = Wire(send_sems, recv_sems, local_sems)
    spot.greet([spot.core, spot.chip, spot.side])
    weight = Gather(wire, spot, in_ref, in_full, held, 0, True, 2)
    gain_loaded = wire.keep(gain_ref, gain_held)
    near = wire.send(gain_ref, gain_full.at[spot.me], spot.core)
    cross = wire.send(gain_ref, gain_full.at[spot.me], spot.chip)
    weight.write()
    gain_loaded.wait()
    own = wire.keep(gain_held, gain_full.at[spot.me])
    weight.relay(0)
    weight.relay(1)
    weight.relay_other(0)
    cross.wait_recv()
    far = wire.send(gain_full.at[spot.across], gain_full.at[spot.across], spot.core)
    weight.relay_other(1)
    own.wait()
    near.wait_recv()
    far.wait_recv()
    weight.end()
    wire.end()


def scalar_masks(places_ref, spot, later):
    def place(device, block):
        return places_ref[0, 2 * device + block]

    partner = spot.own + 1 - 2 * spot.y
    targets = [place(device, block) for device in (spot.own, partner) for block in range(2)]
    masks = []
    for target in targets:
        row = []
        for k in range(4):
            for block in range(2):
                source = place((spot.own + 8 - 2 * k) % 8, block)
                row.append(jnp.where(source > target if later else source < target, 1.0, 0.0).astype(f32))
        masks.append(row)
    return masks


def add_masked(total, piece, masks, source, block, first):
    for group in range(piece.shape[0]):
        states = piece[group].astype(f32)
        for target in range(4):
            term = states * masks[target][2 * source + block]
            if first:
                total[target, group] = term
            else:
                total[target, group] += term


def forward_kernel(places_ref, states_ref, query_ref, key_ref, value_ref, tokens_ref, *refs):
    weights, (prefix_ref, atten_ref, denom_ref, middle_ref), fulls = refs[:4], refs[4:8], refs[8:12]
    ring, total, outgoing, incoming, numer, inner, out_full = refs[12:19]
    held, (send_sems, recv_sems, local_sems) = refs[19:23], refs[23:]
    spot = Spot()
    wire = Wire(send_sems, recv_sems, local_sems)
    spot.greet([spot.core, spot.chip, spot.side, spot.ahead[1], spot.ahead[3]])
    hops = [[wire.send(states_ref.at[b], ring.at[0, b], spot.ahead[1]) for b in range(2)], [], []]
    forms = ((0, True, 1), (0, True, 2), (0, True, 2), (1, False, 2))
    out, gate, up, down = (
        Gather(wire, spot, w, full, own, *form) for w, full, own, form in zip(weights, fulls, held, forms)
    )
    masks = scalar_masks(places_ref, spot, False)

    def forward(step, block):
        hops[step][block].wait_recv()
        if step < 2:
            hops[step + 1].append(wire.send(ring.at[step, block], ring.at[step + 1, block], spot.ahead[1]))

    intra = list(grid_views((query_ref, FDIM), (key_ref, FDIM), (value_ref, VDIM), (numer, VDIM), (inner, 1)))
    intra_kernel(*intra[0])
    for one in (out, gate, up, down):
        one.write()
    intra_kernel(*intra[1])
    forward(0, 0)
    out.relay(0)
    intra_kernel(*intra[2])
    intra_kernel(*intra[3])
    add_masked(total, states_ref.at[0], masks, 0, 0, True)
    gate.relay(0)
    forward(0, 1)
    out.relay_other(0)
    add_masked(total, states_ref.at[1], masks, 0, 1, False)
    for block in range(2):
        add_masked(total, ring.at[0, block], masks, 1, block, False)
    gate.relay(1)
    out.end()
    shard = weights[0].shape[0]
    loads = [wire.keep(fulls[0].at[k], out_full.at[k * shard : (k + 1) * shard]) for k in range(4)]
    forward(1, 0)
    add_masked(total, ring.at[1, 0], masks, 2, 0, False)
    gate.relay_other(0)
    forward(1, 1)
    up.relay(0)
    gate.relay_other(1)
    add_masked(total, ring.at[1, 1], masks, 2, 1, False)
    forward(2, 0)
    up.relay(1)
    add_masked(total, ring.at[2, 0], masks, 3, 0, False)
    up.relay_other(0)
    forward(2, 1)
    add_masked(total, ring.at[2, 1], masks, 3, 1, False)
    outgoing[...] = total[2:].astype(bf16)
    partner = wire.send(outgoing, incoming, spot.side)
    up.relay_other(1)
    down.relay(0)
    partner.wait_recv()
    prefix_ref[...] = (total[:2] + incoming[...].astype(f32)).astype(bf16)
    for parts in grid_views(
        (query_ref, FDIM), (prefix_ref, None), (numer, VDIM), (inner, 1), (atten_ref, VDIM), (denom_ref, 1)
    ):
        inter_kernel(*parts)
    for copy in loads:
        copy.wait()
    down.relay(1)
    middle_ref[...] = tokens_ref[...].astype(f32) + dot(atten_ref[...], out_full[...], (0, 0))
    for one in (gate, up, down):
        one.end()
    wire.end()


def grid_views(*refs):
    for block in range(2):
        for group in range(HEADS // GROUP):
            columns = slice(block * BLOCK, (block + 1) * BLOCK)
            parts = []
            for ref, rows in refs:
                if rows is None:
                    parts.append(ref.at[block : block + 1, group : group + 1])
                else:
                    parts.append(ref.at[group * GROUP * rows : (group + 1) * GROUP * rows, columns])
            yield parts


def add_chunks(total, first, other, count):
    def one(k, carry):
        total[first + k] = (total[first + k].astype(f32) + other[k].astype(f32)).astype(bf16)
        return carry

    lax.fori_loop(0, count, one, 0)


class Flow:
    def __init__(self, wire, spot, base, crossed, sided, lined, result):
        self.wire, self.spot = wire, spot
        self.base, self.crossed, self.sided, self.lined, self.result = base, crossed, sided, lined, result
        self.half = spot.y * 4
        self.pair = self.half + 2 * (spot.z % 2)
        self.mine = self.pair + spot.z // 2

    def cross(self):
        self.x = self.wire.send(self.base.at[1], self.crossed, self.spot.chip)

    def to_side(self):
        self.x.wait_recv()
        add_chunks(self.crossed, 0, self.base.at[0], 8)
        there = pl.ds(4 - self.half, 4)
        self.s = self.wire.send(self.crossed.at[there], self.sided, self.spot.side)

    def to_line(self):
        self.s.wait_recv()
        add_chunks(self.crossed, self.half, self.sided, 4)
        there = pl.ds(2 * self.half + 2 - self.pair, 2)
        self.l = self.wire.send(self.crossed.at[there], self.lined.at[0:2], self.spot.next)

    def to_far(self):
        self.l.wait_recv()
        add_chunks(self.crossed, self.pair, self.lined, 2)
        self.f = self.wire.send(self.crossed.at[2 * self.pair + 1 - self.mine], self.lined.at[2], self.spot.ahead[2])

    def from_far(self):
        self.f.wait_recv()
        mine = self.mine
        self.crossed[mine] = (self.crossed[mine].astype(f32) + self.lined[2].astype(f32)).astype(bf16)
        self.own = self.wire.keep(self.crossed.at[mine], self.result.at[mine])
        self.g = self.wire.send(self.crossed.at[mine], self.result.at[mine], self.spot.ahead[2])

    def along_line(self):
        self.own.wait()
        self.g.wait_recv()
        here = self.result.at[pl.ds(self.pair, 2)]
        self.a = self.wire.send(here, here, self.spot.next)

    def along_side(self):
        self.a.wait_recv()
        here = self.result.at[pl.ds(self.half, 4)]
        self.b = self.wire.send(here, here, self.spot.side)

    def end(self):
        self.b.wait_recv()


def backward_kernel(names, *refs):
    r = SimpleNamespace(**dict(zip(names, refs)))
    spot = Spot()
    wire = Wire(r.send_sems, r.recv_sems, r.local_sems)
    me, y, z = spot.me, spot.y, spot.z
    spot.greet([spot.core, spot.chip, spot.side, *spot.ahead[1:]])
    kept, sent = (r.down_keep, r.gate_keep, r.up_keep), (r.down_send, r.gate_send, r.up_send)
    held, outs = (r.down_core, r.gate_core, r.up_core), (r.down_out, r.gate_out, r.up_out)
    from_core = [wire.send(a, b, spot.core) for a, b in zip(sent, held)]
    first = [
        wire.keep(a, b)
        for a, b in (
            (r.out_full_hbm, r.out_full),
            (r.branch_hbm, r.branch),
            (r.atten_hbm, r.atten),
            (r.denom_hbm, r.denom),
            (r.query_hbm, r.query),
        )
    ]
    stage = r.stage
    staged = {}

    def load(weight, half):
        staged[weight, half] = wire.keep(kept[weight].at[half], stage.at[half])

    def base(weight, half):
        staged[weight, half].wait()
        for slot in range(2):
            add_chunks(held[weight].at[half, slot], 0, stage.at[half, slot], 8)

    def flow(base, crossed, sided, lined, result):
        return Flow(wire, spot, base, crossed, sided, lined, result)

    ffn = [
        flow(
            held[weight].at[half],
            r.crossed.at[2 * weight + half],
            r.sided.at[2 * weight + half],
            r.lined.at[2 * weight + half],
            outs[weight].at[half],
        )
        for weight in range(3)
        for half in range(2)
    ]
    out_flow = flow(r.out_base, r.out_crossed, r.out_sided, r.out_lined, r.out_out)
    in_flow = flow(r.in_base, r.in_crossed, r.in_sided, r.in_lined, r.in_out)
    da, db, ga, gb, ua, ub = ffn
    load(0, 0)
    load(0, 1)
    second = [wire.keep(a, b) for a, b in ((r.key_hbm, r.key), (r.value_hbm, r.value), (r.prefix_hbm, r.prefix))]
    tokens_load = wire.keep(r.tokens_hbm, r.tokens)
    third = [wire.keep(a, b) for a, b in ((r.in_full_hbm, r.in_full), (r.gmiddle_hbm, r.gmiddle))]
    for copy in first:
        copy.wait()
    grad = r.grad
    grad[...] = dot(r.out_full[...], r.branch[...], (1, 1))
    states, gnumer, gdenom = r.states, r.gnumer, r.gdenom
    for parts in grid_views(
        (r.query, FDIM), (r.atten, VDIM), (r.denom, 1), (grad, VDIM), (gnumer, VDIM), (gdenom, 1), (states, None)
    ):
        grad_states_kernel(*parts)
    ring, total, mask = r.ring, r.total, scalar_masks(r.places, spot, True)
    hops = [[wire.send(states.at[b], ring.at[0, b], spot.ahead[1]) for b in range(2)], [], []]

    def forward(step, block):
        hops[step][block].wait_recv()
        if step < 2:
            hops[step + 1].append(wire.send(ring.at[step, block], ring.at[step + 1, block], spot.ahead[1]))

    from_core[0].wait_recv()
    base(0, 0)
    da.cross()
    load(1, 0)
    base(0, 1)
    db.cross()
    load(1, 1)

    core_of = me + 1 - 2 * (me % 2)
    across_core = (core_of + 2) % 4
    shards = (me, spot.across, core_of, across_core)
    width = r.branch.shape[1] // 4

    def out_grad(index):
        rows = pl.ds(pl.multiple_of(shards[index] * width, width), width)
        value = dot(r.atten[rows, :], r.branch[...], (1, 0))
        ref = r.out_base if index < 2 else r.out_send
        for k in range(8):
            ref[index % 2, k] = value[k * 32 : (k + 1) * 32, :].astype(bf16)

    for index in (2, 3):
        out_grad(index)
    out_core = wire.send(r.out_send, r.out_core, spot.core)
    for index in (0, 1):
        out_grad(index)
    for copy in second:
        copy.wait()
    narrow = HEADS * FDIM
    gproj = r.gproj
    gquery, gkey, gvalue = gproj.at[0:narrow], gproj.at[narrow : 2 * narrow], gproj.at[2 * narrow : 2 * narrow + HEADS * VDIM]
    intra = list(
        grid_views(
            (r.query, FDIM),
            (r.key, FDIM),
            (r.value, VDIM),
            (gnumer, VDIM),
            (gdenom, 1),
            (r.prefix, None),
            (gquery, FDIM),
            (r.gkey_in, FDIM),
            (grad, VDIM),
        )
    )
    intra_back_kernel(*intra[0])
    forward(0, 0)
    intra_back_kernel(*intra[1])
    from_core[1].wait_recv()
    base(1, 0)
    load(2, 0)
    base(1, 1)
    load(2, 1)
    forward(0, 1)
    intra_back_kernel(*intra[2])
    intra_back_kernel(*intra[3])
    da.to_side()
    ga.cross()
    for block in range(2):
        add_masked(total, states.at[block], mask, 0, block, block == 0)
        add_masked(total, ring.at[0, block], mask, 1, block, False)
    forward(1, 0)
    add_masked(total, ring.at[1, 0], mask, 2, 0, False)
    from_core[2].wait_recv()
    base(2, 0)
    base(2, 1)
    forward(1, 1)
    add_masked(total, ring.at[1, 1], mask, 2, 1, False)
    db.to_side()
    gb.cross()
    out_core.wait_recv()
    for slot in range(2):
        add_chunks(r.out_base.at[slot], 0, r.out_core.at[slot], 8)
    da.to_line()
    forward(2, 0)
    add_masked(total, ring.at[2, 0], mask, 3, 0, False)
    forward(2, 1)
    add_masked(total, ring.at[2, 1], mask, 3, 1, False)
    r.outgoing[...] = total[2:].astype(bf16)
    partner = wire.send(r.outgoing, r.incoming, spot.side)
    da.to_far()
    ga.to_side()
    ua.cross()
    db.to_line()
    da.from_far()
    tokens_load.wait()
    residual = r.tokens[...].astype(f32)
    inverse = lax.rsqrt(jnp.mean(residual * residual, axis=-1, keepdims=True) + EPS)
    r.normed[...] = (residual * inverse * r.gain_one[...]).astype(bf16)
    db.to_far()
    partner.wait_recv()
    for copy in hops[0]:
        wire.left(copy)
    states[...] = (total[:2] + r.incoming[...].astype(f32)).astype(bf16)
    for parts in grid_views(
        (r.key, FDIM), (r.value, VDIM), (states, None), (r.gkey_in, FDIM), (grad, VDIM), (gkey, FDIM), (gvalue, VDIM)
    ):
        inter_back_kernel(*parts)
    turned = r.turned
    turned[...] = gproj[...].T

    def in_grad(index):
        columns = pl.ds(pl.multiple_of(shards[index] * width, width), width)
        value = dot(r.normed[:, columns], turned[...], (0, 0))
        ref = r.in_base if index < 2 else r.in_send
        for k in range(8):
            ref[index % 2, k] = value[k * 32 : (k + 1) * 32, :].astype(bf16)

    for index in (2, 3):
        in_grad(index)
    in_core = wire.send(r.in_send, r.in_core, spot.core)
    gb.to_side()
    ub.cross()
    da.along_line()
    ga.to_line()
    db.from_far()
    for index in (0, 1):
        in_grad(index)
    da.along_side()
    db.along_line()
    ga.to_far()
    for copy in third:
        copy.wait()
    gmiddle = r.gmiddle
    gnormed = dot(turned[...], r.in_full[...], (1, 1))
    residual = r.tokens[...].astype(f32)
    inverse = lax.rsqrt(jnp.mean(residual * residual, axis=-1, keepdims=True) + EPS)
    gains = r.gains
    gains[0:1, :] = jnp.sum(gnormed * residual * inverse, axis=0, keepdims=True)
    weighted = gnormed * r.gain_one[...]
    slope = jnp.mean(weighted * residual, axis=-1, keepdims=True)
    gmiddle[...] += inverse * weighted - residual * (inverse * inverse * inverse) * slope
    written = wire.keep(gmiddle, r.tokens_out)
    gains[1:2, :] = r.ggain_two[0:1, :]
    small = r.small
    small[...] = jnp.zeros_like(small)
    for index in range(4):
        for row in range(4):
            start = pl.multiple_of(shards[index] * width + (row % 2) * 128, 128)
            small[index, row : row + 1, :] = gains[row // 2 : row // 2 + 1, pl.ds(start, 128)]
    small_in = r.small_in
    small_core = wire.send(small.at[2:4], small_in.at[0:2], spot.core)
    gb.to_line()
    ga.from_far()
    db.along_side()
    in_core.wait_recv()
    for slot in range(2):
        add_chunks(r.in_base.at[slot], 0, r.in_core.at[slot], 8)
    gb.to_far()
    ga.along_line()
    ua.to_side()
    in_flow.cross()
    small_core.wait_recv()
    small[0:2] = small[0:2] + small_in[0:2]
    small_cross = wire.send(small.at[1], small_in.at[2], spot.chip)
    gb.from_far()
    ga.along_side()
    ua.to_line()
    gb.along_line()
    ua.to_far()
    small_cross.wait_recv()
    small[0] = small[0] + small_in[2]
    small_side = wire.send(small.at[0], small_in.at[3], spot.side)
    gb.along_side()
    ua.from_far()
    ub.to_side()
    out_flow.cross()
    ua.along_line()
    ub.to_line()
    small_side.wait_recv()
    small_line = r.small_line
    small_line[z] = small[0] + small_in[3]
    small_sent = [wire.send(small_line.at[z], small_line.at[z], spot.ahead[k]) for k in (1, 2, 3)]
    ua.along_side()
    ub.to_far()
    ub.from_far()
    in_flow.to_side()
    ub.along_line()
    in_flow.to_line()
    ub.along_side()
    out_flow.to_side()
    in_flow.to_far()
    in_flow.from_far()
    out_flow.to_line()
    for copy in small_sent:
        copy.wait_recv()
    r.gains_out[...] = (small_line[0] + small_line[1]) + (small_line[2] + small_line[3])
    in_flow.along_line()
    out_flow.to_far()
    out_flow.from_far()
    in_flow.along_side()
    out_flow.along_line()
    out_flow.along_side()
    written.wait()
    for one in (*ffn, out_flow, in_flow):
        one.end()
    wire.end()


HBM = pl.BlockSpec(memory_space=pltpu.HBM)
VMEM = pl.BlockSpec(memory_space=pltpu.VMEM)
SMEM = pl.BlockSpec(memory_space=pltpu.SMEM)


def sems(count):
    return pltpu.SemaphoreType.DMA((count,))


def gather_call(gains, in_shard):
    return pl.pallas_call(
        gather_kernel,
        out_shape=[jax.ShapeDtypeStruct((4, *a.shape), a.dtype) for a in (gains, in_shard)],
        in_specs=[HBM, HBM],
        out_specs=[HBM, HBM],
        scratch_shapes=[
            pltpu.VMEM(in_shard.shape, bf16),
            pltpu.VMEM(gains.shape, bf16),
            sems(12),
            sems(12),
            sems(4),
        ],
        compiler_params=pltpu.CompilerParams(collective_id=0, has_side_effects=True, vmem_limit_bytes=16 << 20),
    )(gains, in_shard)


def forward_call(places, states, query, key, value, tokens, weights):
    state = states.shape
    rows, model = tokens.shape
    wide = HEADS * VDIM
    return pl.pallas_call(
        forward_kernel,
        out_shape=[
            jax.ShapeDtypeStruct(state, bf16),
            jax.ShapeDtypeStruct((wide, rows), bf16),
            jax.ShapeDtypeStruct((HEADS, rows), f32),
            jax.ShapeDtypeStruct((rows, model), f32),
        ]
        + [jax.ShapeDtypeStruct((4, *w.shape), bf16) for w in weights],
        in_specs=[SMEM] + [VMEM] * 5 + [HBM] * 4,
        out_specs=[VMEM] * 4 + [HBM] * 4,
        scratch_shapes=[
            pltpu.VMEM((3, *state), bf16),
            pltpu.VMEM((4, *state[1:]), f32),
            pltpu.VMEM(state, bf16),
            pltpu.VMEM(state, bf16),
            pltpu.VMEM((wide, rows), f32),
            pltpu.VMEM((HEADS, rows), f32),
            pltpu.VMEM((wide, model), bf16),
            *(pltpu.VMEM(w.shape, bf16) for w in weights),
            sems(36),
            sems(36),
            sems(12),
        ],
        compiler_params=pltpu.CompilerParams(collective_id=1, has_side_effects=True, vmem_limit_bytes=56 << 20),
    )(places, states, query, key, value, tokens, *weights)


def settle_kernel(down_ref, gate_ref, up_ref, down_out, gate_out, up_out):
    tall, broad = down_ref.shape[2:]
    for half in range(2):
        for eighth in range(8):
            down_out[half * tall : (half + 1) * tall, eighth * broad : (eighth + 1) * broad] = down_ref[
                half, eighth
            ].astype(f32)
    for ref, out in ((gate_ref, gate_out), (up_ref, up_out)):
        for half in range(2):
            for eighth in range(8):
                out[eighth * tall : (eighth + 1) * tall, half * broad : (half + 1) * broad] = ref[
                    half, eighth
                ].astype(f32)


def settle_call(down, gate, up):
    tall, broad = down.shape[2:]
    shapes = [(2 * tall, 8 * broad), (8 * tall, 2 * broad), (8 * tall, 2 * broad)]
    return pl.pallas_call(
        settle_kernel,
        out_shape=[jax.ShapeDtypeStruct(shape, f32) for shape in shapes],
        in_specs=[VMEM] * 3,
        out_specs=[VMEM] * 3,
        compiler_params=pltpu.CompilerParams(vmem_limit_bytes=40 << 20),
    )(down, gate, up)


def masked_sums(pieces, masks, dtype):
    total = None
    for index, piece in enumerate(pieces):
        for block in range(piece.shape[0]):
            term = masks[:, index, block][:, None, None, None] * piece[block].astype(f32)[None]
            total = term if total is None else total + term
    return total.astype(dtype)


class Exchange:
    def __init__(self, states, positions, own, count, later):
        self.pieces, self.sources, self.own, self.count, self.later = [states], [own], own, count, later
        self.table = positions.reshape(count, states.shape[0])

    def mask(self, target):
        there = self.table[target][:, None, None]
        here = self.table[jnp.stack(self.sources)][None]
        return ((here > there) if self.later else (here < there)).astype(f32)

    def ring(self):
        return self.pieces[-1], "ctx", [(i, (i + 2) % self.count) for i in range(self.count)]

    def passed(self, piece):
        self.sources.append((self.own - 2 * len(self.pieces)) % self.count)
        self.pieces.append(piece)

    def partner(self):
        return trade(masked_sums(self.pieces, self.mask(self.own ^ 1), bf16), 1, self.count)

    def total(self, received):
        return (masked_sums(self.pieces, self.mask(self.own), f32) + received.astype(f32)).astype(bf16)


def backward_call(arrays):
    names, specs, values = [], [], []
    get = SimpleNamespace(**arrays)
    for name, array in arrays.items():
        names.append(name)
        values.append(array)
        specs.append(SMEM if array.dtype == jnp.int32 else VMEM if array.shape[0] <= 8 and array.dtype == f32 else HBM)
    rows, model = get.tokens_hbm.shape
    columns = get.in_full_hbm.shape[1]
    block = get.down_keep.shape[3:]
    narrow, wide = HEADS * FDIM, HEADS * VDIM
    state = get.prefix_hbm.shape
    outs = dict(
        tokens_out=((rows, model), f32, HBM),
        down_out=((2, 8, *block), bf16, HBM),
        gate_out=((2, 8, *block), bf16, HBM),
        up_out=((2, 8, *block), bf16, HBM),
        out_out=((8, 32, model), bf16, HBM),
        in_out=((8, 32, columns), bf16, HBM),
        gains_out=((8, 128), f32, VMEM),
    )
    scratch = dict(
        down_core=((2, 2, 8, *block), bf16),
        gate_core=((2, 2, 8, *block), bf16),
        up_core=((2, 2, 8, *block), bf16),
        stage=((2, 2, 8, *block), bf16),
        crossed=((6, 8, *block), bf16),
        sided=((6, 4, *block), bf16),
        lined=((6, 3, *block), bf16),
        out_full=((wide, model), bf16),
        branch=((rows, model), bf16),
        atten=((wide, rows), bf16),
        denom=((HEADS, rows), f32),
        query=((narrow, rows), bf16),
        key=((narrow, rows), bf16),
        value=((wide, rows), bf16),
        prefix=(state, bf16),
        tokens=((rows, model), bf16),
        in_full=((model, columns), bf16),
        gmiddle=((rows, model), f32),
        grad=((wide, rows), f32),
        gnumer=((wide, rows), bf16),
        gdenom=((HEADS, rows), f32),
        states=(state, bf16),
        ring=((3, *state), bf16),
        total=((4, *state[1:]), f32),
        outgoing=(state, bf16),
        incoming=(state, bf16),
        gproj=((columns, rows), bf16),
        gkey_in=((narrow, rows), f32),
        normed=((rows, model), bf16),
        turned=((rows, columns), bf16),
        gains=((8, model), f32),
        small=((4, 8, 128), f32),
        small_in=((4, 8, 128), f32),
        small_line=((4, 8, 128), f32),
        out_base=((2, 8, 32, model), bf16),
        out_send=((2, 8, 32, model), bf16),
        out_core=((2, 8, 32, model), bf16),
        out_crossed=((8, 32, model), bf16),
        out_sided=((4, 32, model), bf16),
        out_lined=((3, 32, model), bf16),
        in_base=((2, 8, 32, columns), bf16),
        in_send=((2, 8, 32, columns), bf16),
        in_core=((2, 8, 32, columns), bf16),
        in_crossed=((8, 32, columns), bf16),
        in_sided=((4, 32, columns), bf16),
        in_lined=((3, 32, columns), bf16),
    )
    names += [*outs, *scratch, *dict(send_sems=0, recv_sems=0, local_sems=0)]
    return pl.pallas_call(
        functools.partial(backward_kernel, tuple(names)),
        out_shape=[jax.ShapeDtypeStruct(shape, dtype) for shape, dtype, _ in outs.values()],
        in_specs=specs,
        out_specs=[spec for _, _, spec in outs.values()],
        scratch_shapes=[pltpu.VMEM(shape, dtype) for shape, dtype in scratch.values()]
        + [sems(100), sems(100), sems(32)],
        compiler_params=pltpu.CompilerParams(collective_id=2, has_side_effects=True, vmem_limit_bytes=60 << 20),
    )(*values)


def body(count):
    def layer(
        tokens, block_pos, gain_attn, w_query, w_key, w_value, w_out, gain_ffn, w_gate, w_up, w_down, cotangent
    ):
        own = lax.axis_index("ctx")
        me = lax.axis_index("fsdp").astype(jnp.int32).reshape(1)
        positions = block_pos[0]
        in_shard = jnp.concatenate([w_query, w_key, w_value], axis=1)
        gains = jnp.stack([gain_attn, gain_ffn])
        if count == 8:
            gains, in_full = gather_call(gains, in_shard)
        else:
            gains, in_full = (lax.all_gather(a, "fsdp") for a in (gains, in_shard))
        gain_one, gain_two = (gains[:, k].reshape(-1).astype(f32) for k in (0, 1))
        in_full = in_full.reshape(-1, in_shard.shape[1])
        residual = tokens[0].astype(f32)
        rows = residual.shape[0]
        inv_one = lax.rsqrt(jnp.mean(residual * residual, axis=-1, keepdims=True) + EPS)
        normed_one = (residual * inv_one * gain_one).astype(bf16)
        narrow = HEADS * FDIM
        projected = dot(in_full, normed_one, (0, 1)).astype(bf16)
        query, key, value = projected[:narrow], projected[narrow : 2 * narrow], projected[2 * narrow :]

        unit = 2 * rows * BLOCK * HEADS
        (own_states,) = attention_call(
            states_kernel, ("narrow", "wide"), (("state", bf16),), rows, unit * FEAT
        )(key, value)
        weights = (w_out, w_gate.T, w_up.T, w_down)
        if count == 8:
            prefix, atten, denom, middle, out_full, gates, ups, downs = forward_call(
                block_pos, own_states, query, key, value, tokens[0], weights
            )
            out_full = out_full.reshape(-1, w_out.shape[1])
        else:
            numer, denom = attention_call(
                intra_kernel, ("narrow", "narrow", "wide"), (("wide", f32), ("head", f32)), rows, unit * 256
            )(query, key, value)
            links = Links()
            states = Exchange(own_states, positions, own, count, False)
            for _ in range(1, count // 2):
                states.passed(links.round([states.ring()])[0])
            prefix = states.total(links.round([states.partner()])[0])
            atten, denom = attention_call(
                inter_kernel,
                ("narrow", "state", "wide", "head"),
                (("wide", bf16), ("head", f32)),
                rows,
                unit * FEAT,
            )(query, prefix, numer, denom)
            out_full, gates, ups, downs = (lax.all_gather(w, "fsdp") for w in weights)
            out_full = out_full.reshape(-1, w_out.shape[1])
            middle = residual + dot(atten, out_full, (0, 0))
        results = ffn_call(me, middle, gain_two.reshape(1, -1), cotangent[0], gates, ups, downs)
        output, grad_middle, branch, grad_gain_two = results[:4]
        gate_keep, gate_send, up_keep, up_send, down_keep, down_send = results[4:]
        width = in_full.shape[1]
        pairs = ((down_keep, down_send), (gate_keep, gate_send), (up_keep, up_send))
        if count == 8:
            arrays = dict(
                places=block_pos,
                gain_one=gain_one.reshape(1, -1),
                ggain_two=grad_gain_two,
                out_full_hbm=out_full,
                branch_hbm=branch,
                atten_hbm=atten,
                denom_hbm=denom,
                query_hbm=query,
                key_hbm=key,
                value_hbm=value,
                prefix_hbm=prefix,
                tokens_hbm=tokens[0],
                in_full_hbm=in_full,
                gmiddle_hbm=grad_middle,
                down_keep=down_keep,
                down_send=down_send,
                gate_keep=gate_keep,
                gate_send=gate_send,
                up_keep=up_keep,
                up_send=up_send,
            )
            grad_tokens, down_sum, gate_sum, up_sum, out_sum, in_sum, small = backward_call(arrays)
            gain_sums = small[:4].reshape(2, -1)
        else:
            grad_atten = dot(out_full, branch, (1, 1))
            gnumer, gdenom, grad_states = attention_call(
                grad_states_kernel,
                ("narrow", "wide", "head", "wide"),
                (("wide", bf16), ("head", f32), ("state", bf16)),
                rows,
                unit * FEAT,
            )(query, atten, denom, grad_atten)
            gquery, gkey, gvalue = attention_call(
                intra_back_kernel,
                ("narrow", "narrow", "wide", "wide", "head", "state"),
                (("narrow", bf16), ("narrow", f32), ("wide", f32)),
                rows,
                unit * 512,
            )(query, key, value, gnumer, gdenom, prefix)
            links = Links()
            backward = Exchange(grad_states, positions, own, count, True)
            for _ in range(1, count // 2):
                backward.passed(links.round([backward.ring()])[0])
            later = backward.total(links.round([backward.partner()])[0])
            gkey, gvalue = attention_call(
                inter_back_kernel,
                ("narrow", "wide", "state", "narrow", "wide"),
                (("narrow", bf16), ("wide", bf16)),
                rows,
                unit * 256,
            )(key, value, later, gkey, gvalue)
            gprojected = jnp.concatenate([gquery, gkey, gvalue], axis=0)
            gnormed_one = dot(gprojected, in_full, (0, 1))
            weighted_one = gnormed_one * gain_one
            grad_gain_one = jnp.sum(gnormed_one * residual * inv_one, axis=0)
            grad_tokens = (
                grad_middle
                + inv_one * weighted_one
                - residual
                * (inv_one * inv_one * inv_one)
                * jnp.mean(weighted_one * residual, axis=-1, keepdims=True)
            )

            def summed(keep, send):
                got = lax.ppermute(send, "fsdp", CORE)
                cross = (keep[:, 1].astype(f32) + got[:, 1].astype(f32)).astype(bf16)
                got_cross = lax.ppermute(cross, "fsdp", CHIP)
                total = keep[:, 0].astype(f32) + got[:, 0].astype(f32) + got_cross.astype(f32)
                return lax.psum(total.astype(bf16), "ctx")

            def scattered(grad):
                return lax.psum(lax.psum_scatter(grad, "fsdp", scatter_dimension=0, tiled=True), "ctx")

            down_sum, gate_sum, up_sum = (summed(*pair) for pair in pairs)
            out_sum = scattered(dot(atten, branch, (1, 0)).astype(bf16)).reshape(8, -1, branch.shape[1])
            in_sum = scattered(dot(normed_one, gprojected, (0, 1)).astype(bf16)).reshape(8, -1, width)
            gain_sums = scattered(jnp.stack([grad_gain_one, grad_gain_two[0]], axis=1)).T
        model = branch.shape[1]
        down_grad, gate_grad, up_grad = settle_call(down_sum, gate_sum, up_sum)
        gate_grad, up_grad = gate_grad.T, up_grad.T
        out_grad = out_sum.reshape(-1, model).astype(f32)
        in_grad = in_sum.reshape(-1, width).astype(f32)
        return (
            output[None],
            grad_tokens[None],
            gain_sums[0],
            in_grad[:, :narrow],
            in_grad[:, narrow : 2 * narrow],
            in_grad[:, 2 * narrow : width],
            out_grad,
            gain_sums[1],
            gate_grad,
            up_grad,
            down_grad,
        )

    return layer


def solution(mesh):
    rows = P("fsdp", None)
    seqs = P("fsdp", "ctx", None)
    vec = P("fsdp")
    in_specs = (seqs, rows, vec, rows, rows, rows, rows, vec, rows, rows, rows, seqs)
    out_specs = (seqs, seqs, vec, rows, rows, rows, rows, vec, rows, rows, rows)
    return jax.shard_map(
        body(mesh.shape["ctx"]), mesh=mesh, in_specs=in_specs, out_specs=out_specs, check_vma=False
    )
```

```python
import functools
from types import SimpleNamespace

import jax
import jax.numpy as jnp
from jax import lax
from jax.experimental import pallas as pl
from jax.experimental.pallas import tpu as pltpu
from jax.sharding import PartitionSpec as P

HEADS = 16
FDIM = 16
VDIM = 64
BLOCK = 256
GROUP = 8
FEAT = 160
STATE = GROUP // 2 * FEAT + 2 * GROUP
EPS = 1e-05
ROOT_HALF = 0.7071067811865476

f32 = jnp.float32
bf16 = jnp.bfloat16


def dims(lhs, rhs):
    return (((lhs,), (rhs,)), ((), ()))


def dot(lhs, rhs, contract):
    return lax.dot_general(lhs, rhs, dims(*contract), preferred_element_type=f32)


def turned(u, shift):
    return pltpu.roll(u, FDIM - shift, 0)


def features(u, pair_weight):
    rows = [u, u * u * ROOT_HALF]
    for shift in range(1, 8):
        rows.append(u * turned(u, shift) * ROOT_HALF)
    rows.append(u[:8] * u[8:] * ROOT_HALF)
    one = (lax.broadcasted_iota(jnp.int32, (8, u.shape[1]), 0) == 0).astype(f32)
    linear = jnp.concatenate(rows[:2], axis=0).astype(bf16)
    pairs = jnp.concatenate(rows[2:], axis=0).astype(bf16) * pair_weight
    del rows
    return jnp.concatenate([linear.astype(f32), pairs.astype(f32), one], axis=0).astype(bf16)


def features_back(u, g):
    total = g[:16] + (2.0 * ROOT_HALF) * (g[16:32] * u)
    for shift in range(1, 8):
        here = (2.0 * ROOT_HALF) * g[16 + 16 * shift : 32 + 16 * shift]
        total = total + here * turned(u, shift) + pltpu.roll(here * u, shift, 0)
    here = (2.0 * ROOT_HALF) * g[144:152]
    return total + jnp.concatenate([here * u[8:], here * u[:8]], axis=0)


def halved(ref, head):
    return ref[head * FDIM : (head + 1) * FDIM, :].astype(f32) * 0.5


def write_states(out_ref, feat, value_pair, weight_row, head):
    pair = head // 2
    product = dot(feat, value_pair, (1, 1))
    half = slice(0, 64) if head % 2 == 0 else slice(64, 128)
    out_ref[0, 0, pair * FEAT : (pair + 1) * FEAT, half] = product[:, half].astype(bf16)
    norm = dot(weight_row, feat, (1, 1))
    base = GROUP // 2 * FEAT + 2 * head
    out_ref[0, 0, base : base + 1, :] = norm[:1, :128].astype(bf16)
    out_ref[0, 0, base + 1 : base + 2, :] = jnp.concatenate([norm[:1, 128:], jnp.zeros((1, 96), f32)], axis=1).astype(bf16)


def norm_row(state_ref, head):
    base = GROUP // 2 * FEAT + 2 * head
    return state_ref[0, 0, base : base + 1, :], state_ref[0, 0, base + 1 : base + 2, :32]


def head_state(state_ref, head):
    pair = head // 2
    return state_ref[0, 0, pair * FEAT : (pair + 1) * FEAT, 64 * (head % 2) : 64 * (head % 2) + 64]


def states_kernel(key_ref, value_ref, out_ref):
    ones = jnp.ones((8, BLOCK), bf16)
    for head in range(GROUP):
        feat = features(halved(key_ref, head), 1.0)
        pair = head // 2
        write_states(out_ref, feat, value_ref[pair * 128 : (pair + 1) * 128, :], ones, head)


def intra_kernel(query_ref, key_ref, value_ref, numer_ref, denom_ref):
    for head in range(GROUP):
        rows = slice(head * FDIM, (head + 1) * FDIM)
        wide = slice(head * VDIM, (head + 1) * VDIM)
        scores = dot(key_ref[rows, :], query_ref[rows, :], (0, 0)) * 0.25
        kernel = 1.0 + scores + 0.5 * scores * scores
        denom_ref[head : head + 1, :] = jnp.sum(kernel, axis=0, keepdims=True)
        numer_ref[wide, :] = dot(value_ref[wide, :], kernel.astype(bf16), (1, 0))


def inter_kernel(query_ref, prefix_ref, numer_ref, denom_in_ref, atten_ref, denom_ref):
    for head in range(GROUP):
        wide = slice(head * VDIM, (head + 1) * VDIM)
        feat = features(halved(query_ref, head), 2.0)
        numer = numer_ref[wide, :] + dot(head_state(prefix_ref, head), feat, (0, 0))
        first, second = norm_row(prefix_ref, head)
        denom = denom_in_ref[head : head + 1, :] + dot(first, feat[:128], (1, 0)) + dot(second, feat[128:], (1, 0))
        denom_ref[head : head + 1, :] = denom
        atten_ref[wide, :] = (numer / denom).astype(bf16)


def grad_states_kernel(query_ref, atten_ref, denom_ref, grad_ref, gnumer_ref, gdenom_ref, out_ref):
    for pair in range(GROUP // 2):
        for head in (2 * pair, 2 * pair + 1):
            wide = slice(head * VDIM, (head + 1) * VDIM)
            denom = denom_ref[head : head + 1, :]
            grad = grad_ref[wide, :]
            gnumer_ref[wide, :] = (grad / denom).astype(bf16)
            gdenom = -jnp.sum(grad * atten_ref[wide, :].astype(f32), axis=0, keepdims=True) / denom
            gdenom_ref[head : head + 1, :] = gdenom.astype(bf16).astype(f32)
        for head in (2 * pair, 2 * pair + 1):
            feat = features(halved(query_ref, head), 1.0)
            weights = jnp.broadcast_to(gdenom_ref[head : head + 1, :], (8, BLOCK)).astype(bf16)
            write_states(out_ref, feat, gnumer_ref[pair * 128 : (pair + 1) * 128, :], weights, head)


def intra_back_kernel(
    query_ref, key_ref, value_ref, gnumer_ref, gdenom_ref, prefix_ref, gquery_ref, gkey_ref, gvalue_ref
):
    for head in range(GROUP):
        rows = slice(head * FDIM, (head + 1) * FDIM)
        wide = slice(head * VDIM, (head + 1) * VDIM)
        query, key = query_ref[rows, :], key_ref[rows, :]
        gnumer = gnumer_ref[wide, :]
        gdenom = gdenom_ref[head : head + 1, :]
        scores = dot(key, query, (0, 0)) * 0.25
        kernel = (1.0 + scores + 0.5 * scores * scores).astype(bf16)
        gkernel = dot(value_ref[wide, :], gnumer, (0, 0)) + gdenom
        gscores = ((1.0 + scores) * gkernel).astype(bf16)
        gvalue_ref[wide, :] = dot(gnumer, kernel, (1, 1))
        gkey_ref[rows, :] = dot(query, gscores, (1, 1)) * 0.25
        first, second = norm_row(prefix_ref, head)
        gdenom_low = gdenom.astype(bf16)
        outer_prod = jnp.concatenate([dot(first, gdenom_low, (0, 0)), dot(second, gdenom_low, (0, 0))], axis=0)
        gfeat = dot(head_state(prefix_ref, head), gnumer, (1, 0)) + outer_prod
        gquery = dot(key, gscores, (1, 0)) * 0.25 + 0.5 * features_back(halved(query_ref, head), gfeat)
        gquery_ref[rows, :] = gquery.astype(bf16)


def inter_back_kernel(key_ref, value_ref, later_ref, gkey_in_ref, gvalue_in_ref, gkey_ref, gvalue_ref):
    ones = jnp.ones((1, BLOCK), bf16)
    for head in range(GROUP):
        rows = slice(head * FDIM, (head + 1) * FDIM)
        wide = slice(head * VDIM, (head + 1) * VDIM)
        u = halved(key_ref, head)
        state = head_state(later_ref, head)
        first, second = norm_row(later_ref, head)
        outer_prod = jnp.concatenate([dot(first, ones, (0, 0)), dot(second, ones, (0, 0))], axis=0)
        gfeat = dot(state, value_ref[wide, :], (1, 0)) + outer_prod
        gkey_ref[rows, :] = (gkey_in_ref[rows, :] + 0.5 * features_back(u, gfeat)).astype(bf16)
        feat = features(u, 2.0)
        gvalue_ref[wide, :] = (gvalue_in_ref[wide, :] + dot(state, feat, (0, 0))).astype(bf16)


def attention_call(kernel, ins, outs, tokens, flops):
    blocks = tokens // BLOCK
    groups = HEADS // GROUP
    forms = {
        "narrow": ((GROUP * FDIM, BLOCK), lambda b, g: (g, b), (HEADS * FDIM, tokens)),
        "wide": ((GROUP * VDIM, BLOCK), lambda b, g: (g, b), (HEADS * VDIM, tokens)),
        "head": ((GROUP, BLOCK), lambda b, g: (g, b), (HEADS, tokens)),
        "state": ((1, 1, STATE, 128), lambda b, g: (b, g, 0, 0), (blocks, groups, STATE, 128)),
    }

    def spec(name):
        return pl.BlockSpec(forms[name][0], forms[name][1])

    def call(*arrays):
        moved = sum(a.size * a.dtype.itemsize for a in arrays)
        return pl.pallas_call(
            kernel,
            out_shape=[jax.ShapeDtypeStruct(forms[name][2], dtype) for name, dtype in outs],
            grid=(blocks, groups),
            in_specs=[spec(name) for name in ins],
            out_specs=[spec(name) for name, _ in outs],
            compiler_params=pltpu.CompilerParams(vmem_limit_bytes=40 << 20),
            cost_estimate=pl.CostEstimate(flops=flops, bytes_accessed=2 * moved, transcendentals=0),
        )(*arrays)

    return call


ORDER = (0, 2, 1, 3)


def place(step):
    return (step % 2) * 2 + step // 2


def ffn_begin(me, middle_ref, gain_ref, cot_ref, normed, x_own, x_turned, cot_turned, total, gnormed, inverse):
    width = x_own.shape[2]
    core = me + 1 - 2 * (me % 2)
    normed[...] = (middle_ref[...] * inverse() * gain_ref[...]).astype(bf16)
    for r, shard in enumerate((me, core, (me + 2) % 4, (core + 2) % 4)):
        x_own[r] = normed[:, pl.ds(pl.multiple_of(shard * width, width), width)]
    x_turned[...] = normed[...].T
    cot_turned[...] = cot_ref[...].T
    total[...] = jnp.zeros_like(total)
    gnormed[...] = jnp.zeros_like(gnormed)


def ffn_tile(gates, ups, down, x_turned, cot_turned):
    width = gates.shape[2]
    x_part = x_turned[:width, :]
    gate = dot(gates[0], x_part, (1, 0))
    up = dot(ups[0], x_part, (1, 0))
    for r in range(1, 4):
        x_part = x_turned[r * width : (r + 1) * width, :]
        gate = gate + dot(gates[r], x_part, (1, 0))
        up = up + dot(ups[r], x_part, (1, 0))
    ghidden = dot(down, cot_turned[...], (1, 0))
    sigmoid = jax.nn.sigmoid(gate)
    silu = gate * sigmoid
    hidden = (silu * up).astype(bf16)
    ggate = (ghidden * up * (sigmoid * (1.0 + gate * (1.0 - sigmoid)))).astype(bf16)
    return hidden, ggate, (ghidden * silu).astype(bf16)


def ffn_end(middle_ref, gain_ref, cot_ref, total, gnormed, inverse, output_ref, gmiddle_ref, branch_ref, ggain_ref):
    middle, inv, cot = middle_ref[...], inverse(), cot_ref[...].astype(f32)
    grad = gnormed[...]
    output_ref[...] = (middle + total[...]).astype(bf16)
    ggain_ref[...] = jnp.broadcast_to(jnp.sum(grad * middle * inv, axis=0, keepdims=True), ggain_ref.shape)
    weighted = grad * gain_ref[...]
    slope = jnp.mean(weighted * middle, axis=-1, keepdims=True)
    gmiddle = cot + inv * weighted - middle * (inv * inv * inv) * slope
    gmiddle_ref[...] = gmiddle
    branch_ref[...] = gmiddle.astype(bf16)


def ffn_kernel(me_ref, middle_ref, gain_ref, cot_ref, gates, ups, downs, *refs):
    output_ref, gmiddle_ref, branch_ref, ggain_ref = refs[:4]
    gate_keep, gate_send, up_keep, up_send, down_keep, down_send = refs[4:10]
    normed, x_own, x_turned, cot_turned, total, gnormed = refs[10:]
    step = pl.program_id(0)
    width = gates.shape[2]

    def inverse():
        middle = middle_ref[...]
        return lax.rsqrt(jnp.mean(middle * middle, axis=-1, keepdims=True) + EPS)

    @pl.when(step == 0)
    def _():
        ffn_begin(
            me_ref[0], middle_ref, gain_ref, cot_ref, normed, x_own, x_turned, cot_turned, total, gnormed, inverse
        )

    hidden, ggate, gup = ffn_tile(gates, ups, downs[0], x_turned, cot_turned)
    down = downs[0]
    total[...] += dot(hidden, down, (0, 0))
    gdown = dot(hidden, cot_ref[...], (1, 0))
    tall, broad = down_keep.shape[3:]

    def store(ref, slot, grad):
        for half in range(2):
            for eighth in range(8):
                ref[half, slot, eighth] = grad[
                    half * tall : (half + 1) * tall, eighth * broad : (eighth + 1) * broad
                ].astype(bf16)

    @pl.when(step < 2)
    def _():
        store(down_keep, 0, gdown)

    @pl.when(step >= 2)
    def _():
        store(down_send, 0, gdown)

    def store_turned(keep, send, r, grad):
        ref = send if r % 2 else keep
        for half in range(2):
            for eighth in range(2):
                ref[half, r // 2, eighth] = grad[
                    eighth * tall : (eighth + 1) * tall, half * broad : (half + 1) * broad
                ].astype(bf16)

    for r in range(4):
        part = slice(r * width, (r + 1) * width)
        gnormed[:, part] += dot(ggate, gates[r], (0, 0)) + dot(gup, ups[r], (0, 0))
        store_turned(gate_keep, gate_send, r, dot(ggate, x_own[r], (1, 0)))
        store_turned(up_keep, up_send, r, dot(gup, x_own[r], (1, 0)))

    @pl.when(step == 3)
    def _():
        ffn_end(middle_ref, gain_ref, cot_ref, total, gnormed, inverse, output_ref, gmiddle_ref, branch_ref, ggain_ref)


def ffn_call(me, middle, gain, cot, gates, ups, downs):
    rows, model = middle.shape
    _, hidden, width = gates.shape
    tile = downs.shape[1]
    once = pl.Buffered(1)

    def whole(shape, **kw):
        return pl.BlockSpec(shape, lambda s, me: (0,) * len(shape), **kw)

    columns = pl.BlockSpec((4, tile, width), lambda s, me: (0, me[0] ^ place(s), 0))
    block = (tile // 2, model // 8)
    pair = pl.BlockSpec((2, 2, 2, *block), lambda s, me: (0, 0, me[0] ^ place(s), 0, 0))
    grads = jax.ShapeDtypeStruct((2, 2, 8, *block), bf16)
    return pl.pallas_call(
        ffn_kernel,
        out_shape=[
            jax.ShapeDtypeStruct((rows, model), bf16),
            jax.ShapeDtypeStruct((rows, model), f32),
            jax.ShapeDtypeStruct((rows, model), bf16),
            jax.ShapeDtypeStruct((8, model), f32),
            grads,
            grads,
            grads,
            grads,
            grads,
            grads,
        ],
        grid_spec=pltpu.PrefetchScalarGridSpec(
            num_scalar_prefetch=1,
            grid=(4,),
            in_specs=[
                whole((rows, model), pipeline_mode=once),
                whole((1, model)),
                whole((rows, model), pipeline_mode=once),
                columns,
                columns,
                pl.BlockSpec((1, tile, model), lambda s, me: (me[0] ^ place(s), 0, 0)),
            ],
            out_specs=[
                whole((rows, model), pipeline_mode=once),
                whole((rows, model), pipeline_mode=once),
                whole((rows, model), pipeline_mode=once),
                whole((8, model)),
                pair,
                pair,
                pair,
                pair,
                pl.BlockSpec((2, 1, 8, *block), lambda s, me: (0, jnp.minimum(s, 1), 0, 0, 0)),
                pl.BlockSpec((2, 1, 8, *block), lambda s, me: (0, jnp.maximum(s - 2, 0), 0, 0, 0)),
            ],
            scratch_shapes=[
                pltpu.VMEM((rows, model), bf16),
                pltpu.VMEM((4, rows, width), bf16),
                pltpu.VMEM((model, rows), bf16),
                pltpu.VMEM((model, rows), bf16),
                pltpu.VMEM((rows, model), f32),
                pltpu.VMEM((rows, model), f32),
            ],
        ),
        compiler_params=pltpu.CompilerParams(vmem_limit_bytes=58 << 20),
        cost_estimate=pl.CostEstimate(
            flops=18 * rows * model * hidden, bytes_accessed=14 * hidden * model, transcendentals=0
        ),
    )(me, middle, gain, cot, gates, ups, downs)


CORE = [(0, 1), (1, 0), (2, 3), (3, 2)]
CHIP = [(0, 2), (2, 0), (1, 3), (3, 1)]


class Links:
    def __init__(self):
        self.last = ()

    def round(self, sends, beside=()):
        arrays = [send[0] for send in sends]
        if self.last:
            arrays = lax.optimization_barrier((*arrays, *self.last))[: len(arrays)]
        results = [lax.ppermute(a, axis, perm) for a, (_, axis, perm) in zip(arrays, sends)]
        self.last = (*results, *beside)
        return results


def trade(array, bits, count):
    return array, "ctx", [(i, i ^ bits) for i in range(count)]


MESH = pl.DeviceIdType.MESH


class Spot:
    def __init__(self):
        self.me = lax.axis_index("fsdp")
        self.own = lax.axis_index("ctx")
        self.core = {"fsdp": self.me + 1 - 2 * (self.me % 2)}
        self.across = (self.me + 2) % 4
        self.chip = {"fsdp": self.across}
        self.y = self.own % 2
        self.z = self.own // 2
        self.side = {"ctx": self.own + 1 - 2 * self.y}
        self.next = {"ctx": self.own + 2 - 4 * (self.z % 2)}
        self.ahead = [None] + [{"ctx": (self.own + 2 * k) % 8} for k in (1, 2, 3)]

    def greet(self, neighbours):
        barrier = pltpu.get_barrier_semaphore()
        for neighbour in neighbours:
            pl.semaphore_signal(barrier, inc=1, device_id=neighbour, device_id_type=MESH)
        pl.semaphore_wait(barrier, len(neighbours))


class Wire:
    def __init__(self, send_sems, recv_sems, local_sems):
        self.send_sems, self.recv_sems, self.local_sems = send_sems, recv_sems, local_sems
        self.sent, self.local, self.count = [], [], 0

    def send(self, source, target, device):
        k = self.count
        self.count += 1
        copy = pltpu.make_async_remote_copy(
            src_ref=source,
            dst_ref=target,
            send_sem=self.send_sems.at[k],
            recv_sem=self.recv_sems.at[k],
            device_id=device,
            device_id_type=MESH,
        )
        copy.start()
        self.sent.append(copy)
        return copy

    def keep(self, source, target):
        copy = pltpu.make_async_copy(source, target, self.local_sems.at[len(self.local)])
        copy.start()
        self.local.append(copy)
        return copy

    def left(self, copy):
        copy.wait_send()
        self.sent = [other for other in self.sent if other is not copy]

    def end(self):
        for copy in self.sent:
            copy.wait_send()


def tile_at(step):
    me = lax.axis_index("fsdp")
    place = 3 - step
    return 2 * ((me // 2 + place // 2) % 2) + (me % 2 + place) % 2


def ffn_send_kernel(middle_ref, gain_ref, cot_ref, gates, ups, downs, *refs):
    output_ref, gmiddle_ref, branch_ref, ggain_ref = refs[:4]
    gate_keep, up_keep, down_keep, down_cross, gate_got, up_got, down_got, crossed = refs[4:12]
    normed, x_own, x_turned, cot_turned, total, gnormed = refs[12:18]
    sending, down_first, down_second, down_in, crossing, send_sems, recv_sems = refs[18:]
    step = pl.program_id(0)
    spot = Spot()
    tall, broad = down_keep.shape[2:]
    width = gates.shape[2]

    def copy(k, source, target, device):
        return pltpu.make_async_remote_copy(
            src_ref=source,
            dst_ref=target,
            send_sem=send_sems.at[k],
            recv_sem=recv_sems.at[k],
            device_id=device,
            device_id_type=MESH,
        )

    def tile_copy(at, which):
        got = (gate_got, up_got)[which].at[:, :, pl.ds(2 * tile_at(at), 2)]
        return copy(2 * at + which, sending.at[at % 2, which], got, spot.core)

    first = copy(8, down_first, down_in, spot.core)
    second = copy(9, down_second, down_got, spot.core)
    cross = copy(10, crossing, crossed, spot.chip)

    def inverse():
        middle = middle_ref[...]
        return lax.rsqrt(jnp.mean(middle * middle, axis=-1, keepdims=True) + EPS)

    @pl.when(step == 0)
    def _():
        spot.greet([spot.core, spot.chip])
        ffn_begin(
            spot.me, middle_ref, gain_ref, cot_ref, normed, x_own, x_turned, cot_turned, total, gnormed, inverse
        )

    hidden, ggate, gup = ffn_tile(gates, ups, downs[0], x_turned, cot_turned)
    gdown = dot(hidden, cot_ref[...], (1, 0))

    def down_block(half, eighth):
        return gdown[half * tall : (half + 1) * tall, eighth * broad : (eighth + 1) * broad]

    def store(ref):
        for half in range(2):
            for eighth in range(8):
                ref[half, eighth] = down_block(half, eighth).astype(bf16)

    @pl.when(step == 0)
    def _():
        store(down_first)
        first.start()

    @pl.when(step == 1)
    def _():
        first.wait_recv()
        for half, ref in enumerate((crossing, down_cross)):
            for eighth in range(8):
                ref[eighth] = (down_block(half, eighth) + down_in[half, eighth].astype(f32)).astype(bf16)
        cross.start()

    @pl.when(step == 2)
    def _():
        store(down_second)
        second.start()

    @pl.when(step == 3)
    def _():
        store(down_keep)

    for at in range(4):

        @pl.when(step == at)
        def _(at=at):
            if at >= 2:
                tile_copy(at - 2, 0).wait_send()
                tile_copy(at - 2, 1).wait_send()
            for which, grad in enumerate((ggate, gup)):
                for slot in range(2):
                    value = dot(grad, x_own[2 * slot + 1], (1, 0))
                    for half in range(2):
                        for eighth in range(2):
                            sending[at % 2, which, half, slot, eighth] = value[
                                eighth * tall : (eighth + 1) * tall, half * broad : (half + 1) * broad
                            ].astype(bf16)
                tile_copy(at, which).start()

    for grad, ref in ((ggate, gate_keep), (gup, up_keep)):
        for slot in range(2):
            value = dot(grad, x_own[2 * slot], (1, 0))
            for half in range(2):
                for eighth in range(2):
                    ref[half, slot, eighth] = value[
                        eighth * tall : (eighth + 1) * tall, half * broad : (half + 1) * broad
                    ].astype(bf16)
    for r in range(4):
        part = slice(r * width, (r + 1) * width)
        gnormed[:, part] += dot(ggate, gates[r], (0, 0)) + dot(gup, ups[r], (0, 0))
    total[...] += dot(hidden, downs[0], (0, 0))

    @pl.when(step == 3)
    def _():
        ffn_end(middle_ref, gain_ref, cot_ref, total, gnormed, inverse, output_ref, gmiddle_ref, branch_ref, ggain_ref)
        for at in range(4):
            for which in range(2):
                tile_copy(at, which).wait_recv()
                if at >= 2:
                    tile_copy(at, which).wait_send()
        first.wait_send()
        second.wait()
        cross.wait()


def ffn_send_call(middle, gain, cot, gates, ups, downs):
    rows, model = middle.shape
    width = gates.shape[2]
    tile = downs.shape[1]
    once = pl.Buffered(1)
    block = (tile // 2, model // 8)

    def whole(*shape, **kw):
        return pl.BlockSpec(shape, lambda s: (0,) * len(shape), **kw)

    columns = pl.BlockSpec((4, tile, width), lambda s: (0, tile_at(s), 0))
    pair = pl.BlockSpec((2, 2, 2, *block), lambda s: (0, 0, tile_at(s), 0, 0))
    grads = jax.ShapeDtypeStruct((2, 2, 8, *block), bf16)
    halves = jax.ShapeDtypeStruct((2, 8, *block), bf16)
    one = jax.ShapeDtypeStruct((8, *block), bf16)
    return pl.pallas_call(
        ffn_send_kernel,
        out_shape=[
            jax.ShapeDtypeStruct((rows, model), bf16),
            jax.ShapeDtypeStruct((rows, model), f32),
            jax.ShapeDtypeStruct((rows, model), bf16),
            jax.ShapeDtypeStruct((8, model), f32),
            grads,
            grads,
            halves,
            one,
            grads,
            grads,
            halves,
            one,
        ],
        grid=(4,),
        in_specs=[
            whole(rows, model, pipeline_mode=once),
            whole(1, model),
            whole(rows, model, pipeline_mode=once),
            columns,
            columns,
            pl.BlockSpec((1, tile, model), lambda s: (tile_at(s), 0, 0)),
        ],
        out_specs=[
            whole(rows, model, pipeline_mode=once),
            whole(rows, model, pipeline_mode=once),
            whole(rows, model, pipeline_mode=once),
            whole(8, model),
            pair,
            pair,
            whole(2, 8, *block, pipeline_mode=once),
            whole(8, *block, pipeline_mode=once),
            HBM,
            HBM,
            HBM,
            HBM,
        ],
        scratch_shapes=[
            pltpu.VMEM((rows, model), bf16),
            pltpu.VMEM((4, rows, width), bf16),
            pltpu.VMEM((model, rows), bf16),
            pltpu.VMEM((model, rows), bf16),
            pltpu.VMEM((rows, model), f32),
            pltpu.VMEM((rows, model), f32),
            pltpu.VMEM((2, 2, 2, 2, 2, *block), bf16),
            pltpu.VMEM((2, 8, *block), bf16),
            pltpu.VMEM((2, 8, *block), bf16),
            pltpu.VMEM((2, 8, *block), bf16),
            pltpu.VMEM((8, *block), bf16),
            sems(11),
            sems(11),
        ],
        compiler_params=pltpu.CompilerParams(collective_id=3, has_side_effects=True, vmem_limit_bytes=60 << 20),
    )(middle, gain, cot, gates, ups, downs)


class Gather:
    def __init__(self, wire, spot, shard, full, held, axis, split, chunks):
        self.wire, self.spot, self.full, self.axis, self.split = wire, spot, full, axis, split
        self.part = shard.shape[axis] // (2 if split else 1)
        self.size = self.part // chunks
        me = spot.me
        self.held, self.loaded = held, wire.keep(shard, held)
        here = [self.view(shard, c, spot.y) for c in range(chunks)]
        there = [self.view(full.at[me], c, spot.y) for c in range(chunks)]
        self.cross = [wire.send(a, b, spot.chip) for a, b in zip(here, there)]
        self.near = wire.send(shard, full.at[me], spot.core)
        self.side, self.far = {}, []

    def write(self):
        self.loaded.wait()
        self.own = self.wire.keep(self.held, self.full.at[self.spot.me])

    def view(self, ref, chunk, y):
        start = chunk * self.size + (y * self.part if self.split else 0)
        index = [slice(None)] * 2
        index[self.axis] = pl.ds(pl.multiple_of(start, self.size), self.size)
        return ref.at[tuple(index)]

    def relay(self, chunk):
        self.cross[chunk].wait_recv()
        part = self.view(self.full.at[self.spot.across], chunk, self.spot.y)
        if self.split:
            self.side[chunk] = self.wire.send(part, part, self.spot.side)
        self.far.append(self.wire.send(part, part, self.spot.core))

    def relay_other(self, chunk):
        self.side[chunk].wait_recv()
        part = self.view(self.full.at[self.spot.across], chunk, 1 - self.spot.y)
        self.far.append(self.wire.send(part, part, self.spot.core))

    def end(self):
        self.own.wait()
        self.near.wait_recv()
        for copy in self.far:
            copy.wait_recv()


def gather_kernel(gain_ref, in_ref, gain_full, in_full, held, gain_held, send_sems, recv_sems, local_sems):
    spot = Spot()
    wire = Wire(send_sems, recv_sems, local_sems)
    spot.greet([spot.core, spot.chip, spot.side])
    weight = Gather(wire, spot, in_ref, in_full, held, 0, True, 2)
    gain_loaded = wire.keep(gain_ref, gain_held)
    near = wire.send(gain_ref, gain_full.at[spot.me], spot.core)
    cross = wire.send(gain_ref, gain_full.at[spot.me], spot.chip)
    weight.write()
    gain_loaded.wait()
    own = wire.keep(gain_held, gain_full.at[spot.me])
    weight.relay(0)
    weight.relay(1)
    weight.relay_other(0)
    cross.wait_recv()
    far = wire.send(gain_full.at[spot.across], gain_full.at[spot.across], spot.core)
    weight.relay_other(1)
    own.wait()
    near.wait_recv()
    far.wait_recv()
    weight.end()
    wire.end()


class StateSum:
    def __init__(self, wire, spot, places_ref, later, states, beside, outgoing, ring, result):
        self.wire, self.spot, self.states, self.beside = wire, spot, states, beside
        self.outgoing, self.ring, self.result = outgoing, ring, result
        self.sent = {}

        def place(device, block):
            return places_ref[0, 2 * device + block]

        partner = spot.own + 1 - 2 * spot.y
        sources = [place(device, block) for device in (spot.own, partner) for block in range(2)]
        self.masks = {}
        for k in range(4):
            for block in range(2):
                target = place((spot.own + 8 - 2 * k) % 8, block)
                self.masks[k, block] = [
                    jnp.where(source > target if later else source < target, 1.0, 0.0).astype(f32)
                    for source in sources
                ]

    def part(self, k, block, group):
        refs = (self.states.at[0], self.states.at[1], self.beside.at[0], self.beside.at[1])
        terms = [ref[group].astype(f32) * mask for ref, mask in zip(refs, self.masks[k, block])]
        return (terms[0] + terms[1]) + (terms[2] + terms[3])

    def trade(self):
        self.traded = self.wire.send(self.states, self.beside, self.spot.side)

    def first(self, block):
        if block == 0:
            self.traded.wait_recv()
        for group in range(HEADS // GROUP):
            self.outgoing[block, group] = self.part(1, block, group).astype(bf16)
        self.sent[0, block] = self.wire.send(self.outgoing.at[block], self.ring.at[0, block], self.spot.ahead[1])

    def hop(self, step, block):
        self.sent[step, block].wait_recv()
        target = self.result if step == 2 else self.ring.at[step]
        for group in range(HEADS // GROUP):
            value = self.ring[step, block, group].astype(f32) + self.part((step + 2) % 4, block, group)
            target[block, group] = value.astype(bf16)
        if step < 2:
            self.sent[step + 1, block] = self.wire.send(
                self.ring.at[step, block], self.ring.at[step + 1, block], self.spot.ahead[1]
            )


def forward_kernel(places_ref, states_ref, query_ref, key_ref, value_ref, tokens_ref, *refs):
    weights, (prefix_ref, atten_ref, denom_ref, middle_ref), fulls = refs[:4], refs[4:8], refs[8:12]
    ring, outgoing, beside, numer, inner, out_full = refs[12:18]
    held, (send_sems, recv_sems, local_sems) = refs[18:23], refs[23:]
    spot = Spot()
    wire = Wire(send_sems, recv_sems, local_sems)
    spot.greet([spot.core, spot.chip, spot.side, spot.ahead[1], spot.ahead[3]])
    sums = StateSum(wire, spot, places_ref, False, states_ref, beside, outgoing, ring, prefix_ref)
    sums.trade()
    out_w, gate_w, up_w, down_w = weights
    half = down_w.shape[1] // 2
    left, right = slice(0, half), slice(half, 2 * half)
    out = Gather(wire, spot, out_w, fulls[0], held[0], 0, True, 1)
    gate = Gather(wire, spot, gate_w, fulls[1], held[1], 0, True, 2)
    up = Gather(wire, spot, up_w, fulls[2], held[2], 0, True, 2)
    down_left = Gather(wire, spot, down_w.at[:, left], fulls[3].at[:, :, left], held[3], 1, True, 1)
    down_right = Gather(wire, spot, down_w.at[:, right], fulls[3].at[:, :, right], held[4], 1, False, 2)
    everything = (out, gate, up, down_left, down_right)
    intra = list(grid_views((query_ref, FDIM), (key_ref, FDIM), (value_ref, VDIM), (numer, VDIM), (inner, 1)))
    intra_kernel(*intra[0])
    for one in everything:
        one.write()
    intra_kernel(*intra[1])
    out.relay(0)
    intra_kernel(*intra[2])
    intra_kernel(*intra[3])
    gate.relay(0)
    sums.first(0)
    sums.first(1)
    gate.relay(1)
    out.relay_other(0)
    sums.hop(0, 0)
    out.end()
    shard = out_w.shape[0]
    loads = [wire.keep(fulls[0].at[k], out_full.at[k * shard : (k + 1) * shard]) for k in range(4)]
    up.relay(0)
    gate.relay_other(0)
    sums.hop(0, 1)
    up.relay(1)
    gate.relay_other(1)
    sums.hop(1, 0)
    down_left.relay(0)
    up.relay_other(0)
    sums.hop(1, 1)
    down_right.relay(0)
    up.relay_other(1)
    sums.hop(2, 0)
    down_right.relay(1)
    down_left.relay_other(0)
    sums.hop(2, 1)
    for parts in grid_views(
        (query_ref, FDIM), (prefix_ref, None), (numer, VDIM), (inner, 1), (atten_ref, VDIM), (denom_ref, 1)
    ):
        inter_kernel(*parts)
    for copy in loads:
        copy.wait()
    middle_ref[...] = tokens_ref[...].astype(f32) + dot(atten_ref[...], out_full[...], (0, 0))
    for one in everything[1:]:
        one.end()
    wire.end()


def grid_views(*refs):
    for block in range(2):
        for group in range(HEADS // GROUP):
            columns = slice(block * BLOCK, (block + 1) * BLOCK)
            parts = []
            for ref, rows in refs:
                if rows is None:
                    parts.append(ref.at[block : block + 1, group : group + 1])
                else:
                    parts.append(ref.at[group * GROUP * rows : (group + 1) * GROUP * rows, columns])
            yield parts


def add_chunks(total, first, other, count):
    def one(k, carry):
        total[first + k] = (total[first + k].astype(f32) + other[k].astype(f32)).astype(bf16)
        return carry

    lax.fori_loop(0, count, one, 0)


class Flow:
    def __init__(self, wire, spot, kept, sent, crossed, sided, lined, result):
        self.wire, self.spot = wire, spot
        self.kept, self.sent, self.crossed, self.sided, self.lined, self.result = kept, sent, crossed, sided, lined, result
        self.half = spot.y * 4
        self.pair = self.half + 2 * (spot.z % 2)
        self.mine = self.pair + spot.z // 2

    def cross(self):
        self.arrive = self.wire.send(self.sent, self.crossed, self.spot.chip).wait_recv

    def to_side(self):
        self.arrive()
        add_chunks(self.crossed, 0, self.kept, 8)
        there = pl.ds(4 - self.half, 4)
        self.s = self.wire.send(self.crossed.at[there], self.sided, self.spot.side)

    def to_line(self):
        self.s.wait_recv()
        add_chunks(self.crossed, self.half, self.sided, 4)
        there = pl.ds(2 * self.half + 2 - self.pair, 2)
        self.l = self.wire.send(self.crossed.at[there], self.lined.at[0:2], self.spot.next)

    def to_far(self):
        self.l.wait_recv()
        add_chunks(self.crossed, self.pair, self.lined, 2)
        self.f = self.wire.send(self.crossed.at[2 * self.pair + 1 - self.mine], self.lined.at[2], self.spot.ahead[2])

    def from_far(self):
        self.f.wait_recv()
        mine = self.mine
        self.crossed[mine] = (self.crossed[mine].astype(f32) + self.lined[2].astype(f32)).astype(bf16)
        self.own = self.wire.keep(self.crossed.at[mine], self.result.at[mine])
        self.g = self.wire.send(self.crossed.at[mine], self.result.at[mine], self.spot.ahead[2])

    def along_line(self):
        self.own.wait()
        self.g.wait_recv()
        here = self.result.at[pl.ds(self.pair, 2)]
        self.a = self.wire.send(here, here, self.spot.next)

    def along_side(self):
        self.a.wait_recv()
        here = self.result.at[pl.ds(self.half, 4)]
        self.b = self.wire.send(here, here, self.spot.side)

    def end(self):
        self.b.wait_recv()


def backward_kernel(names, *refs):
    r = SimpleNamespace(**dict(zip(names, refs)))
    spot = Spot()
    wire = Wire(r.send_sems, r.recv_sems, r.local_sems)
    me, z = spot.me, spot.z
    spot.greet([spot.core, spot.chip, spot.side, *spot.ahead[1:]])

    def load(*pairs):
        return [wire.keep(a, b) for a, b in pairs]

    def ready(copies):
        for copy in copies:
            copy.wait()

    first = load(
        (r.out_full_hbm, r.out_full),
        (r.branch_hbm, r.branch),
        (r.atten_hbm, r.atten),
        (r.denom_hbm, r.denom),
        (r.query_hbm, r.query),
    )
    arrived = load((r.first_cross, r.crossed.at[0]))
    down_loads = load((r.down_got, r.down_core), (r.down_keep, r.down_stage))
    kept, held = (r.gate_keep, r.up_keep), (r.gate_core, r.up_core)
    bases = (0, 1, 2, 3)
    stage = r.stage
    got = {weight: load((ref, held[weight])) for weight, ref in ((bases[0] // 2, (r.gate_got, r.up_got)[bases[0] // 2]),)}
    staged = {}

    def fetch(index):
        weight, half = bases[index] // 2, bases[index] % 2
        staged[index] = wire.keep(kept[weight].at[half], stage.at[index % 2])

    fetch(0)
    fetch(1)
    second = load((r.key_hbm, r.key), (r.value_hbm, r.value), (r.prefix_hbm, r.prefix))
    other = 1 - bases[0] // 2
    got[other] = load(((r.gate_got, r.up_got)[other], held[other]))
    tokens_load = load((r.tokens_hbm, r.tokens))
    third = load((r.in_full_hbm, r.in_full), (r.gmiddle_hbm, r.gmiddle))

    def base(index):
        weight, half = bases[index] // 2, bases[index] % 2
        ready(got[weight])
        got[weight] = []
        staged[index].wait()
        for slot in range(2):
            add_chunks(held[weight].at[half, slot], 0, stage.at[index % 2, slot], 8)
        if index < 2:
            fetch(index + 2)

    def down_base():
        ready(down_loads)
        for half in range(2):
            add_chunks(r.down_core.at[half], 0, r.down_stage.at[half], 8)

    def flow(index, kept_ref, sent_ref, result):
        return Flow(wire, spot, kept_ref, sent_ref, r.crossed.at[index], r.sided.at[index], r.lined.at[index], result)

    da, db = (flow(half, r.down_core.at[half], r.second_cross, r.down_out.at[half]) for half in range(2))
    da.arrive = arrived[0].wait
    ga, gb = (flow(2 + half, r.gate_core.at[half, 0], r.gate_core.at[half, 1], r.gate_out.at[half]) for half in range(2))
    ua, ub = (flow(4 + half, r.up_core.at[half, 0], r.up_core.at[half, 1], r.up_out.at[half]) for half in range(2))
    out_flow = Flow(
        wire, spot, r.out_base.at[0], r.out_base.at[1], r.out_crossed, r.out_sided, r.out_lined, r.out_out
    )
    in_flow = Flow(wire, spot, r.in_base.at[0], r.in_base.at[1], r.in_crossed, r.in_sided, r.in_lined, r.in_out)
    states, gnumer, gdenom, grad = r.states, r.gnumer, r.gdenom, r.grad
    sums = StateSum(wire, spot, r.places, True, states, r.beside, r.outgoing, r.ring, r.later)

    def grad_atten():
        ready(first)
        grad[...] = dot(r.out_full[...], r.branch[...], (1, 1))

    def grad_states():
        for parts in grid_views(
            (r.query, FDIM), (r.atten, VDIM), (r.denom, 1), (grad, VDIM), (gnumer, VDIM), (gdenom, 1), (states, None)
        ):
            grad_states_kernel(*parts)
        sums.trade()

    core_of = me + 1 - 2 * (me % 2)
    shards = (me, spot.across, core_of, (core_of + 2) % 4)
    width = r.branch.shape[1] // 4

    def out_grads(other):
        for slot in range(2):
            rows = pl.ds(pl.multiple_of(shards[2 * other + slot] * width, width), width)
            value = dot(r.atten[rows, :], r.branch[...], (1, 0))
            ref = r.out_send if other else r.out_base
            for k in range(8):
                ref[slot, k] = value[k * 32 : (k + 1) * 32, :].astype(bf16)
        if other:
            r.out_wait = wire.send(r.out_send, r.out_core, spot.core).wait_recv

    def out_base():
        r.out_wait()
        for slot in range(2):
            add_chunks(r.out_base.at[slot], 0, r.out_core.at[slot], 8)

    narrow = HEADS * FDIM
    gproj = r.gproj
    gquery, gkey = gproj.at[0:narrow], gproj.at[narrow : 2 * narrow]
    gvalue = gproj.at[2 * narrow : 2 * narrow + HEADS * VDIM]
    intra_views = list(
        grid_views(
            (r.query, FDIM),
            (r.key, FDIM),
            (r.value, VDIM),
            (gnumer, VDIM),
            (gdenom, 1),
            (r.prefix, None),
            (gquery, FDIM),
            (r.gkey_in, FDIM),
            (grad, VDIM),
        )
    )

    def intra(index):
        if index == 0:
            ready(second)
        intra_back_kernel(*intra_views[index])

    def inverse(residual):
        return lax.rsqrt(jnp.mean(residual * residual, axis=-1, keepdims=True) + EPS)

    def normalise():
        ready(tokens_load)
        residual = r.tokens[...].astype(f32)
        r.normed[...] = (residual * inverse(residual) * r.gain_one[...]).astype(bf16)

    turned = r.turned

    def inter_back():
        for parts in grid_views(
            (r.key, FDIM),
            (r.value, VDIM),
            (r.later, None),
            (r.gkey_in, FDIM),
            (grad, VDIM),
            (gkey, FDIM),
            (gvalue, VDIM),
        ):
            inter_back_kernel(*parts)
        turned[...] = gproj[...].T

    def in_grads(other):
        for slot in range(2):
            columns = pl.ds(pl.multiple_of(shards[2 * other + slot] * width, width), width)
            value = dot(r.normed[:, columns], turned[...], (0, 0))
            ref = r.in_send if other else r.in_base
            for k in range(8):
                ref[slot, k] = value[k * 32 : (k + 1) * 32, :].astype(bf16)
        if other:
            r.in_wait = wire.send(r.in_send, r.in_core, spot.core).wait_recv

    def in_base():
        r.in_wait()
        for slot in range(2):
            add_chunks(r.in_base.at[slot], 0, r.in_core.at[slot], 8)

    gains, small, small_in, small_line = r.gains, r.small, r.small_in, r.small_line

    def tokens_grad():
        ready(third)
        gnormed = dot(turned[...], r.in_full[...], (1, 1))
        residual = r.tokens[...].astype(f32)
        inv = inverse(residual)
        gains[0:1, :] = jnp.sum(gnormed * residual * inv, axis=0, keepdims=True)
        weighted = gnormed * r.gain_one[...]
        slope = jnp.mean(weighted * residual, axis=-1, keepdims=True)
        r.gmiddle[...] += inv * weighted - residual * (inv * inv * inv) * slope
        r.written = wire.keep(r.gmiddle, r.tokens_out)

    def gain_grads():
        gains[1:2, :] = r.ggain_two[0:1, :]
        small[...] = jnp.zeros_like(small)
        for index in range(4):
            for row in range(4):
                start = pl.multiple_of(shards[index] * width + (row % 2) * 128, 128)
                small[index, row : row + 1, :] = gains[row // 2 : row // 2 + 1, pl.ds(start, 128)]
        r.small_wait = wire.send(small.at[2:4], small_in.at[0:2], spot.core).wait_recv

    def gains_cross():
        r.small_wait()
        small[0:2] = small[0:2] + small_in[0:2]
        r.small_wait = wire.send(small.at[1], small_in.at[2], spot.chip).wait_recv

    def gains_side():
        r.small_wait()
        small[0] = small[0] + small_in[2]
        r.small_wait = wire.send(small.at[0], small_in.at[3], spot.side).wait_recv

    def gains_line():
        r.small_wait()
        small_line[z] = small[0] + small_in[3]
        r.small_sent = [wire.send(small_line.at[z], small_line.at[z], spot.ahead[k]) for k in (1, 2, 3)]

    def gains_end():
        for copy in r.small_sent:
            copy.wait_recv()
        r.gains_out[...] = (small_line[0] + small_line[1]) + (small_line[2] + small_line[3])

    down_base()
    da.to_side()
    grad_atten()
    grad_states()
    intra(0)
    intra(1)
    intra(2)
    intra(3)
    da.to_line()
    base(0)
    ga.cross()
    base(1)
    normalise()
    base(2)
    da.to_far()
    base(3)
    ub.cross()
    gb.cross()
    out_grads(1)
    out_grads(0)
    da.from_far()
    out_base()
    sums.first(0)
    sums.first(1)
    da.along_line()
    ga.to_side()
    ua.cross()
    sums.hop(0, 0)
    ga.to_line()
    sums.hop(0, 1)
    da.along_side()
    ub.to_side()
    out_flow.cross()
    sums.hop(1, 0)
    da.end()
    ga.to_far()
    gb.to_side()
    db.cross()
    ub.to_line()
    sums.hop(1, 1)
    gb.to_line()
    sums.hop(2, 0)
    ga.from_far()
    ua.to_side()
    ub.to_far()
    sums.hop(2, 1)
    inter_back()
    out_flow.to_side()
    in_grads(1)
    ga.along_line()
    in_grads(0)
    tokens_grad()
    ub.from_far()
    in_base()
    in_flow.cross()
    gain_grads()
    ga.along_side()
    out_flow.to_line()
    gb.to_far()
    gains_cross()
    ua.to_line()
    ub.along_line()
    out_flow.to_far()
    db.to_side()
    gb.from_far()
    ga.end()
    ua.to_far()
    ub.along_side()
    out_flow.from_far()
    db.to_line()
    gb.along_line()
    ua.from_far()
    out_flow.along_line()
    in_flow.to_side()
    gains_side()
    ub.end()
    db.to_far()
    gb.along_side()
    ua.along_line()
    in_flow.to_line()
    gains_line()
    out_flow.along_side()
    db.from_far()
    ua.along_side()
    gb.end()
    in_flow.to_far()
    gains_end()
    db.along_line()
    out_flow.end()
    in_flow.from_far()
    db.along_side()
    ua.end()
    in_flow.along_line()
    in_flow.along_side()
    db.end()
    in_flow.end()
    r.written.wait()
    wire.end()


HBM = pl.BlockSpec(memory_space=pltpu.HBM)
VMEM = pl.BlockSpec(memory_space=pltpu.VMEM)
SMEM = pl.BlockSpec(memory_space=pltpu.SMEM)


def sems(count):
    return pltpu.SemaphoreType.DMA((count,))


def gather_call(gains, in_shard):
    return pl.pallas_call(
        gather_kernel,
        out_shape=[jax.ShapeDtypeStruct((4, *a.shape), a.dtype) for a in (gains, in_shard)],
        in_specs=[HBM, HBM],
        out_specs=[HBM, HBM],
        scratch_shapes=[
            pltpu.VMEM(in_shard.shape, bf16),
            pltpu.VMEM(gains.shape, bf16),
            sems(12),
            sems(12),
            sems(4),
        ],
        compiler_params=pltpu.CompilerParams(collective_id=0, has_side_effects=True, vmem_limit_bytes=16 << 20),
    )(gains, in_shard)


def forward_call(places, states, query, key, value, tokens, weights):
    state = states.shape
    rows, model = tokens.shape
    wide = HEADS * VDIM
    return pl.pallas_call(
        forward_kernel,
        out_shape=[
            jax.ShapeDtypeStruct(state, bf16),
            jax.ShapeDtypeStruct((wide, rows), bf16),
            jax.ShapeDtypeStruct((HEADS, rows), f32),
            jax.ShapeDtypeStruct((rows, model), f32),
        ]
        + [jax.ShapeDtypeStruct((4, *w.shape), bf16) for w in weights],
        in_specs=[SMEM] + [VMEM] * 5 + [HBM] * 4,
        out_specs=[VMEM] * 4 + [HBM] * 4,
        scratch_shapes=[
            pltpu.VMEM((3, *state), bf16),
            pltpu.VMEM(state, bf16),
            pltpu.VMEM(state, bf16),
            pltpu.VMEM((wide, rows), f32),
            pltpu.VMEM((HEADS, rows), f32),
            pltpu.VMEM((wide, model), bf16),
            *(pltpu.VMEM(w.shape, bf16) for w in weights[:3]),
            *[pltpu.VMEM((weights[3].shape[0], weights[3].shape[1] // 2), bf16)] * 2,
            sems(40),
            sems(40),
            sems(16),
        ],
        compiler_params=pltpu.CompilerParams(collective_id=1, has_side_effects=True, vmem_limit_bytes=56 << 20),
    )(places, states, query, key, value, tokens, *weights)


def settle_kernel(down_ref, gate_ref, up_ref, out_ref, in_ref, output_ref, tokens_ref, *outs):
    tall, broad = down_ref.shape[2:]
    down_out, gate_out, up_out, out_out = outs[:4]
    for half in range(2):
        down_out[half * tall : (half + 1) * tall, :] = down_ref[half, 0].astype(f32)
        gate_out[:, half * broad : (half + 1) * broad] = gate_ref[half, 0].astype(f32)
        up_out[:, half * broad : (half + 1) * broad] = up_ref[half, 0].astype(f32)
    out_out[...] = out_ref[0].astype(f32)
    start = 0
    for out in outs[4:7]:
        stop = start + out.shape[1]
        out[...] = in_ref[0, :, start:stop].astype(f32)
        start = stop
    outs[7][...] = output_ref[...]
    outs[8][...] = tokens_ref[...]


def settle_call(down, gate, up, out, ins, output, tokens):
    tall, broad = down.shape[2:]
    size, model = out.shape[1:]
    narrow = HEADS * FDIM
    rows = output.shape[0]
    blocks = pl.BlockSpec((2, 1, tall, broad), lambda k: (0, k, 0, 0))

    def line(height, width):
        return pl.BlockSpec((height, width), lambda k: (k, 0))

    def eighths(a):
        return pl.BlockSpec((1, *a.shape[1:]), lambda k: (k, 0, 0))

    shapes = [(2 * tall, 8 * broad), (8 * tall, 2 * broad), (8 * tall, 2 * broad), (8 * size, model)]
    widths = (narrow, narrow, ins.shape[2] - 2 * narrow)
    shapes += [(8 * size, width) for width in widths]
    whole = [line(rows // 8, model)] * 2
    return pl.pallas_call(
        settle_kernel,
        out_shape=[jax.ShapeDtypeStruct(shape, f32) for shape in shapes]
        + [jax.ShapeDtypeStruct(a.shape, a.dtype) for a in (output, tokens)],
        grid=(8,),
        in_specs=[blocks, blocks, blocks, eighths(out), eighths(ins), *whole],
        out_specs=[
            pl.BlockSpec((2 * tall, broad), lambda k: (0, k)),
            line(tall, 2 * broad),
            line(tall, 2 * broad),
            line(size, model),
            *(line(size, width) for width in widths),
            *whole,
        ],
        compiler_params=pltpu.CompilerParams(vmem_limit_bytes=60 << 20),
    )(down, gate, up, out, ins, output, tokens)


def masked_sums(pieces, masks, dtype):
    total = None
    for index, piece in enumerate(pieces):
        for block in range(piece.shape[0]):
            term = masks[:, index, block][:, None, None, None] * piece[block].astype(f32)[None]
            total = term if total is None else total + term
    return total.astype(dtype)


class Exchange:
    def __init__(self, states, positions, own, count, later):
        self.pieces, self.sources, self.own, self.count, self.later = [states], [own], own, count, later
        self.table = positions.reshape(count, states.shape[0])

    def mask(self, target):
        there = self.table[target][:, None, None]
        here = self.table[jnp.stack(self.sources)][None]
        return ((here > there) if self.later else (here < there)).astype(f32)

    def ring(self):
        return self.pieces[-1], "ctx", [(i, (i + 2) % self.count) for i in range(self.count)]

    def passed(self, piece):
        self.sources.append((self.own - 2 * len(self.pieces)) % self.count)
        self.pieces.append(piece)

    def partner(self):
        return trade(masked_sums(self.pieces, self.mask(self.own ^ 1), bf16), 1, self.count)

    def total(self, received):
        return (masked_sums(self.pieces, self.mask(self.own), f32) + received.astype(f32)).astype(bf16)


def backward_call(arrays):
    names, specs, values = [], [], []
    get = SimpleNamespace(**arrays)
    for name, array in arrays.items():
        names.append(name)
        values.append(array)
        specs.append(SMEM if array.dtype == jnp.int32 else VMEM if array.shape[0] <= 8 and array.dtype == f32 else HBM)
    rows, model = get.tokens_hbm.shape
    columns = get.in_full_hbm.shape[1]
    block = get.down_keep.shape[2:]
    narrow, wide = HEADS * FDIM, HEADS * VDIM
    state = get.prefix_hbm.shape
    outs = dict(
        tokens_out=((rows, model), f32, HBM),
        down_out=((2, 8, *block), bf16, HBM),
        gate_out=((2, 8, *block), bf16, HBM),
        up_out=((2, 8, *block), bf16, HBM),
        out_out=((8, 32, model), bf16, HBM),
        in_out=((8, 32, columns), bf16, HBM),
        gains_out=((8, 128), f32, VMEM),
    )
    scratch = dict(
        down_core=((2, 8, *block), bf16),
        down_stage=((2, 8, *block), bf16),
        gate_core=((2, 2, 8, *block), bf16),
        up_core=((2, 2, 8, *block), bf16),
        stage=((2, 2, 8, *block), bf16),
        crossed=((6, 8, *block), bf16),
        sided=((6, 4, *block), bf16),
        lined=((6, 3, *block), bf16),
        out_full=((wide, model), bf16),
        branch=((rows, model), bf16),
        atten=((wide, rows), bf16),
        denom=((HEADS, rows), f32),
        query=((narrow, rows), bf16),
        key=((narrow, rows), bf16),
        value=((wide, rows), bf16),
        prefix=(state, bf16),
        tokens=((rows, model), bf16),
        in_full=((model, columns), bf16),
        gmiddle=((rows, model), f32),
        grad=((wide, rows), f32),
        gnumer=((wide, rows), bf16),
        gdenom=((HEADS, rows), f32),
        states=(state, bf16),
        ring=((3, *state), bf16),
        outgoing=(state, bf16),
        beside=(state, bf16),
        later=(state, bf16),
        gproj=((columns, rows), bf16),
        gkey_in=((narrow, rows), f32),
        normed=((rows, model), bf16),
        turned=((rows, columns), bf16),
        gains=((8, model), f32),
        small=((4, 8, 128), f32),
        small_in=((4, 8, 128), f32),
        small_line=((4, 8, 128), f32),
        out_base=((2, 8, 32, model), bf16),
        out_send=((2, 8, 32, model), bf16),
        out_core=((2, 8, 32, model), bf16),
        out_crossed=((8, 32, model), bf16),
        out_sided=((4, 32, model), bf16),
        out_lined=((3, 32, model), bf16),
        in_base=((2, 8, 32, columns), bf16),
        in_send=((2, 8, 32, columns), bf16),
        in_core=((2, 8, 32, columns), bf16),
        in_crossed=((8, 32, columns), bf16),
        in_sided=((4, 32, columns), bf16),
        in_lined=((3, 32, columns), bf16),
    )
    names += [*outs, *scratch, *dict(send_sems=0, recv_sems=0, local_sems=0)]
    return pl.pallas_call(
        functools.partial(backward_kernel, tuple(names)),
        out_shape=[jax.ShapeDtypeStruct(shape, dtype) for shape, dtype, _ in outs.values()],
        in_specs=specs,
        out_specs=[spec for _, _, spec in outs.values()],
        scratch_shapes=[pltpu.VMEM(shape, dtype) for shape, dtype in scratch.values()]
        + [sems(100), sems(100), sems(48)],
        compiler_params=pltpu.CompilerParams(collective_id=2, has_side_effects=True, vmem_limit_bytes=60 << 20),
    )(*values)


def body(count):
    def layer(
        tokens, block_pos, gain_attn, w_query, w_key, w_value, w_out, gain_ffn, w_gate, w_up, w_down, cotangent
    ):
        own = lax.axis_index("ctx")
        me = lax.axis_index("fsdp").astype(jnp.int32).reshape(1)
        positions = block_pos[0]
        in_shard = jnp.concatenate([w_query, w_key, w_value], axis=1)
        gains = jnp.stack([gain_attn, gain_ffn])
        if count == 8:
            gains, in_full = gather_call(gains, in_shard)
        else:
            gains, in_full = (lax.all_gather(a, "fsdp") for a in (gains, in_shard))
        gain_one, gain_two = (gains[:, k].reshape(-1).astype(f32) for k in (0, 1))
        in_full = in_full.reshape(-1, in_shard.shape[1])
        residual = tokens[0].astype(f32)
        rows = residual.shape[0]
        inv_one = lax.rsqrt(jnp.mean(residual * residual, axis=-1, keepdims=True) + EPS)
        normed_one = (residual * inv_one * gain_one).astype(bf16)
        narrow = HEADS * FDIM
        projected = dot(in_full, normed_one, (0, 1)).astype(bf16)
        query, key, value = projected[:narrow], projected[narrow : 2 * narrow], projected[2 * narrow :]

        unit = 2 * rows * BLOCK * HEADS
        (own_states,) = attention_call(
            states_kernel, ("narrow", "wide"), (("state", bf16),), rows, unit * FEAT
        )(key, value)
        weights = (w_out, w_gate.T, w_up.T, w_down)
        if count == 8:
            prefix, atten, denom, middle, out_full, gates, ups, downs = forward_call(
                block_pos, own_states, query, key, value, tokens[0], weights
            )
            out_full = out_full.reshape(-1, w_out.shape[1])
        else:
            numer, denom = attention_call(
                intra_kernel, ("narrow", "narrow", "wide"), (("wide", f32), ("head", f32)), rows, unit * 256
            )(query, key, value)
            links = Links()
            states = Exchange(own_states, positions, own, count, False)
            for _ in range(1, count // 2):
                states.passed(links.round([states.ring()])[0])
            prefix = states.total(links.round([states.partner()])[0])
            atten, denom = attention_call(
                inter_kernel,
                ("narrow", "state", "wide", "head"),
                (("wide", bf16), ("head", f32)),
                rows,
                unit * FEAT,
            )(query, prefix, numer, denom)
            out_full, gates, ups, downs = (lax.all_gather(w, "fsdp") for w in weights)
            out_full = out_full.reshape(-1, w_out.shape[1])
            middle = residual + dot(atten, out_full, (0, 0))
        ffn_inputs = (middle, gain_two.reshape(1, -1), cotangent[0], gates, ups, downs)
        width = in_full.shape[1]
        if count == 8:
            results = ffn_send_call(*ffn_inputs)
            output, grad_middle, branch, grad_gain_two = results[:4]
            gate_keep, up_keep, down_keep, second_cross, gate_got, up_got, down_got, first_cross = results[4:]
            arrays = dict(
                places=block_pos,
                gain_one=gain_one.reshape(1, -1),
                ggain_two=grad_gain_two,
                out_full_hbm=out_full,
                branch_hbm=branch,
                atten_hbm=atten,
                denom_hbm=denom,
                query_hbm=query,
                key_hbm=key,
                value_hbm=value,
                prefix_hbm=prefix,
                tokens_hbm=tokens[0],
                in_full_hbm=in_full,
                gmiddle_hbm=grad_middle,
                down_keep=down_keep,
                down_got=down_got,
                first_cross=first_cross,
                second_cross=second_cross,
                gate_keep=gate_keep,
                gate_got=gate_got,
                up_keep=up_keep,
                up_got=up_got,
            )
            grad_tokens, down_sum, gate_sum, up_sum, out_sum, in_sum, small = backward_call(arrays)
            gain_sums = small[:4].reshape(2, -1)
        else:
            results = ffn_call(me, *ffn_inputs)
            output, grad_middle, branch, grad_gain_two = results[:4]
            pairs = [results[k : k + 2] for k in (8, 4, 6)]
            grad_atten = dot(out_full, branch, (1, 1))
            gnumer, gdenom, grad_states = attention_call(
                grad_states_kernel,
                ("narrow", "wide", "head", "wide"),
                (("wide", bf16), ("head", f32), ("state", bf16)),
                rows,
                unit * FEAT,
            )(query, atten, denom, grad_atten)
            gquery, gkey, gvalue = attention_call(
                intra_back_kernel,
                ("narrow", "narrow", "wide", "wide", "head", "state"),
                (("narrow", bf16), ("narrow", f32), ("wide", f32)),
                rows,
                unit * 512,
            )(query, key, value, gnumer, gdenom, prefix)
            links = Links()
            backward = Exchange(grad_states, positions, own, count, True)
            for _ in range(1, count // 2):
                backward.passed(links.round([backward.ring()])[0])
            later = backward.total(links.round([backward.partner()])[0])
            gkey, gvalue = attention_call(
                inter_back_kernel,
                ("narrow", "wide", "state", "narrow", "wide"),
                (("narrow", bf16), ("wide", bf16)),
                rows,
                unit * 256,
            )(key, value, later, gkey, gvalue)
            gprojected = jnp.concatenate([gquery, gkey, gvalue], axis=0)
            gnormed_one = dot(gprojected, in_full, (0, 1))
            weighted_one = gnormed_one * gain_one
            grad_gain_one = jnp.sum(gnormed_one * residual * inv_one, axis=0)
            grad_tokens = (
                grad_middle
                + inv_one * weighted_one
                - residual
                * (inv_one * inv_one * inv_one)
                * jnp.mean(weighted_one * residual, axis=-1, keepdims=True)
            )

            def summed(keep, send):
                got = lax.ppermute(send, "fsdp", CORE)
                cross = (keep[:, 1].astype(f32) + got[:, 1].astype(f32)).astype(bf16)
                got_cross = lax.ppermute(cross, "fsdp", CHIP)
                total = keep[:, 0].astype(f32) + got[:, 0].astype(f32) + got_cross.astype(f32)
                return lax.psum(total.astype(bf16), "ctx")

            def scattered(grad):
                return lax.psum(lax.psum_scatter(grad, "fsdp", scatter_dimension=0, tiled=True), "ctx")

            down_sum, gate_sum, up_sum = (summed(*pair) for pair in pairs)
            out_sum = scattered(dot(atten, branch, (1, 0)).astype(bf16)).reshape(8, -1, branch.shape[1])
            in_sum = scattered(dot(normed_one, gprojected, (0, 1)).astype(bf16)).reshape(8, -1, width)
            gain_sums = scattered(jnp.stack([grad_gain_one, grad_gain_two[0]], axis=1)).T
        down_grad, gate_grad, up_grad, out_grad, *in_grads, output, grad_tokens = settle_call(
            down_sum, gate_sum, up_sum, out_sum, in_sum, output, grad_tokens
        )
        return (
            output[None],
            grad_tokens[None],
            gain_sums[0],
            *in_grads,
            out_grad,
            gain_sums[1],
            gate_grad.T,
            up_grad.T,
            down_grad,
        )

    return layer


def solution(mesh):
    rows = P("fsdp", None)
    seqs = P("fsdp", "ctx", None)
    vec = P("fsdp")
    in_specs = (seqs, rows, vec, rows, rows, rows, rows, vec, rows, rows, rows, seqs)
    out_specs = (seqs, seqs, vec, rows, rows, rows, rows, vec, rows, rows, rows)
    return jax.shard_map(
        body(mesh.shape["ctx"]), mesh=mesh, in_specs=in_specs, out_specs=out_specs, check_vma=False
    )
```

```python
import functools
from types import SimpleNamespace

import jax
import jax.numpy as jnp
from jax import lax
from jax.experimental import pallas as pl
from jax.experimental.pallas import tpu as pltpu
from jax.sharding import PartitionSpec as P

HEADS = 16
FDIM = 16
VDIM = 64
BLOCK = 256
GROUP = 8
FEAT = 160
STATE = GROUP // 2 * FEAT + 2 * GROUP
EPS = 1e-05
ROOT_HALF = 0.7071067811865476

f32 = jnp.float32
bf16 = jnp.bfloat16


def dims(lhs, rhs):
    return (((lhs,), (rhs,)), ((), ()))


def dot(lhs, rhs, contract):
    return lax.dot_general(lhs, rhs, dims(*contract), preferred_element_type=f32)


def turned(u, shift):
    return pltpu.roll(u, FDIM - shift, 0)


def features(u, pair_weight):
    rows = [u, u * u * ROOT_HALF]
    for shift in range(1, 8):
        rows.append(u * turned(u, shift) * ROOT_HALF)
    rows.append(u[:8] * u[8:] * ROOT_HALF)
    one = (lax.broadcasted_iota(jnp.int32, (8, u.shape[1]), 0) == 0).astype(f32)
    linear = jnp.concatenate(rows[:2], axis=0).astype(bf16)
    pairs = jnp.concatenate(rows[2:], axis=0).astype(bf16) * pair_weight
    del rows
    return jnp.concatenate([linear.astype(f32), pairs.astype(f32), one], axis=0).astype(bf16)


def features_back(u, g):
    total = g[:16] + (2.0 * ROOT_HALF) * (g[16:32] * u)
    for shift in range(1, 8):
        here = (2.0 * ROOT_HALF) * g[16 + 16 * shift : 32 + 16 * shift]
        total = total + here * turned(u, shift) + pltpu.roll(here * u, shift, 0)
    here = (2.0 * ROOT_HALF) * g[144:152]
    return total + jnp.concatenate([here * u[8:], here * u[:8]], axis=0)


def halved(ref, head):
    return ref[head * FDIM : (head + 1) * FDIM, :].astype(f32) * 0.5


def write_states(out_ref, feat, value_pair, weight_row, head):
    pair = head // 2
    product = dot(feat, value_pair, (1, 1))
    half = slice(0, 64) if head % 2 == 0 else slice(64, 128)
    out_ref[0, 0, pair * FEAT : (pair + 1) * FEAT, half] = product[:, half].astype(bf16)
    norm = dot(weight_row, feat, (1, 1))
    base = GROUP // 2 * FEAT + 2 * head
    out_ref[0, 0, base : base + 1, :] = norm[:1, :128].astype(bf16)
    out_ref[0, 0, base + 1 : base + 2, :] = jnp.concatenate([norm[:1, 128:], jnp.zeros((1, 96), f32)], axis=1).astype(bf16)


def norm_row(state_ref, head):
    base = GROUP // 2 * FEAT + 2 * head
    return state_ref[0, 0, base : base + 1, :], state_ref[0, 0, base + 1 : base + 2, :32]


def head_state(state_ref, head):
    pair = head // 2
    return state_ref[0, 0, pair * FEAT : (pair + 1) * FEAT, 64 * (head % 2) : 64 * (head % 2) + 64]


def states_kernel(key_ref, value_ref, out_ref):
    ones = jnp.ones((8, BLOCK), bf16)
    for head in range(GROUP):
        feat = features(halved(key_ref, head), 1.0)
        pair = head // 2
        write_states(out_ref, feat, value_ref[pair * 128 : (pair + 1) * 128, :], ones, head)


def intra_kernel(query_ref, key_ref, value_ref, numer_ref, denom_ref):
    for head in range(GROUP):
        rows = slice(head * FDIM, (head + 1) * FDIM)
        wide = slice(head * VDIM, (head + 1) * VDIM)
        scores = dot(key_ref[rows, :], query_ref[rows, :], (0, 0)) * 0.25
        kernel = 1.0 + scores + 0.5 * scores * scores
        denom_ref[head : head + 1, :] = jnp.sum(kernel, axis=0, keepdims=True)
        numer_ref[wide, :] = dot(value_ref[wide, :], kernel.astype(bf16), (1, 0))


def inter_kernel(query_ref, prefix_ref, numer_ref, denom_in_ref, atten_ref, denom_ref):
    for head in range(GROUP):
        wide = slice(head * VDIM, (head + 1) * VDIM)
        feat = features(halved(query_ref, head), 2.0)
        numer = numer_ref[wide, :] + dot(head_state(prefix_ref, head), feat, (0, 0))
        first, second = norm_row(prefix_ref, head)
        denom = denom_in_ref[head : head + 1, :] + dot(first, feat[:128], (1, 0)) + dot(second, feat[128:], (1, 0))
        denom_ref[head : head + 1, :] = denom
        atten_ref[wide, :] = (numer / denom).astype(bf16)


def grad_states_kernel(query_ref, atten_ref, denom_ref, grad_ref, gnumer_ref, gdenom_ref, out_ref):
    for pair in range(GROUP // 2):
        for head in (2 * pair, 2 * pair + 1):
            wide = slice(head * VDIM, (head + 1) * VDIM)
            denom = denom_ref[head : head + 1, :]
            grad = grad_ref[wide, :]
            gnumer_ref[wide, :] = (grad / denom).astype(bf16)
            gdenom = -jnp.sum(grad * atten_ref[wide, :].astype(f32), axis=0, keepdims=True) / denom
            gdenom_ref[head : head + 1, :] = gdenom.astype(bf16).astype(f32)
        for head in (2 * pair, 2 * pair + 1):
            feat = features(halved(query_ref, head), 1.0)
            weights = jnp.broadcast_to(gdenom_ref[head : head + 1, :], (8, BLOCK)).astype(bf16)
            write_states(out_ref, feat, gnumer_ref[pair * 128 : (pair + 1) * 128, :], weights, head)


def intra_back_kernel(
    query_ref, key_ref, value_ref, gnumer_ref, gdenom_ref, prefix_ref, gquery_ref, gkey_ref, gvalue_ref
):
    for head in range(GROUP):
        rows = slice(head * FDIM, (head + 1) * FDIM)
        wide = slice(head * VDIM, (head + 1) * VDIM)
        query, key = query_ref[rows, :], key_ref[rows, :]
        gnumer = gnumer_ref[wide, :]
        gdenom = gdenom_ref[head : head + 1, :]
        scores = dot(key, query, (0, 0)) * 0.25
        kernel = (1.0 + scores + 0.5 * scores * scores).astype(bf16)
        gkernel = dot(value_ref[wide, :], gnumer, (0, 0)) + gdenom
        gscores = ((1.0 + scores) * gkernel).astype(bf16)
        gvalue_ref[wide, :] = dot(gnumer, kernel, (1, 1))
        gkey_ref[rows, :] = dot(query, gscores, (1, 1)) * 0.25
        first, second = norm_row(prefix_ref, head)
        gdenom_low = gdenom.astype(bf16)
        outer_prod = jnp.concatenate([dot(first, gdenom_low, (0, 0)), dot(second, gdenom_low, (0, 0))], axis=0)
        gfeat = dot(head_state(prefix_ref, head), gnumer, (1, 0)) + outer_prod
        gquery = dot(key, gscores, (1, 0)) * 0.25 + 0.5 * features_back(halved(query_ref, head), gfeat)
        gquery_ref[rows, :] = gquery.astype(bf16)


def inter_back_kernel(key_ref, value_ref, later_ref, gkey_in_ref, gvalue_in_ref, gkey_ref, gvalue_ref):
    ones = jnp.ones((1, BLOCK), bf16)
    for head in range(GROUP):
        rows = slice(head * FDIM, (head + 1) * FDIM)
        wide = slice(head * VDIM, (head + 1) * VDIM)
        u = halved(key_ref, head)
        state = head_state(later_ref, head)
        first, second = norm_row(later_ref, head)
        outer_prod = jnp.concatenate([dot(first, ones, (0, 0)), dot(second, ones, (0, 0))], axis=0)
        gfeat = dot(state, value_ref[wide, :], (1, 0)) + outer_prod
        gkey_ref[rows, :] = (gkey_in_ref[rows, :] + 0.5 * features_back(u, gfeat)).astype(bf16)
        feat = features(u, 2.0)
        gvalue_ref[wide, :] = (gvalue_in_ref[wide, :] + dot(state, feat, (0, 0))).astype(bf16)


def attention_call(kernel, ins, outs, tokens, flops):
    blocks = tokens // BLOCK
    groups = HEADS // GROUP
    forms = {
        "narrow": ((GROUP * FDIM, BLOCK), lambda b, g: (g, b), (HEADS * FDIM, tokens)),
        "wide": ((GROUP * VDIM, BLOCK), lambda b, g: (g, b), (HEADS * VDIM, tokens)),
        "head": ((GROUP, BLOCK), lambda b, g: (g, b), (HEADS, tokens)),
        "state": ((1, 1, STATE, 128), lambda b, g: (b, g, 0, 0), (blocks, groups, STATE, 128)),
    }

    def spec(name):
        return pl.BlockSpec(forms[name][0], forms[name][1])

    def call(*arrays):
        moved = sum(a.size * a.dtype.itemsize for a in arrays)
        return pl.pallas_call(
            kernel,
            out_shape=[jax.ShapeDtypeStruct(forms[name][2], dtype) for name, dtype in outs],
            grid=(blocks, groups),
            in_specs=[spec(name) for name in ins],
            out_specs=[spec(name) for name, _ in outs],
            compiler_params=pltpu.CompilerParams(vmem_limit_bytes=40 << 20),
            cost_estimate=pl.CostEstimate(flops=flops, bytes_accessed=2 * moved, transcendentals=0),
        )(*arrays)

    return call


ORDER = (0, 2, 1, 3)


def place(step):
    return (step % 2) * 2 + step // 2


def ffn_begin(me, middle_ref, gain_ref, cot_ref, normed, x_own, x_turned, cot_turned, total, gnormed, inverse):
    width = x_own.shape[2]
    core = me + 1 - 2 * (me % 2)
    normed[...] = (middle_ref[...] * inverse() * gain_ref[...]).astype(bf16)
    for r, shard in enumerate((me, core, (me + 2) % 4, (core + 2) % 4)):
        x_own[r] = normed[:, pl.ds(pl.multiple_of(shard * width, width), width)]
    x_turned[...] = normed[...].T
    cot_turned[...] = cot_ref[...].T
    total[...] = jnp.zeros_like(total)
    gnormed[...] = jnp.zeros_like(gnormed)


def ffn_tile(gates, ups, down, x_turned, cot_turned):
    width = gates.shape[2]
    x_part = x_turned[:width, :]
    gate = dot(gates[0], x_part, (1, 0))
    up = dot(ups[0], x_part, (1, 0))
    for r in range(1, 4):
        x_part = x_turned[r * width : (r + 1) * width, :]
        gate = gate + dot(gates[r], x_part, (1, 0))
        up = up + dot(ups[r], x_part, (1, 0))
    ghidden = dot(down, cot_turned[...], (1, 0))
    sigmoid = jax.nn.sigmoid(gate)
    silu = gate * sigmoid
    hidden = (silu * up).astype(bf16)
    ggate = (ghidden * up * (sigmoid * (1.0 + gate * (1.0 - sigmoid)))).astype(bf16)
    return hidden, ggate, (ghidden * silu).astype(bf16)


def ffn_end(middle_ref, gain_ref, cot_ref, total, gnormed, inverse, output_ref, gmiddle_ref, branch_ref, ggain_ref):
    middle, inv, cot = middle_ref[...], inverse(), cot_ref[...].astype(f32)
    grad = gnormed[...]
    output_ref[...] = (middle + total[...]).astype(bf16)
    ggain_ref[...] = jnp.broadcast_to(jnp.sum(grad * middle * inv, axis=0, keepdims=True), ggain_ref.shape)
    weighted = grad * gain_ref[...]
    slope = jnp.mean(weighted * middle, axis=-1, keepdims=True)
    gmiddle = cot + inv * weighted - middle * (inv * inv * inv) * slope
    gmiddle_ref[...] = gmiddle
    branch_ref[...] = gmiddle.astype(bf16)


def ffn_kernel(me_ref, middle_ref, gain_ref, cot_ref, gates, ups, downs, *refs):
    output_ref, gmiddle_ref, branch_ref, ggain_ref = refs[:4]
    gate_keep, gate_send, up_keep, up_send, down_keep, down_send = refs[4:10]
    normed, x_own, x_turned, cot_turned, total, gnormed = refs[10:]
    step = pl.program_id(0)
    width = gates.shape[2]

    def inverse():
        middle = middle_ref[...]
        return lax.rsqrt(jnp.mean(middle * middle, axis=-1, keepdims=True) + EPS)

    @pl.when(step == 0)
    def _():
        ffn_begin(
            me_ref[0], middle_ref, gain_ref, cot_ref, normed, x_own, x_turned, cot_turned, total, gnormed, inverse
        )

    hidden, ggate, gup = ffn_tile(gates, ups, downs[0], x_turned, cot_turned)
    down = downs[0]
    total[...] += dot(hidden, down, (0, 0))
    gdown = dot(hidden, cot_ref[...], (1, 0))
    tall, broad = down_keep.shape[3:]

    def store(ref, slot, grad):
        for half in range(2):
            for eighth in range(8):
                ref[half, slot, eighth] = grad[
                    half * tall : (half + 1) * tall, eighth * broad : (eighth + 1) * broad
                ].astype(bf16)

    @pl.when(step < 2)
    def _():
        store(down_keep, 0, gdown)

    @pl.when(step >= 2)
    def _():
        store(down_send, 0, gdown)

    def store_turned(keep, send, r, grad):
        ref = send if r % 2 else keep
        for half in range(2):
            for eighth in range(2):
                ref[half, r // 2, eighth] = grad[
                    eighth * tall : (eighth + 1) * tall, half * broad : (half + 1) * broad
                ].astype(bf16)

    for r in range(4):
        part = slice(r * width, (r + 1) * width)
        gnormed[:, part] += dot(ggate, gates[r], (0, 0)) + dot(gup, ups[r], (0, 0))
        store_turned(gate_keep, gate_send, r, dot(ggate, x_own[r], (1, 0)))
        store_turned(up_keep, up_send, r, dot(gup, x_own[r], (1, 0)))

    @pl.when(step == 3)
    def _():
        ffn_end(middle_ref, gain_ref, cot_ref, total, gnormed, inverse, output_ref, gmiddle_ref, branch_ref, ggain_ref)


def ffn_call(me, middle, gain, cot, gates, ups, downs):
    rows, model = middle.shape
    _, hidden, width = gates.shape
    tile = downs.shape[1]
    once = pl.Buffered(1)

    def whole(shape, **kw):
        return pl.BlockSpec(shape, lambda s, me: (0,) * len(shape), **kw)

    columns = pl.BlockSpec((4, tile, width), lambda s, me: (0, me[0] ^ place(s), 0))
    block = (tile // 2, model // 8)
    pair = pl.BlockSpec((2, 2, 2, *block), lambda s, me: (0, 0, me[0] ^ place(s), 0, 0))
    grads = jax.ShapeDtypeStruct((2, 2, 8, *block), bf16)
    return pl.pallas_call(
        ffn_kernel,
        out_shape=[
            jax.ShapeDtypeStruct((rows, model), bf16),
            jax.ShapeDtypeStruct((rows, model), f32),
            jax.ShapeDtypeStruct((rows, model), bf16),
            jax.ShapeDtypeStruct((8, model), f32),
            grads,
            grads,
            grads,
            grads,
            grads,
            grads,
        ],
        grid_spec=pltpu.PrefetchScalarGridSpec(
            num_scalar_prefetch=1,
            grid=(4,),
            in_specs=[
                whole((rows, model), pipeline_mode=once),
                whole((1, model)),
                whole((rows, model), pipeline_mode=once),
                columns,
                columns,
                pl.BlockSpec((1, tile, model), lambda s, me: (me[0] ^ place(s), 0, 0)),
            ],
            out_specs=[
                whole((rows, model), pipeline_mode=once),
                whole((rows, model), pipeline_mode=once),
                whole((rows, model), pipeline_mode=once),
                whole((8, model)),
                pair,
                pair,
                pair,
                pair,
                pl.BlockSpec((2, 1, 8, *block), lambda s, me: (0, jnp.minimum(s, 1), 0, 0, 0)),
                pl.BlockSpec((2, 1, 8, *block), lambda s, me: (0, jnp.maximum(s - 2, 0), 0, 0, 0)),
            ],
            scratch_shapes=[
                pltpu.VMEM((rows, model), bf16),
                pltpu.VMEM((4, rows, width), bf16),
                pltpu.VMEM((model, rows), bf16),
                pltpu.VMEM((model, rows), bf16),
                pltpu.VMEM((rows, model), f32),
                pltpu.VMEM((rows, model), f32),
            ],
        ),
        compiler_params=pltpu.CompilerParams(vmem_limit_bytes=58 << 20),
        cost_estimate=pl.CostEstimate(
            flops=18 * rows * model * hidden, bytes_accessed=14 * hidden * model, transcendentals=0
        ),
    )(me, middle, gain, cot, gates, ups, downs)


CORE = [(0, 1), (1, 0), (2, 3), (3, 2)]
CHIP = [(0, 2), (2, 0), (1, 3), (3, 1)]


class Links:
    def __init__(self):
        self.last = ()

    def round(self, sends, beside=()):
        arrays = [send[0] for send in sends]
        if self.last:
            arrays = lax.optimization_barrier((*arrays, *self.last))[: len(arrays)]
        results = [lax.ppermute(a, axis, perm) for a, (_, axis, perm) in zip(arrays, sends)]
        self.last = (*results, *beside)
        return results


def trade(array, bits, count):
    return array, "ctx", [(i, i ^ bits) for i in range(count)]


MESH = pl.DeviceIdType.MESH


class Spot:
    def __init__(self):
        self.me = lax.axis_index("fsdp")
        self.own = lax.axis_index("ctx")
        self.core = {"fsdp": self.me + 1 - 2 * (self.me % 2)}
        self.across = (self.me + 2) % 4
        self.chip = {"fsdp": self.across}
        self.y = self.own % 2
        self.z = self.own // 2
        self.side = {"ctx": self.own + 1 - 2 * self.y}
        self.next = {"ctx": self.own + 2 - 4 * (self.z % 2)}
        self.ahead = [None] + [{"ctx": (self.own + 2 * k) % 8} for k in (1, 2, 3)]

    def greet(self, neighbours):
        barrier = pltpu.get_barrier_semaphore()
        for neighbour in neighbours:
            pl.semaphore_signal(barrier, inc=1, device_id=neighbour, device_id_type=MESH)
        pl.semaphore_wait(barrier, len(neighbours))


class Wire:
    def __init__(self, send_sems, recv_sems, local_sems):
        self.send_sems, self.recv_sems, self.local_sems = send_sems, recv_sems, local_sems
        self.sent, self.local, self.count = [], [], 0

    def send(self, source, target, device):
        k = self.count
        self.count += 1
        copy = pltpu.make_async_remote_copy(
            src_ref=source,
            dst_ref=target,
            send_sem=self.send_sems.at[k],
            recv_sem=self.recv_sems.at[k],
            device_id=device,
            device_id_type=MESH,
        )
        copy.start()
        self.sent.append(copy)
        return copy

    def keep(self, source, target):
        copy = pltpu.make_async_copy(source, target, self.local_sems.at[len(self.local)])
        copy.start()
        self.local.append(copy)
        return copy

    def left(self, copy):
        copy.wait_send()
        self.sent = [other for other in self.sent if other is not copy]

    def end(self):
        for copy in self.sent:
            copy.wait_send()


def tile_at(step):
    me = lax.axis_index("fsdp")
    place = 3 - step
    return 2 * ((me // 2 + place // 2) % 2) + (me % 2 + place) % 2


def ffn_send_kernel(middle_ref, gain_ref, cot_ref, gates, ups, downs, *refs):
    output_ref, gmiddle_ref, branch_ref, ggain_ref = refs[:4]
    gate_keep, up_keep, down_keep, down_cross, gate_got, up_got, down_got, crossed = refs[4:12]
    normed, x_own, x_turned, cot_turned, total, gnormed = refs[12:18]
    sending, down_first, down_second, down_in, crossing, send_sems, recv_sems = refs[18:]
    step = pl.program_id(0)
    spot = Spot()
    tall, broad = down_keep.shape[2:]
    width = gates.shape[2]

    def copy(k, source, target, device):
        return pltpu.make_async_remote_copy(
            src_ref=source,
            dst_ref=target,
            send_sem=send_sems.at[k],
            recv_sem=recv_sems.at[k],
            device_id=device,
            device_id_type=MESH,
        )

    def tile_copy(at, which):
        got = (gate_got, up_got)[which].at[:, :, pl.ds(2 * tile_at(at), 2)]
        return copy(2 * at + which, sending.at[at % 2, which], got, spot.core)

    first = copy(8, down_first, down_in, spot.core)
    second = copy(9, down_second, down_got, spot.core)
    cross = copy(10, crossing, crossed, spot.chip)

    def inverse():
        middle = middle_ref[...]
        return lax.rsqrt(jnp.mean(middle * middle, axis=-1, keepdims=True) + EPS)

    @pl.when(step == 0)
    def _():
        spot.greet([spot.core, spot.chip])
        ffn_begin(
            spot.me, middle_ref, gain_ref, cot_ref, normed, x_own, x_turned, cot_turned, total, gnormed, inverse
        )

    hidden, ggate, gup = ffn_tile(gates, ups, downs[0], x_turned, cot_turned)
    gdown = dot(hidden, cot_ref[...], (1, 0))

    def down_block(half, eighth):
        return gdown[half * tall : (half + 1) * tall, eighth * broad : (eighth + 1) * broad]

    def store(ref):
        for half in range(2):
            for eighth in range(8):
                ref[half, eighth] = down_block(half, eighth).astype(bf16)

    @pl.when(step == 0)
    def _():
        store(down_first)
        first.start()

    @pl.when(step == 1)
    def _():
        first.wait_recv()
        for half, ref in enumerate((crossing, down_cross)):
            for eighth in range(8):
                ref[eighth] = (down_block(half, eighth) + down_in[half, eighth].astype(f32)).astype(bf16)
        cross.start()

    @pl.when(step == 2)
    def _():
        store(down_second)
        second.start()

    @pl.when(step == 3)
    def _():
        store(down_keep)

    for at in range(4):

        @pl.when(step == at)
        def _(at=at):
            if at >= 2:
                tile_copy(at - 2, 0).wait_send()
                tile_copy(at - 2, 1).wait_send()
            for which, grad in enumerate((ggate, gup)):
                for slot in range(2):
                    value = dot(grad, x_own[2 * slot + 1], (1, 0))
                    for half in range(2):
                        for eighth in range(2):
                            sending[at % 2, which, half, slot, eighth] = value[
                                eighth * tall : (eighth + 1) * tall, half * broad : (half + 1) * broad
                            ].astype(bf16)
                tile_copy(at, which).start()

    for grad, ref in ((ggate, gate_keep), (gup, up_keep)):
        for slot in range(2):
            value = dot(grad, x_own[2 * slot], (1, 0))
            for half in range(2):
                for eighth in range(2):
                    ref[half, slot, eighth] = value[
                        eighth * tall : (eighth + 1) * tall, half * broad : (half + 1) * broad
                    ].astype(bf16)
    for r in range(4):
        part = slice(r * width, (r + 1) * width)
        gnormed[:, part] += dot(ggate, gates[r], (0, 0)) + dot(gup, ups[r], (0, 0))
    total[...] += dot(hidden, downs[0], (0, 0))

    @pl.when(step == 3)
    def _():
        ffn_end(middle_ref, gain_ref, cot_ref, total, gnormed, inverse, output_ref, gmiddle_ref, branch_ref, ggain_ref)
        for at in range(4):
            for which in range(2):
                tile_copy(at, which).wait_recv()
                if at >= 2:
                    tile_copy(at, which).wait_send()
        first.wait_send()
        second.wait()
        cross.wait()


def ffn_send_call(middle, gain, cot, gates, ups, downs):
    rows, model = middle.shape
    width = gates.shape[2]
    tile = downs.shape[1]
    once = pl.Buffered(1)
    block = (tile // 2, model // 8)

    def whole(*shape, **kw):
        return pl.BlockSpec(shape, lambda s: (0,) * len(shape), **kw)

    columns = pl.BlockSpec((4, tile, width), lambda s: (0, tile_at(s), 0))
    pair = pl.BlockSpec((2, 2, 2, *block), lambda s: (0, 0, tile_at(s), 0, 0))
    grads = jax.ShapeDtypeStruct((2, 2, 8, *block), bf16)
    halves = jax.ShapeDtypeStruct((2, 8, *block), bf16)
    one = jax.ShapeDtypeStruct((8, *block), bf16)
    return pl.pallas_call(
        ffn_send_kernel,
        out_shape=[
            jax.ShapeDtypeStruct((rows, model), bf16),
            jax.ShapeDtypeStruct((rows, model), f32),
            jax.ShapeDtypeStruct((rows, model), bf16),
            jax.ShapeDtypeStruct((8, model), f32),
            grads,
            grads,
            halves,
            one,
            grads,
            grads,
            halves,
            one,
        ],
        grid=(4,),
        in_specs=[
            whole(rows, model, pipeline_mode=once),
            whole(1, model),
            whole(rows, model, pipeline_mode=once),
            columns,
            columns,
            pl.BlockSpec((1, tile, model), lambda s: (tile_at(s), 0, 0)),
        ],
        out_specs=[
            whole(rows, model, pipeline_mode=once),
            whole(rows, model, pipeline_mode=once),
            whole(rows, model, pipeline_mode=once),
            whole(8, model),
            pair,
            pair,
            whole(2, 8, *block, pipeline_mode=once),
            whole(8, *block, pipeline_mode=once),
            HBM,
            HBM,
            HBM,
            HBM,
        ],
        scratch_shapes=[
            pltpu.VMEM((rows, model), bf16),
            pltpu.VMEM((4, rows, width), bf16),
            pltpu.VMEM((model, rows), bf16),
            pltpu.VMEM((model, rows), bf16),
            pltpu.VMEM((rows, model), f32),
            pltpu.VMEM((rows, model), f32),
            pltpu.VMEM((2, 2, 2, 2, 2, *block), bf16),
            pltpu.VMEM((2, 8, *block), bf16),
            pltpu.VMEM((2, 8, *block), bf16),
            pltpu.VMEM((2, 8, *block), bf16),
            pltpu.VMEM((8, *block), bf16),
            sems(11),
            sems(11),
        ],
        compiler_params=pltpu.CompilerParams(collective_id=3, has_side_effects=True, vmem_limit_bytes=60 << 20),
    )(middle, gain, cot, gates, ups, downs)


class Gather:
    def __init__(self, wire, spot, shard, full, held, axis, split, chunks):
        self.wire, self.spot, self.full, self.axis, self.split = wire, spot, full, axis, split
        self.part = shard.shape[axis] // (2 if split else 1)
        self.size = self.part // chunks
        me = spot.me
        self.held, self.loaded = held, wire.keep(shard, full.at[me] if held is None else held)
        here = [self.view(shard, c, spot.y) for c in range(chunks)]
        there = [self.view(full.at[me], c, spot.y) for c in range(chunks)]
        self.cross = [wire.send(a, b, spot.chip) for a, b in zip(here, there)]
        self.near = wire.send(shard, full.at[me], spot.core)
        self.side, self.far = {}, []

    def write(self):
        self.loaded.wait()
        self.own = None if self.held is None else self.wire.keep(self.held, self.full.at[self.spot.me])

    def view(self, ref, chunk, y):
        start = chunk * self.size + (y * self.part if self.split else 0)
        index = [slice(None)] * 2
        index[self.axis] = pl.ds(pl.multiple_of(start, self.size), self.size)
        return ref.at[tuple(index)]

    def relay(self, chunk):
        self.cross[chunk].wait_recv()
        part = self.view(self.full.at[self.spot.across], chunk, self.spot.y)
        if self.split:
            self.side[chunk] = self.wire.send(part, part, self.spot.side)
        self.far.append(self.wire.send(part, part, self.spot.core))

    def relay_other(self, chunk):
        self.side[chunk].wait_recv()
        part = self.view(self.full.at[self.spot.across], chunk, 1 - self.spot.y)
        self.far.append(self.wire.send(part, part, self.spot.core))

    def end(self):
        if self.own is not None:
            self.own.wait()
        self.near.wait_recv()
        for copy in self.far:
            copy.wait_recv()


class StateSum:
    def __init__(self, wire, spot, places_ref, later, states, beside, outgoing, ring, result):
        self.wire, self.spot, self.states, self.beside = wire, spot, states, beside
        self.outgoing, self.ring, self.result = outgoing, ring, result
        self.sent = {}

        def place(device, block):
            return places_ref[0, 2 * device + block]

        partner = spot.own + 1 - 2 * spot.y
        sources = [place(device, block) for device in (spot.own, partner) for block in range(2)]
        self.masks = {}
        for k in range(4):
            for block in range(2):
                target = place((spot.own + 8 - 2 * k) % 8, block)
                self.masks[k, block] = [
                    jnp.where(source > target if later else source < target, 1.0, 0.0).astype(f32)
                    for source in sources
                ]

    def part(self, k, block, group):
        refs = (self.states.at[0], self.states.at[1], self.beside.at[0], self.beside.at[1])
        terms = [ref[group].astype(f32) * mask for ref, mask in zip(refs, self.masks[k, block])]
        return (terms[0] + terms[1]) + (terms[2] + terms[3])

    def trade(self):
        self.traded = self.wire.send(self.states, self.beside, self.spot.side)

    def first(self, block):
        if block == 0:
            self.traded.wait_recv()
        for group in range(self.states.shape[1]):
            self.outgoing[block, group] = self.part(1, block, group).astype(bf16)
        self.sent[0, block] = self.wire.send(self.outgoing.at[block], self.ring.at[0, block], self.spot.ahead[1])

    def hop(self, step, block):
        self.sent[step, block].wait_recv()
        target = self.result if step == 2 else self.ring.at[step]
        for group in range(self.states.shape[1]):
            value = self.ring[step, block, group].astype(f32) + self.part((step + 2) % 4, block, group)
            target[block, group] = value.astype(bf16)
        if step < 2:
            self.sent[step + 1, block] = self.wire.send(
                self.ring.at[step, block], self.ring.at[step + 1, block], self.spot.ahead[1]
            )


class StateRing:
    def __init__(self, wire, spot, places_ref, later, states, beside, outgoing, ring, result):
        self.wire, self.spot, self.states, self.beside = wire, spot, states, beside
        self.outgoing, self.ring, self.result = outgoing, ring, result
        self.sent, self.traded = {}, {}

        def place(device, block):
            return places_ref[0, 2 * device + block]

        sources = [place((spot.own + 8 - 2 * k) % 8, block) for k in range(4) for block in range(2)]
        self.masks = {}
        for beyond, device in enumerate((spot.own, spot.own + 1 - 2 * spot.y)):
            for block in range(2):
                target = place(device, block)
                self.masks[beyond, block] = [
                    jnp.where(source > target if later else source < target, 1.0, 0.0).astype(f32)
                    for source in sources
                ]

    def part(self, beyond, block, group):
        refs = [ref.at[b] for ref in (self.states, *(self.ring.at[k] for k in range(3))) for b in range(2)]
        total = None
        for ref, mask in zip(refs, self.masks[beyond, block]):
            term = ref[group].astype(f32) * mask
            total = term if total is None else total + term
        return total

    def start(self):
        for block in range(2):
            self.pass_on(0, block, self.states.at[block])

    def pass_on(self, step, block, source):
        self.sent[step, block] = self.wire.send(source, self.ring.at[step, block], self.spot.ahead[1])

    def forward(self, step, block):
        self.sent[step, block].wait_recv()
        if step < 2:
            self.pass_on(step + 1, block, self.ring.at[step, block])

    def partner(self, block):
        for group in range(self.states.shape[1]):
            self.outgoing[block, group] = self.part(1, block, group).astype(bf16)
        self.traded[block] = self.wire.send(self.outgoing.at[block], self.beside.at[block], self.spot.side)

    def finish(self, block):
        self.traded[block].wait_recv()
        for group in range(self.states.shape[1]):
            value = self.part(0, block, group) + self.beside[block, group].astype(f32)
            self.result[block, group] = value.astype(bf16)


def forward_kernel(places_ref, tokens_ref, gains_ref, in_ref, *refs):
    weights, (gains, query_ref, key_ref, value_ref, prefix_ref, atten_ref, denom_ref, middle_ref) = refs[:4], refs[4:12]
    in_out, out_out, *fulls = refs[12:17]
    in_full, out_full, normed, own_states, rings, outgoing, beside, numer, inner = refs[17:26]
    held, (send_sems, recv_sems, local_sems) = refs[26:30], refs[30:]
    spot = Spot()
    wire = Wire(send_sems, recv_sems, local_sems)
    spot.greet([spot.core, spot.chip, spot.side, spot.ahead[1], spot.ahead[3]])
    me = spot.me
    ins = Gather(wire, spot, in_ref, in_full, None, 0, True, 2)
    gain_own = wire.keep(gains_ref, gains.at[me])
    gain_near = wire.send(gains_ref, gains.at[me], spot.core)
    gain_cross = wire.send(gains_ref, gains.at[me], spot.chip)
    out_w, gate_w, up_w, down_w = weights
    half = down_w.shape[1] // 2
    left, right = slice(0, half), slice(half, 2 * half)
    out = Gather(wire, spot, out_w, out_full, None, 0, True, 1)
    gate = Gather(wire, spot, gate_w, fulls[0], held[0], 0, True, 2)
    up = Gather(wire, spot, up_w, fulls[1], held[1], 0, True, 2)
    down_left = Gather(wire, spot, down_w.at[:, left], fulls[2].at[:, :, left], held[2], 1, True, 1)
    down_right = Gather(wire, spot, down_w.at[:, right], fulls[2].at[:, :, right], held[3], 1, False, 2)
    everything = (ins, out, gate, up, down_left, down_right)
    groups = [slice(k, k + 1) for k in range(HEADS // GROUP)]
    views = [
        [ref.at[:, at] for ref in (own_states, beside, outgoing)] + [rings.at[:, :, at], prefix_ref.at[:, at]]
        for at in groups
    ]
    sums = StateSum(wire, spot, places_ref, False, *views[0])
    ring = StateRing(wire, spot, places_ref, False, *views[1])
    intra = list(grid_views((query_ref, FDIM), (key_ref, FDIM), (value_ref, VDIM), (numer, VDIM), (inner, 1)))

    def statistics():
        residual = tokens_ref[...].astype(f32)
        inverse = lax.rsqrt(jnp.mean(residual * residual, axis=-1, keepdims=True) + EPS)
        middle_ref[...] = residual * inverse
        gain_cross.wait_recv()
        across = gains.at[spot.across]
        everything[0].gain_far = wire.send(across, across, spot.core)
        for one in everything:
            one.write()

    def project():
        gain_own.wait()
        gain_near.wait_recv()
        ins.gain_far.wait_recv()
        ins.end()
        ins.saved = wire.keep(in_full, in_out)
        width = in_ref.shape[0]
        for k in range(4):
            part = slice(k * width, (k + 1) * width)
            normed[:, part] = (middle_ref[:, part] * gains[k, 0:1, :].astype(f32)).astype(bf16)
        for start, ref in ((0, query_ref), (HEADS * FDIM, key_ref), (2 * HEADS * FDIM, value_ref)):
            stop = start + ref.shape[0]
            total = None
            for k in range(4):
                term = dot(normed[:, k * width : (k + 1) * width], in_full[k, :, start:stop], (1, 0))
                total = term if total is None else total + term
            ref[...] = total.astype(bf16).T

    def states():
        for parts in grid_views((key_ref, FDIM), (value_ref, VDIM), (own_states, None)):
            states_kernel(*parts)
        sums.trade()
        ring.start()

    def inter():
        for parts in grid_views(
            (query_ref, FDIM), (prefix_ref, None), (numer, VDIM), (inner, 1), (atten_ref, VDIM), (denom_ref, 1)
        ):
            inter_kernel(*parts)

    def middle():
        out.end()
        out.saved = wire.keep(out_full, out_out)
        total = tokens_ref[...].astype(f32)
        width = out_w.shape[0]
        for k in range(4):
            total = total + dot(atten_ref[k * width : (k + 1) * width, :], out_full[k], (0, 0))
        middle_ref[...] = total

    ins.relay(0)
    ins.relay(1)
    statistics()
    ins.relay_other(1)
    ins.relay_other(0)
    out.relay(0)
    project()
    gate.relay(0)
    states()
    ring.forward(0, 0)
    intra_kernel(*intra[0])
    gate.relay_other(0)
    gate.relay(1)
    intra_kernel(*intra[1])
    ring.forward(0, 1)
    sums.first(0)
    up.relay(0)
    intra_kernel(*intra[2])
    intra_kernel(*intra[3])
    ring.forward(1, 0)
    sums.first(1)
    sums.hop(0, 0)
    up.relay(1)
    ring.forward(2, 0)
    out.relay_other(0)
    ring.forward(1, 1)
    sums.hop(0, 1)
    sums.hop(1, 0)
    ring.forward(2, 1)
    ring.partner(1)
    ring.partner(0)
    down_left.relay(0)
    sums.hop(1, 1)
    sums.hop(2, 0)
    down_right.relay(0)
    ring.finish(0)
    ring.finish(1)
    up.relay_other(1)
    sums.hop(2, 1)
    gate.relay_other(1)
    down_right.relay(1)
    inter()
    middle()
    up.relay_other(0)
    down_left.relay_other(0)
    for one in everything[2:]:
        one.end()
    ins.saved.wait()
    out.saved.wait()
    wire.end()


def grid_views(*refs):
    for block in range(2):
        for group in range(HEADS // GROUP):
            columns = slice(block * BLOCK, (block + 1) * BLOCK)
            parts = []
            for ref, rows in refs:
                if rows is None:
                    parts.append(ref.at[block : block + 1, group : group + 1])
                else:
                    parts.append(ref.at[group * GROUP * rows : (group + 1) * GROUP * rows, columns])
            yield parts


def add_chunks(total, first, other, count):
    def one(k, carry):
        total[first + k] = (total[first + k].astype(f32) + other[k].astype(f32)).astype(bf16)
        return carry

    lax.fori_loop(0, count, one, 0)


class Flow:
    def __init__(self, wire, spot, kept, sent, crossed, sided, lined, result):
        self.wire, self.spot = wire, spot
        self.kept, self.sent, self.crossed, self.sided, self.lined, self.result = kept, sent, crossed, sided, lined, result
        self.half = spot.y * 4
        self.pair = self.half + 2 * (spot.z % 2)
        self.mine = self.pair + spot.z // 2

    def cross(self):
        self.arrive = self.wire.send(self.sent, self.crossed, self.spot.chip).wait_recv

    def to_side(self):
        self.arrive()
        add_chunks(self.crossed, 0, self.kept, 8)
        there = pl.ds(4 - self.half, 4)
        self.s = self.wire.send(self.crossed.at[there], self.sided, self.spot.side)

    def to_line(self):
        self.s.wait_recv()
        add_chunks(self.crossed, self.half, self.sided, 4)
        there = pl.ds(2 * self.half + 2 - self.pair, 2)
        self.l = self.wire.send(self.crossed.at[there], self.lined.at[0:2], self.spot.next)

    def to_far(self):
        self.l.wait_recv()
        add_chunks(self.crossed, self.pair, self.lined, 2)
        self.f = self.wire.send(self.crossed.at[2 * self.pair + 1 - self.mine], self.lined.at[2], self.spot.ahead[2])

    def from_far(self):
        self.f.wait_recv()
        mine = self.mine
        self.crossed[mine] = (self.crossed[mine].astype(f32) + self.lined[2].astype(f32)).astype(bf16)
        self.own = self.wire.keep(self.crossed.at[mine], self.result.at[mine])
        self.g = self.wire.send(self.crossed.at[mine], self.result.at[mine], self.spot.ahead[2])

    def along_line(self):
        self.own.wait()
        self.g.wait_recv()
        here = self.result.at[pl.ds(self.pair, 2)]
        self.a = self.wire.send(here, here, self.spot.next)

    def along_side(self):
        self.a.wait_recv()
        here = self.result.at[pl.ds(self.half, 4)]
        self.b = self.wire.send(here, here, self.spot.side)

    def end(self):
        self.b.wait_recv()


def backward_kernel(names, *refs):
    r = SimpleNamespace(**dict(zip(names, refs)))
    spot = Spot()
    wire = Wire(r.send_sems, r.recv_sems, r.local_sems)
    me, z = spot.me, spot.z
    spot.greet([spot.core, spot.chip, spot.side, *spot.ahead[1:]])

    def load(*pairs):
        return [wire.keep(a, b) for a, b in pairs]

    def ready(copies):
        for copy in copies:
            copy.wait()

    first = load(
        (r.out_full_hbm, r.out_full),
        (r.branch_hbm, r.branch),
        (r.atten_hbm, r.atten),
        (r.denom_hbm, r.denom),
        (r.query_hbm, r.query),
    )
    arrived = load((r.first_cross, r.crossed.at[0]))
    down_loads = load((r.down_got, r.down_core), (r.down_keep, r.down_stage))
    kept, held = (r.gate_keep, r.up_keep), (r.gate_core, r.up_core)
    bases = (2, 0, 1, 3)
    stage = r.stage
    got = {weight: load((ref, held[weight])) for weight, ref in ((bases[0] // 2, (r.gate_got, r.up_got)[bases[0] // 2]),)}
    staged = {}

    def fetch(index):
        weight, half = bases[index] // 2, bases[index] % 2
        staged[index] = wire.keep(kept[weight].at[half], stage.at[index % 2])

    fetch(0)
    fetch(1)
    second = load((r.key_hbm, r.key), (r.value_hbm, r.value), (r.prefix_hbm, r.prefix))
    other = 1 - bases[0] // 2
    got[other] = load(((r.gate_got, r.up_got)[other], held[other]))
    tokens_load = load((r.tokens_hbm, r.tokens))
    third = load((r.in_full_hbm, r.in_full), (r.gmiddle_hbm, r.gmiddle))

    def base(index):
        weight, half = bases[index] // 2, bases[index] % 2
        ready(got[weight])
        got[weight] = []
        staged[index].wait()
        for slot in range(2):
            add_chunks(held[weight].at[half, slot], 0, stage.at[index % 2, slot], 8)
        if index < 2:
            fetch(index + 2)

    def down_base():
        ready(down_loads)
        for half in range(2):
            add_chunks(r.down_core.at[half], 0, r.down_stage.at[half], 8)

    def flow(index, kept_ref, sent_ref, result):
        return Flow(wire, spot, kept_ref, sent_ref, r.crossed.at[index], r.sided.at[index], r.lined.at[index], result)

    da, db = (flow(half, r.down_core.at[half], r.second_cross, r.down_out.at[half]) for half in range(2))
    da.arrive = arrived[0].wait
    ga, gb = (flow(2 + half, r.gate_core.at[half, 0], r.gate_core.at[half, 1], r.gate_out.at[half]) for half in range(2))
    ua, ub = (flow(4 + half, r.up_core.at[half, 0], r.up_core.at[half, 1], r.up_out.at[half]) for half in range(2))
    out_flow = Flow(
        wire, spot, r.out_base.at[0], r.out_base.at[1], r.out_crossed, r.out_sided, r.out_lined, r.out_out
    )
    in_flow = Flow(wire, spot, r.in_base.at[0], r.in_base.at[1], r.in_crossed, r.in_sided, r.in_lined, r.in_out)
    states, gnumer, gdenom, grad = r.states, r.gnumer, r.gdenom, r.grad
    ring = StateRing(wire, spot, r.places, True, states, r.beside, r.outgoing, r.ring, r.later)

    def grad_atten():
        ready(first)
        grad[...] = dot(r.out_full[...], r.branch[...], (1, 1))

    def grad_states():
        for parts in grid_views(
            (r.query, FDIM), (r.atten, VDIM), (r.denom, 1), (grad, VDIM), (gnumer, VDIM), (gdenom, 1), (states, None)
        ):
            grad_states_kernel(*parts)
        ring.start()

    core_of = me + 1 - 2 * (me % 2)
    shards = (me, spot.across, core_of, (core_of + 2) % 4)
    width = r.branch.shape[1] // 4

    def out_grads(other):
        for slot in range(2):
            rows = pl.ds(pl.multiple_of(shards[2 * other + slot] * width, width), width)
            value = dot(r.atten[rows, :], r.branch[...], (1, 0))
            ref = r.out_send if other else r.out_base
            for k in range(8):
                ref[slot, k] = value[k * 32 : (k + 1) * 32, :].astype(bf16)
        if other:
            r.out_wait = wire.send(r.out_send, r.out_core, spot.core).wait_recv

    def out_base():
        r.out_wait()
        for slot in range(2):
            add_chunks(r.out_base.at[slot], 0, r.out_core.at[slot], 8)

    narrow = HEADS * FDIM
    gproj = r.gproj
    gquery, gkey = gproj.at[0:narrow], gproj.at[narrow : 2 * narrow]
    gvalue = gproj.at[2 * narrow : 2 * narrow + HEADS * VDIM]
    intra_views = list(
        grid_views(
            (r.query, FDIM),
            (r.key, FDIM),
            (r.value, VDIM),
            (gnumer, VDIM),
            (gdenom, 1),
            (r.prefix, None),
            (gquery, FDIM),
            (r.gkey_in, FDIM),
            (grad, VDIM),
        )
    )

    def intra(index):
        if index == 0:
            ready(second)
        intra_back_kernel(*intra_views[index])

    def inverse(residual):
        return lax.rsqrt(jnp.mean(residual * residual, axis=-1, keepdims=True) + EPS)

    def normalise():
        ready(tokens_load)
        residual = r.tokens[...].astype(f32)
        r.normed[...] = (residual * inverse(residual) * r.gain_one[...]).astype(bf16)

    turned = r.turned

    def inter_back():
        for parts in grid_views(
            (r.key, FDIM),
            (r.value, VDIM),
            (r.later, None),
            (r.gkey_in, FDIM),
            (grad, VDIM),
            (gkey, FDIM),
            (gvalue, VDIM),
        ):
            inter_back_kernel(*parts)
        turned[...] = gproj[...].T

    def in_grads(other):
        for slot in range(2):
            columns = pl.ds(pl.multiple_of(shards[2 * other + slot] * width, width), width)
            value = dot(r.normed[:, columns], turned[...], (0, 0))
            ref = r.in_send if other else r.in_base
            for k in range(8):
                ref[slot, k] = value[k * 32 : (k + 1) * 32, :].astype(bf16)
        if other:
            r.in_wait = wire.send(r.in_send, r.in_core, spot.core).wait_recv

    def in_base():
        r.in_wait()
        for slot in range(2):
            add_chunks(r.in_base.at[slot], 0, r.in_core.at[slot], 8)

    gains, small, small_in, small_line = r.gains, r.small, r.small_in, r.small_line

    def tokens_grad():
        ready(third)
        gnormed = dot(turned[...], r.in_full[...], (1, 1))
        residual = r.tokens[...].astype(f32)
        inv = inverse(residual)
        gains[0:1, :] = jnp.sum(gnormed * residual * inv, axis=0, keepdims=True)
        weighted = gnormed * r.gain_one[...]
        slope = jnp.mean(weighted * residual, axis=-1, keepdims=True)
        r.gmiddle[...] += inv * weighted - residual * (inv * inv * inv) * slope
        r.written = wire.keep(r.gmiddle, r.tokens_out)

    def gain_grads():
        gains[1:2, :] = r.ggain_two[0:1, :]
        small[...] = jnp.zeros_like(small)
        for index in range(4):
            for row in range(4):
                start = pl.multiple_of(shards[index] * width + (row % 2) * 128, 128)
                small[index, row : row + 1, :] = gains[row // 2 : row // 2 + 1, pl.ds(start, 128)]
        r.small_wait = wire.send(small.at[2:4], small_in.at[0:2], spot.core).wait_recv

    def gains_cross():
        r.small_wait()
        small[0:2] = small[0:2] + small_in[0:2]
        r.small_wait = wire.send(small.at[1], small_in.at[2], spot.chip).wait_recv

    def gains_side():
        r.small_wait()
        small[0] = small[0] + small_in[2]
        r.small_wait = wire.send(small.at[0], small_in.at[3], spot.side).wait_recv

    def gains_line():
        r.small_wait()
        small_line[z] = small[0] + small_in[3]
        r.small_sent = [wire.send(small_line.at[z], small_line.at[z], spot.ahead[k]) for k in (1, 2, 3)]

    def gains_end():
        for copy in r.small_sent:
            copy.wait_recv()
        r.gains_out[...] = (small_line[0] + small_line[1]) + (small_line[2] + small_line[3])

    db.cross()
    grad_atten()
    grad_states()
    down_base()
    ring.forward(0, 0)
    out_grads(1)
    base(0)
    out_grads(0)
    ua.cross()
    out_base()
    da.to_side()
    ring.forward(0, 1)
    out_flow.cross()
    db.to_side()
    ring.forward(1, 0)
    base(1)
    ring.forward(1, 1)
    ua.to_side()
    da.to_line()
    base(2)
    ga.cross()
    out_flow.to_side()
    db.to_line()
    intra(0)
    ring.forward(2, 0)
    ring.forward(2, 1)
    ring.partner(1)
    intra(1)
    da.to_far()
    ring.partner(0)
    out_flow.to_line()
    intra(2)
    gb.cross()
    da.from_far()
    intra(3)
    out_flow.to_far()
    db.to_far()
    ga.to_side()
    da.along_line()
    ring.finish(1)
    out_flow.from_far()
    ua.to_line()
    db.from_far()
    base(3)
    da.along_side()
    ub.cross()
    ring.finish(0)
    gb.to_side()
    ga.to_line()
    inter_back()
    db.along_line()
    normalise()
    in_grads(1)
    in_grads(0)
    ua.to_far()
    ga.to_far()
    in_base()
    in_flow.cross()
    db.along_side()
    out_flow.along_line()
    ub.to_side()
    gb.to_line()
    tokens_grad()
    ua.from_far()
    ga.from_far()
    gb.to_far()
    out_flow.along_side()
    ua.along_line()
    ga.along_line()
    in_flow.to_side()
    gb.from_far()
    ub.to_line()
    ga.along_side()
    ub.to_far()
    gb.along_line()
    gb.along_side()
    ub.from_far()
    in_flow.to_line()
    ua.along_side()
    ub.along_line()
    in_flow.to_far()
    in_flow.from_far()
    ub.along_side()
    gain_grads()
    gains_cross()
    in_flow.along_line()
    ua.end()
    gains_side()
    db.end()
    da.end()
    in_flow.along_side()
    gb.end()
    out_flow.end()
    gains_line()
    gains_end()
    ga.end()
    ub.end()
    in_flow.end()
    r.written.wait()
    wire.end()


HBM = pl.BlockSpec(memory_space=pltpu.HBM)
VMEM = pl.BlockSpec(memory_space=pltpu.VMEM)
SMEM = pl.BlockSpec(memory_space=pltpu.SMEM)


def sems(count):
    return pltpu.SemaphoreType.DMA((count,))


def forward_call(places, tokens, gains, in_shard, weights):
    rows, model = tokens.shape
    narrow, wide = HEADS * FDIM, HEADS * VDIM
    state = (rows // BLOCK, HEADS // GROUP, STATE, 128)
    tall, model_half = weights[3].shape[0], weights[3].shape[1] // 2

    def low(*shape):
        return jax.ShapeDtypeStruct(shape, bf16)

    return pl.pallas_call(
        forward_kernel,
        out_shape=[
            low(4, *gains.shape),
            low(narrow, rows),
            low(narrow, rows),
            low(wide, rows),
            low(*state),
            low(wide, rows),
            jax.ShapeDtypeStruct((HEADS, rows), f32),
            jax.ShapeDtypeStruct((rows, model), f32),
            low(4, *in_shard.shape),
        ]
        + [low(4, *w.shape) for w in weights],
        in_specs=[SMEM, VMEM] + [HBM] * 6,
        out_specs=[VMEM] * 8 + [HBM] * 5,
        scratch_shapes=[
            pltpu.VMEM((4, *in_shard.shape), bf16),
            pltpu.VMEM((4, *weights[0].shape), bf16),
            pltpu.VMEM((rows, model), bf16),
            pltpu.VMEM(state, bf16),
            pltpu.VMEM((3, *state), bf16),
            pltpu.VMEM(state, bf16),
            pltpu.VMEM(state, bf16),
            pltpu.VMEM((wide, rows), f32),
            pltpu.VMEM((HEADS, rows), f32),
            *(pltpu.VMEM(w.shape, bf16) for w in weights[1:3]),
            *[pltpu.VMEM((tall, model_half), bf16)] * 2,
            sems(64),
            sems(64),
            sems(24),
        ],
        compiler_params=pltpu.CompilerParams(collective_id=1, has_side_effects=True, vmem_limit_bytes=58 << 20),
    )(places, tokens, gains, in_shard, *weights)


def settle_kernel(down_ref, gate_ref, up_ref, out_ref, in_ref, output_ref, tokens_ref, *outs):
    tall, broad = down_ref.shape[2:]
    down_out, gate_out, up_out, out_out = outs[:4]
    for half in range(2):
        down_out[half * tall : (half + 1) * tall, :] = down_ref[half, 0].astype(f32)
        gate_out[:, half * broad : (half + 1) * broad] = gate_ref[half, 0].astype(f32)
        up_out[:, half * broad : (half + 1) * broad] = up_ref[half, 0].astype(f32)
    out_out[...] = out_ref[0].astype(f32)
    start = 0
    for out in outs[4:7]:
        stop = start + out.shape[1]
        out[...] = in_ref[0, :, start:stop].astype(f32)
        start = stop
    outs[7][...] = output_ref[...]
    outs[8][...] = tokens_ref[...]


def settle_call(down, gate, up, out, ins, output, tokens):
    tall, broad = down.shape[2:]
    size, model = out.shape[1:]
    narrow = HEADS * FDIM
    rows = output.shape[0]
    blocks = pl.BlockSpec((2, 1, tall, broad), lambda k: (0, k, 0, 0))

    def line(height, width):
        return pl.BlockSpec((height, width), lambda k: (k, 0))

    def eighths(a):
        return pl.BlockSpec((1, *a.shape[1:]), lambda k: (k, 0, 0))

    shapes = [(2 * tall, 8 * broad), (8 * tall, 2 * broad), (8 * tall, 2 * broad), (8 * size, model)]
    widths = (narrow, narrow, ins.shape[2] - 2 * narrow)
    shapes += [(8 * size, width) for width in widths]
    whole = [line(rows // 8, model)] * 2
    return pl.pallas_call(
        settle_kernel,
        out_shape=[jax.ShapeDtypeStruct(shape, f32) for shape in shapes]
        + [jax.ShapeDtypeStruct(a.shape, a.dtype) for a in (output, tokens)],
        grid=(8,),
        in_specs=[blocks, blocks, blocks, eighths(out), eighths(ins), *whole],
        out_specs=[
            pl.BlockSpec((2 * tall, broad), lambda k: (0, k)),
            line(tall, 2 * broad),
            line(tall, 2 * broad),
            line(size, model),
            *(line(size, width) for width in widths),
            *whole,
        ],
        compiler_params=pltpu.CompilerParams(vmem_limit_bytes=60 << 20),
    )(down, gate, up, out, ins, output, tokens)


def masked_sums(pieces, masks, dtype):
    total = None
    for index, piece in enumerate(pieces):
        for block in range(piece.shape[0]):
            term = masks[:, index, block][:, None, None, None] * piece[block].astype(f32)[None]
            total = term if total is None else total + term
    return total.astype(dtype)


class Exchange:
    def __init__(self, states, positions, own, count, later):
        self.pieces, self.sources, self.own, self.count, self.later = [states], [own], own, count, later
        self.table = positions.reshape(count, states.shape[0])

    def mask(self, target):
        there = self.table[target][:, None, None]
        here = self.table[jnp.stack(self.sources)][None]
        return ((here > there) if self.later else (here < there)).astype(f32)

    def ring(self):
        return self.pieces[-1], "ctx", [(i, (i + 2) % self.count) for i in range(self.count)]

    def passed(self, piece):
        self.sources.append((self.own - 2 * len(self.pieces)) % self.count)
        self.pieces.append(piece)

    def partner(self):
        return trade(masked_sums(self.pieces, self.mask(self.own ^ 1), bf16), 1, self.count)

    def total(self, received):
        return (masked_sums(self.pieces, self.mask(self.own), f32) + received.astype(f32)).astype(bf16)


def backward_call(arrays):
    names, specs, values = [], [], []
    get = SimpleNamespace(**arrays)
    for name, array in arrays.items():
        names.append(name)
        values.append(array)
        specs.append(SMEM if array.dtype == jnp.int32 else VMEM if array.shape[0] <= 8 and array.dtype == f32 else HBM)
    rows, model = get.tokens_hbm.shape
    columns = get.in_full_hbm.shape[1]
    block = get.down_keep.shape[2:]
    narrow, wide = HEADS * FDIM, HEADS * VDIM
    state = get.prefix_hbm.shape
    outs = dict(
        tokens_out=((rows, model), f32, HBM),
        down_out=((2, 8, *block), bf16, HBM),
        gate_out=((2, 8, *block), bf16, HBM),
        up_out=((2, 8, *block), bf16, HBM),
        out_out=((8, 32, model), bf16, HBM),
        in_out=((8, 32, columns), bf16, HBM),
        gains_out=((8, 128), f32, VMEM),
    )
    scratch = dict(
        down_core=((2, 8, *block), bf16),
        down_stage=((2, 8, *block), bf16),
        gate_core=((2, 2, 8, *block), bf16),
        up_core=((2, 2, 8, *block), bf16),
        stage=((2, 2, 8, *block), bf16),
        crossed=((6, 8, *block), bf16),
        sided=((6, 4, *block), bf16),
        lined=((6, 3, *block), bf16),
        out_full=((wide, model), bf16),
        branch=((rows, model), bf16),
        atten=((wide, rows), bf16),
        denom=((HEADS, rows), f32),
        query=((narrow, rows), bf16),
        key=((narrow, rows), bf16),
        value=((wide, rows), bf16),
        prefix=(state, bf16),
        tokens=((rows, model), bf16),
        in_full=((model, columns), bf16),
        gmiddle=((rows, model), f32),
        grad=((wide, rows), f32),
        gnumer=((wide, rows), bf16),
        gdenom=((HEADS, rows), f32),
        states=(state, bf16),
        ring=((3, *state), bf16),
        outgoing=(state, bf16),
        beside=(state, bf16),
        later=(state, bf16),
        gproj=((columns, rows), bf16),
        gkey_in=((narrow, rows), f32),
        normed=((rows, model), bf16),
        turned=((rows, columns), bf16),
        gains=((8, model), f32),
        small=((4, 8, 128), f32),
        small_in=((4, 8, 128), f32),
        small_line=((4, 8, 128), f32),
        out_base=((2, 8, 32, model), bf16),
        out_send=((2, 8, 32, model), bf16),
        out_core=((2, 8, 32, model), bf16),
        out_crossed=((8, 32, model), bf16),
        out_sided=((4, 32, model), bf16),
        out_lined=((3, 32, model), bf16),
        in_base=((2, 8, 32, columns), bf16),
        in_send=((2, 8, 32, columns), bf16),
        in_core=((2, 8, 32, columns), bf16),
        in_crossed=((8, 32, columns), bf16),
        in_sided=((4, 32, columns), bf16),
        in_lined=((3, 32, columns), bf16),
    )
    names += [*outs, *scratch, *dict(send_sems=0, recv_sems=0, local_sems=0)]
    return pl.pallas_call(
        functools.partial(backward_kernel, tuple(names)),
        out_shape=[jax.ShapeDtypeStruct(shape, dtype) for shape, dtype, _ in outs.values()],
        in_specs=specs,
        out_specs=[spec for _, _, spec in outs.values()],
        scratch_shapes=[pltpu.VMEM(shape, dtype) for shape, dtype in scratch.values()]
        + [sems(100), sems(100), sems(48)],
        compiler_params=pltpu.CompilerParams(collective_id=2, has_side_effects=True, vmem_limit_bytes=60 << 20),
    )(*values)


def body(count):
    def layer(
        tokens, block_pos, gain_attn, w_query, w_key, w_value, w_out, gain_ffn, w_gate, w_up, w_down, cotangent
    ):
        own = lax.axis_index("ctx")
        me = lax.axis_index("fsdp").astype(jnp.int32).reshape(1)
        positions = block_pos[0]
        in_shard = jnp.concatenate([w_query, w_key, w_value], axis=1)
        gains = jnp.stack([gain_attn, gain_ffn])
        weights = (w_out, w_gate.T, w_up.T, w_down)
        narrow = HEADS * FDIM
        rows = tokens.shape[1]
        unit = 2 * rows * BLOCK * HEADS
        width = in_shard.shape[1]
        if count == 8:
            forward = forward_call(block_pos, tokens[0], gains, in_shard, weights)
            gains, query, key, value, prefix, atten, denom, middle, in_full, out_full, gates, ups, downs = forward
        else:
            gains, in_full = (lax.all_gather(a, "fsdp") for a in (gains, in_shard))
        gain_one, gain_two = (gains[:, k].reshape(-1).astype(f32) for k in (0, 1))
        in_full = in_full.reshape(-1, width)
        if count == 8:
            out_full = out_full.reshape(-1, w_out.shape[1])
        else:
            residual = tokens[0].astype(f32)
            inv_one = lax.rsqrt(jnp.mean(residual * residual, axis=-1, keepdims=True) + EPS)
            normed_one = (residual * inv_one * gain_one).astype(bf16)
            projected = dot(in_full, normed_one, (0, 1)).astype(bf16)
            query, key, value = projected[:narrow], projected[narrow : 2 * narrow], projected[2 * narrow :]
            (own_states,) = attention_call(
                states_kernel, ("narrow", "wide"), (("state", bf16),), rows, unit * FEAT
            )(key, value)
            numer, denom = attention_call(
                intra_kernel, ("narrow", "narrow", "wide"), (("wide", f32), ("head", f32)), rows, unit * 256
            )(query, key, value)
            links = Links()
            states = Exchange(own_states, positions, own, count, False)
            for _ in range(1, count // 2):
                states.passed(links.round([states.ring()])[0])
            prefix = states.total(links.round([states.partner()])[0])
            atten, denom = attention_call(
                inter_kernel,
                ("narrow", "state", "wide", "head"),
                (("wide", bf16), ("head", f32)),
                rows,
                unit * FEAT,
            )(query, prefix, numer, denom)
            out_full, gates, ups, downs = (lax.all_gather(w, "fsdp") for w in weights)
            out_full = out_full.reshape(-1, w_out.shape[1])
            middle = residual + dot(atten, out_full, (0, 0))
        ffn_inputs = (middle, gain_two.reshape(1, -1), cotangent[0], gates, ups, downs)
        if count == 8:
            results = ffn_send_call(*ffn_inputs)
            output, grad_middle, branch, grad_gain_two = results[:4]
            gate_keep, up_keep, down_keep, second_cross, gate_got, up_got, down_got, first_cross = results[4:]
            arrays = dict(
                places=block_pos,
                gain_one=gain_one.reshape(1, -1),
                ggain_two=grad_gain_two,
                out_full_hbm=out_full,
                branch_hbm=branch,
                atten_hbm=atten,
                denom_hbm=denom,
                query_hbm=query,
                key_hbm=key,
                value_hbm=value,
                prefix_hbm=prefix,
                tokens_hbm=tokens[0],
                in_full_hbm=in_full,
                gmiddle_hbm=grad_middle,
                down_keep=down_keep,
                down_got=down_got,
                first_cross=first_cross,
                second_cross=second_cross,
                gate_keep=gate_keep,
                gate_got=gate_got,
                up_keep=up_keep,
                up_got=up_got,
            )
            grad_tokens, down_sum, gate_sum, up_sum, out_sum, in_sum, small = backward_call(arrays)
            gain_sums = small[:4].reshape(2, -1)
        else:
            results = ffn_call(me, *ffn_inputs)
            output, grad_middle, branch, grad_gain_two = results[:4]
            pairs = [results[k : k + 2] for k in (8, 4, 6)]
            grad_atten = dot(out_full, branch, (1, 1))
            gnumer, gdenom, grad_states = attention_call(
                grad_states_kernel,
                ("narrow", "wide", "head", "wide"),
                (("wide", bf16), ("head", f32), ("state", bf16)),
                rows,
                unit * FEAT,
            )(query, atten, denom, grad_atten)
            gquery, gkey, gvalue = attention_call(
                intra_back_kernel,
                ("narrow", "narrow", "wide", "wide", "head", "state"),
                (("narrow", bf16), ("narrow", f32), ("wide", f32)),
                rows,
                unit * 512,
            )(query, key, value, gnumer, gdenom, prefix)
            links = Links()
            backward = Exchange(grad_states, positions, own, count, True)
            for _ in range(1, count // 2):
                backward.passed(links.round([backward.ring()])[0])
            later = backward.total(links.round([backward.partner()])[0])
            gkey, gvalue = attention_call(
                inter_back_kernel,
                ("narrow", "wide", "state", "narrow", "wide"),
                (("narrow", bf16), ("wide", bf16)),
                rows,
                unit * 256,
            )(key, value, later, gkey, gvalue)
            gprojected = jnp.concatenate([gquery, gkey, gvalue], axis=0)
            gnormed_one = dot(gprojected, in_full, (0, 1))
            weighted_one = gnormed_one * gain_one
            grad_gain_one = jnp.sum(gnormed_one * residual * inv_one, axis=0)
            grad_tokens = (
                grad_middle
                + inv_one * weighted_one
                - residual
                * (inv_one * inv_one * inv_one)
                * jnp.mean(weighted_one * residual, axis=-1, keepdims=True)
            )

            def summed(keep, send):
                got = lax.ppermute(send, "fsdp", CORE)
                cross = (keep[:, 1].astype(f32) + got[:, 1].astype(f32)).astype(bf16)
                got_cross = lax.ppermute(cross, "fsdp", CHIP)
                total = keep[:, 0].astype(f32) + got[:, 0].astype(f32) + got_cross.astype(f32)
                return lax.psum(total.astype(bf16), "ctx")

            def scattered(grad):
                return lax.psum(lax.psum_scatter(grad, "fsdp", scatter_dimension=0, tiled=True), "ctx")

            down_sum, gate_sum, up_sum = (summed(*pair) for pair in pairs)
            out_sum = scattered(dot(atten, branch, (1, 0)).astype(bf16)).reshape(8, -1, branch.shape[1])
            in_sum = scattered(dot(normed_one, gprojected, (0, 1)).astype(bf16)).reshape(8, -1, width)
            gain_sums = scattered(jnp.stack([grad_gain_one, grad_gain_two[0]], axis=1)).T
        down_grad, gate_grad, up_grad, out_grad, *in_grads, output, grad_tokens = settle_call(
            down_sum, gate_sum, up_sum, out_sum, in_sum, output, grad_tokens
        )
        return (
            output[None],
            grad_tokens[None],
            gain_sums[0],
            *in_grads,
            out_grad,
            gain_sums[1],
            gate_grad.T,
            up_grad.T,
            down_grad,
        )

    return layer


def solution(mesh):
    rows = P("fsdp", None)
    seqs = P("fsdp", "ctx", None)
    vec = P("fsdp")
    in_specs = (seqs, rows, vec, rows, rows, rows, rows, vec, rows, rows, rows, seqs)
    out_specs = (seqs, seqs, vec, rows, rows, rows, rows, vec, rows, rows, rows)
    return jax.shard_map(
        body(mesh.shape["ctx"]), mesh=mesh, in_specs=in_specs, out_specs=out_specs, check_vma=False
    )
```

```python
import functools
from types import SimpleNamespace

import jax
import jax.numpy as jnp
from jax import lax
from jax.experimental import pallas as pl
from jax.experimental.pallas import tpu as pltpu
from jax.sharding import PartitionSpec as P

HEADS = 16
FDIM = 16
VDIM = 64
BLOCK = 256
GROUP = 8
FEAT = 160
STATE = GROUP // 2 * FEAT + 2 * GROUP
EPS = 1e-05
ROOT_HALF = 0.7071067811865476

f32 = jnp.float32
bf16 = jnp.bfloat16


def dims(lhs, rhs):
    return (((lhs,), (rhs,)), ((), ()))


def dot(lhs, rhs, contract):
    return lax.dot_general(lhs, rhs, dims(*contract), preferred_element_type=f32)


def turned(u, shift):
    return pltpu.roll(u, FDIM - shift, 0)


def features(u, pair_weight):
    rows = [u, u * u * ROOT_HALF]
    for shift in range(1, 8):
        rows.append(u * turned(u, shift) * ROOT_HALF)
    rows.append(u[:8] * u[8:] * ROOT_HALF)
    one = (lax.broadcasted_iota(jnp.int32, (8, u.shape[1]), 0) == 0).astype(f32)
    linear = jnp.concatenate(rows[:2], axis=0).astype(bf16)
    pairs = jnp.concatenate(rows[2:], axis=0).astype(bf16) * pair_weight
    del rows
    return jnp.concatenate([linear.astype(f32), pairs.astype(f32), one], axis=0).astype(bf16)


def features_back(u, g):
    total = g[:16] + (2.0 * ROOT_HALF) * (g[16:32] * u)
    for shift in range(1, 8):
        here = (2.0 * ROOT_HALF) * g[16 + 16 * shift : 32 + 16 * shift]
        total = total + here * turned(u, shift) + pltpu.roll(here * u, shift, 0)
    here = (2.0 * ROOT_HALF) * g[144:152]
    return total + jnp.concatenate([here * u[8:], here * u[:8]], axis=0)


def halved(ref, head):
    return ref[head * FDIM : (head + 1) * FDIM, :].astype(f32) * 0.5


def write_states(out_ref, feat, value_pair, weight_row, head):
    pair = head // 2
    product = dot(feat, value_pair, (1, 1))
    half = slice(0, 64) if head % 2 == 0 else slice(64, 128)
    out_ref[0, 0, pair * FEAT : (pair + 1) * FEAT, half] = product[:, half].astype(bf16)
    norm = dot(weight_row, feat, (1, 1))
    base = GROUP // 2 * FEAT + 2 * head
    out_ref[0, 0, base : base + 1, :] = norm[:1, :128].astype(bf16)
    out_ref[0, 0, base + 1 : base + 2, :] = jnp.concatenate([norm[:1, 128:], jnp.zeros((1, 96), f32)], axis=1).astype(bf16)


def norm_row(state_ref, head):
    base = GROUP // 2 * FEAT + 2 * head
    return state_ref[0, 0, base : base + 1, :], state_ref[0, 0, base + 1 : base + 2, :32]


def head_state(state_ref, head):
    pair = head // 2
    return state_ref[0, 0, pair * FEAT : (pair + 1) * FEAT, 64 * (head % 2) : 64 * (head % 2) + 64]


def states_kernel(key_ref, value_ref, out_ref):
    ones = jnp.ones((8, BLOCK), bf16)
    for head in range(GROUP):
        feat = features(halved(key_ref, head), 1.0)
        pair = head // 2
        write_states(out_ref, feat, value_ref[pair * 128 : (pair + 1) * 128, :], ones, head)


def intra_kernel(query_ref, key_ref, value_ref, numer_ref, denom_ref):
    for head in range(GROUP):
        rows = slice(head * FDIM, (head + 1) * FDIM)
        wide = slice(head * VDIM, (head + 1) * VDIM)
        scores = dot(key_ref[rows, :], query_ref[rows, :], (0, 0)) * 0.25
        kernel = 1.0 + scores + 0.5 * scores * scores
        denom_ref[head : head + 1, :] = jnp.sum(kernel, axis=0, keepdims=True)
        numer_ref[wide, :] = dot(value_ref[wide, :], kernel.astype(bf16), (1, 0))


def inter_kernel(query_ref, prefix_ref, numer_ref, denom_in_ref, atten_ref, denom_ref):
    for head in range(GROUP):
        wide = slice(head * VDIM, (head + 1) * VDIM)
        feat = features(halved(query_ref, head), 2.0)
        numer = numer_ref[wide, :] + dot(head_state(prefix_ref, head), feat, (0, 0))
        first, second = norm_row(prefix_ref, head)
        denom = denom_in_ref[head : head + 1, :] + dot(first, feat[:128], (1, 0)) + dot(second, feat[128:], (1, 0))
        denom_ref[head : head + 1, :] = denom
        atten_ref[wide, :] = (numer / denom).astype(bf16)


def grad_states_kernel(query_ref, atten_ref, denom_ref, grad_ref, gnumer_ref, gdenom_ref, out_ref):
    for pair in range(GROUP // 2):
        for head in (2 * pair, 2 * pair + 1):
            wide = slice(head * VDIM, (head + 1) * VDIM)
            denom = denom_ref[head : head + 1, :]
            grad = grad_ref[wide, :]
            gnumer_ref[wide, :] = (grad / denom).astype(bf16)
            gdenom = -jnp.sum(grad * atten_ref[wide, :].astype(f32), axis=0, keepdims=True) / denom
            gdenom_ref[head : head + 1, :] = gdenom.astype(bf16).astype(f32)
        for head in (2 * pair, 2 * pair + 1):
            feat = features(halved(query_ref, head), 1.0)
            weights = jnp.broadcast_to(gdenom_ref[head : head + 1, :], (8, BLOCK)).astype(bf16)
            write_states(out_ref, feat, gnumer_ref[pair * 128 : (pair + 1) * 128, :], weights, head)


def intra_back_kernel(
    query_ref, key_ref, value_ref, gnumer_ref, gdenom_ref, prefix_ref, gquery_ref, gkey_ref, gvalue_ref
):
    for head in range(GROUP):
        rows = slice(head * FDIM, (head + 1) * FDIM)
        wide = slice(head * VDIM, (head + 1) * VDIM)
        query, key = query_ref[rows, :], key_ref[rows, :]
        gnumer = gnumer_ref[wide, :]
        gdenom = gdenom_ref[head : head + 1, :]
        scores = dot(key, query, (0, 0)) * 0.25
        kernel = (1.0 + scores + 0.5 * scores * scores).astype(bf16)
        gkernel = dot(value_ref[wide, :], gnumer, (0, 0)) + gdenom
        gscores = ((1.0 + scores) * gkernel).astype(bf16)
        gvalue_ref[wide, :] = dot(gnumer, kernel, (1, 1))
        gkey_ref[rows, :] = dot(query, gscores, (1, 1)) * 0.25
        first, second = norm_row(prefix_ref, head)
        gdenom_low = gdenom.astype(bf16)
        outer_prod = jnp.concatenate([dot(first, gdenom_low, (0, 0)), dot(second, gdenom_low, (0, 0))], axis=0)
        gfeat = dot(head_state(prefix_ref, head), gnumer, (1, 0)) + outer_prod
        gquery = dot(key, gscores, (1, 0)) * 0.25 + 0.5 * features_back(halved(query_ref, head), gfeat)
        gquery_ref[rows, :] = gquery.astype(bf16)


def inter_back_kernel(key_ref, value_ref, later_ref, gkey_in_ref, gvalue_in_ref, gkey_ref, gvalue_ref):
    ones = jnp.ones((1, BLOCK), bf16)
    for head in range(GROUP):
        rows = slice(head * FDIM, (head + 1) * FDIM)
        wide = slice(head * VDIM, (head + 1) * VDIM)
        u = halved(key_ref, head)
        state = head_state(later_ref, head)
        first, second = norm_row(later_ref, head)
        outer_prod = jnp.concatenate([dot(first, ones, (0, 0)), dot(second, ones, (0, 0))], axis=0)
        gfeat = dot(state, value_ref[wide, :], (1, 0)) + outer_prod
        gkey_ref[rows, :] = (gkey_in_ref[rows, :] + 0.5 * features_back(u, gfeat)).astype(bf16)
        feat = features(u, 2.0)
        gvalue_ref[wide, :] = (gvalue_in_ref[wide, :] + dot(state, feat, (0, 0))).astype(bf16)


def attention_call(kernel, ins, outs, tokens, flops):
    blocks = tokens // BLOCK
    groups = HEADS // GROUP
    forms = {
        "narrow": ((GROUP * FDIM, BLOCK), lambda b, g: (g, b), (HEADS * FDIM, tokens)),
        "wide": ((GROUP * VDIM, BLOCK), lambda b, g: (g, b), (HEADS * VDIM, tokens)),
        "head": ((GROUP, BLOCK), lambda b, g: (g, b), (HEADS, tokens)),
        "state": ((1, 1, STATE, 128), lambda b, g: (b, g, 0, 0), (blocks, groups, STATE, 128)),
    }

    def spec(name):
        return pl.BlockSpec(forms[name][0], forms[name][1])

    def call(*arrays):
        moved = sum(a.size * a.dtype.itemsize for a in arrays)
        return pl.pallas_call(
            kernel,
            out_shape=[jax.ShapeDtypeStruct(forms[name][2], dtype) for name, dtype in outs],
            grid=(blocks, groups),
            in_specs=[spec(name) for name in ins],
            out_specs=[spec(name) for name, _ in outs],
            compiler_params=pltpu.CompilerParams(vmem_limit_bytes=40 << 20),
            cost_estimate=pl.CostEstimate(flops=flops, bytes_accessed=2 * moved, transcendentals=0),
        )(*arrays)

    return call


ORDER = (0, 2, 1, 3)


def place(step):
    return (step % 2) * 2 + step // 2


def ffn_begin(me, middle_ref, gain_ref, cot_ref, normed, x_own, x_turned, cot_turned, total, gnormed, inverse):
    width = x_own.shape[2]
    core = me + 1 - 2 * (me % 2)
    normed[...] = (middle_ref[...] * inverse() * gain_ref[1:2, :]).astype(bf16)
    for r, shard in enumerate((me, core, (me + 2) % 4, (core + 2) % 4)):
        x_own[r] = normed[:, pl.ds(pl.multiple_of(shard * width, width), width)]
    x_turned[...] = normed[...].T
    cot_turned[...] = cot_ref[...].T
    total[...] = jnp.zeros_like(total)
    gnormed[...] = jnp.zeros_like(gnormed)


def ffn_tile(gates, ups, down, x_turned, cot_turned):
    width = gates.shape[2]
    x_part = x_turned[:width, :]
    gate = dot(gates[0], x_part, (1, 0))
    up = dot(ups[0], x_part, (1, 0))
    for r in range(1, 4):
        x_part = x_turned[r * width : (r + 1) * width, :]
        gate = gate + dot(gates[r], x_part, (1, 0))
        up = up + dot(ups[r], x_part, (1, 0))
    ghidden = dot(down, cot_turned[...], (1, 0))
    sigmoid = jax.nn.sigmoid(gate)
    silu = gate * sigmoid
    hidden = (silu * up).astype(bf16)
    ggate = (ghidden * up * (sigmoid * (1.0 + gate * (1.0 - sigmoid)))).astype(bf16)
    return hidden, ggate, (ghidden * silu).astype(bf16)


def ffn_end(middle_ref, gain_ref, cot_ref, total, gnormed, inverse, output_ref, gmiddle_ref, branch_ref, ggain_ref):
    middle, inv, cot = middle_ref[...], inverse(), cot_ref[...].astype(f32)
    grad = gnormed[...]
    output_ref[...] = (middle + total[...]).astype(bf16)
    ggain_ref[...] = jnp.broadcast_to(jnp.sum(grad * middle * inv, axis=0, keepdims=True), ggain_ref.shape)
    weighted = grad * gain_ref[1:2, :]
    slope = jnp.mean(weighted * middle, axis=-1, keepdims=True)
    gmiddle = cot + inv * weighted - middle * (inv * inv * inv) * slope
    gmiddle_ref[...] = gmiddle
    branch_ref[...] = gmiddle.astype(bf16)


def ffn_kernel(me_ref, middle_ref, gain_ref, cot_ref, gates, ups, downs, *refs):
    output_ref, gmiddle_ref, branch_ref, ggain_ref = refs[:4]
    gate_keep, gate_send, up_keep, up_send, down_keep, down_send = refs[4:10]
    normed, x_own, x_turned, cot_turned, total, gnormed = refs[10:]
    step = pl.program_id(0)
    width = gates.shape[2]

    def inverse():
        middle = middle_ref[...]
        return lax.rsqrt(jnp.mean(middle * middle, axis=-1, keepdims=True) + EPS)

    @pl.when(step == 0)
    def _():
        ffn_begin(
            me_ref[0], middle_ref, gain_ref, cot_ref, normed, x_own, x_turned, cot_turned, total, gnormed, inverse
        )

    hidden, ggate, gup = ffn_tile(gates, ups, downs[0], x_turned, cot_turned)
    down = downs[0]
    total[...] += dot(hidden, down, (0, 0))
    gdown = dot(hidden, cot_ref[...], (1, 0))
    tall, broad = down_keep.shape[3:]

    def store(ref, slot, grad):
        for half in range(2):
            for eighth in range(8):
                ref[half, slot, eighth] = grad[
                    half * tall : (half + 1) * tall, eighth * broad : (eighth + 1) * broad
                ].astype(bf16)

    @pl.when(step < 2)
    def _():
        store(down_keep, 0, gdown)

    @pl.when(step >= 2)
    def _():
        store(down_send, 0, gdown)

    def store_turned(keep, send, r, grad):
        ref = send if r % 2 else keep
        for half in range(2):
            for eighth in range(2):
                ref[half, r // 2, eighth] = grad[
                    eighth * tall : (eighth + 1) * tall, half * broad : (half + 1) * broad
                ].astype(bf16)

    for r in range(4):
        part = slice(r * width, (r + 1) * width)
        gnormed[:, part] += dot(ggate, gates[r], (0, 0)) + dot(gup, ups[r], (0, 0))
        store_turned(gate_keep, gate_send, r, dot(ggate, x_own[r], (1, 0)))
        store_turned(up_keep, up_send, r, dot(gup, x_own[r], (1, 0)))

    @pl.when(step == 3)
    def _():
        ffn_end(middle_ref, gain_ref, cot_ref, total, gnormed, inverse, output_ref, gmiddle_ref, branch_ref, ggain_ref)


def ffn_call(me, middle, gain, cot, gates, ups, downs):
    rows, model = middle.shape
    _, hidden, width = gates.shape
    tile = downs.shape[1]
    once = pl.Buffered(1)

    def whole(shape, **kw):
        return pl.BlockSpec(shape, lambda s, me: (0,) * len(shape), **kw)

    columns = pl.BlockSpec((4, tile, width), lambda s, me: (0, me[0] ^ place(s), 0))
    block = (tile // 2, model // 8)
    pair = pl.BlockSpec((2, 2, 2, *block), lambda s, me: (0, 0, me[0] ^ place(s), 0, 0))
    grads = jax.ShapeDtypeStruct((2, 2, 8, *block), bf16)
    return pl.pallas_call(
        ffn_kernel,
        out_shape=[
            jax.ShapeDtypeStruct((rows, model), bf16),
            jax.ShapeDtypeStruct((rows, model), f32),
            jax.ShapeDtypeStruct((rows, model), bf16),
            jax.ShapeDtypeStruct((8, model), f32),
            grads,
            grads,
            grads,
            grads,
            grads,
            grads,
        ],
        grid_spec=pltpu.PrefetchScalarGridSpec(
            num_scalar_prefetch=1,
            grid=(4,),
            in_specs=[
                whole((rows, model), pipeline_mode=once),
                whole((2, model)),
                whole((rows, model), pipeline_mode=once),
                columns,
                columns,
                pl.BlockSpec((1, tile, model), lambda s, me: (me[0] ^ place(s), 0, 0)),
            ],
            out_specs=[
                whole((rows, model), pipeline_mode=once),
                whole((rows, model), pipeline_mode=once),
                whole((rows, model), pipeline_mode=once),
                whole((8, model)),
                pair,
                pair,
                pair,
                pair,
                pl.BlockSpec((2, 1, 8, *block), lambda s, me: (0, jnp.minimum(s, 1), 0, 0, 0)),
                pl.BlockSpec((2, 1, 8, *block), lambda s, me: (0, jnp.maximum(s - 2, 0), 0, 0, 0)),
            ],
            scratch_shapes=[
                pltpu.VMEM((rows, model), bf16),
                pltpu.VMEM((4, rows, width), bf16),
                pltpu.VMEM((model, rows), bf16),
                pltpu.VMEM((model, rows), bf16),
                pltpu.VMEM((rows, model), f32),
                pltpu.VMEM((rows, model), f32),
            ],
        ),
        compiler_params=pltpu.CompilerParams(vmem_limit_bytes=58 << 20),
        cost_estimate=pl.CostEstimate(
            flops=18 * rows * model * hidden, bytes_accessed=14 * hidden * model, transcendentals=0
        ),
    )(me, middle, gain, cot, gates, ups, downs)


CORE = [(0, 1), (1, 0), (2, 3), (3, 2)]
CHIP = [(0, 2), (2, 0), (1, 3), (3, 1)]


class Links:
    def __init__(self):
        self.last = ()

    def round(self, sends, beside=()):
        arrays = [send[0] for send in sends]
        if self.last:
            arrays = lax.optimization_barrier((*arrays, *self.last))[: len(arrays)]
        results = [lax.ppermute(a, axis, perm) for a, (_, axis, perm) in zip(arrays, sends)]
        self.last = (*results, *beside)
        return results


def trade(array, bits, count):
    return array, "ctx", [(i, i ^ bits) for i in range(count)]


MESH = pl.DeviceIdType.MESH


class Spot:
    def __init__(self):
        self.me = lax.axis_index("fsdp")
        self.own = lax.axis_index("ctx")
        self.core = {"fsdp": self.me + 1 - 2 * (self.me % 2)}
        self.across = (self.me + 2) % 4
        self.chip = {"fsdp": self.across}
        self.y = self.own % 2
        self.z = self.own // 2
        self.side = {"ctx": self.own + 1 - 2 * self.y}
        self.next = {"ctx": self.own + 2 - 4 * (self.z % 2)}
        self.ahead = [None] + [{"ctx": (self.own + 2 * k) % 8} for k in (1, 2, 3)]

    def greet(self, neighbours):
        barrier = pltpu.get_barrier_semaphore()
        for neighbour in neighbours:
            pl.semaphore_signal(barrier, inc=1, device_id=neighbour, device_id_type=MESH)
        pl.semaphore_wait(barrier, len(neighbours))


class Wire:
    def __init__(self, send_sems, recv_sems, local_sems):
        self.send_sems, self.recv_sems, self.local_sems = send_sems, recv_sems, local_sems
        self.sent, self.local, self.count = [], [], 0

    def send(self, source, target, device):
        k = self.count
        self.count += 1
        copy = pltpu.make_async_remote_copy(
            src_ref=source,
            dst_ref=target,
            send_sem=self.send_sems.at[k],
            recv_sem=self.recv_sems.at[k],
            device_id=device,
            device_id_type=MESH,
        )
        copy.start()
        self.sent.append(copy)
        return copy

    def keep(self, source, target):
        copy = pltpu.make_async_copy(source, target, self.local_sems.at[len(self.local)])
        copy.start()
        self.local.append(copy)
        return copy

    def left(self, copy):
        copy.wait_send()
        self.sent = [other for other in self.sent if other is not copy]

    def end(self):
        for copy in self.sent:
            copy.wait_send()


def tile_at(step):
    me = lax.axis_index("fsdp")
    place = 3 - step
    return 2 * ((me // 2 + place // 2) % 2) + (me % 2 + place) % 2


def ffn_send_kernel(middle_ref, gain_ref, cot_ref, gates, ups, downs, *refs):
    output_ref, gmiddle_ref, branch_ref, ggain_ref = refs[:4]
    gate_keep, up_keep, down_keep, down_cross, gate_got, up_got, down_got, crossed = refs[4:12]
    normed, x_own, x_turned, cot_turned, total, gnormed = refs[12:18]
    sending, down_first, down_second, down_in, crossing, send_sems, recv_sems = refs[18:]
    step = pl.program_id(0)
    spot = Spot()
    tall, broad = down_keep.shape[2:]
    width = gates.shape[2]

    def copy(k, source, target, device):
        return pltpu.make_async_remote_copy(
            src_ref=source,
            dst_ref=target,
            send_sem=send_sems.at[k],
            recv_sem=recv_sems.at[k],
            device_id=device,
            device_id_type=MESH,
        )

    def tile_copy(at, which):
        got = (gate_got, up_got)[which].at[:, :, pl.ds(2 * tile_at(at), 2)]
        return copy(2 * at + which, sending.at[at % 2, which], got, spot.core)

    first = copy(8, down_first, down_in, spot.core)
    second = copy(9, down_second, down_got, spot.core)
    cross = copy(10, crossing, crossed, spot.chip)

    def inverse():
        middle = middle_ref[...]
        return lax.rsqrt(jnp.mean(middle * middle, axis=-1, keepdims=True) + EPS)

    @pl.when(step == 0)
    def _():
        spot.greet([spot.core, spot.chip])
        ffn_begin(
            spot.me, middle_ref, gain_ref, cot_ref, normed, x_own, x_turned, cot_turned, total, gnormed, inverse
        )

    hidden, ggate, gup = ffn_tile(gates, ups, downs[0], x_turned, cot_turned)
    gdown = dot(hidden, cot_ref[...], (1, 0))

    def down_block(half, eighth):
        return gdown[half * tall : (half + 1) * tall, eighth * broad : (eighth + 1) * broad]

    def store(ref):
        for half in range(2):
            for eighth in range(8):
                ref[half, eighth] = down_block(half, eighth).astype(bf16)

    @pl.when(step == 0)
    def _():
        store(down_first)
        first.start()

    @pl.when(step == 1)
    def _():
        first.wait_recv()
        for half, ref in enumerate((crossing, down_cross)):
            for eighth in range(8):
                ref[eighth] = (down_block(half, eighth) + down_in[half, eighth].astype(f32)).astype(bf16)
        cross.start()

    @pl.when(step == 2)
    def _():
        store(down_second)
        second.start()

    @pl.when(step == 3)
    def _():
        store(down_keep)

    for at in range(4):

        @pl.when(step == at)
        def _(at=at):
            if at >= 2:
                tile_copy(at - 2, 0).wait_send()
                tile_copy(at - 2, 1).wait_send()
            for which, grad in enumerate((ggate, gup)):
                for slot in range(2):
                    value = dot(grad, x_own[2 * slot + 1], (1, 0))
                    for half in range(2):
                        for eighth in range(2):
                            sending[at % 2, which, half, slot, eighth] = value[
                                eighth * tall : (eighth + 1) * tall, half * broad : (half + 1) * broad
                            ].astype(bf16)
                tile_copy(at, which).start()

    for grad, ref in ((ggate, gate_keep), (gup, up_keep)):
        for slot in range(2):
            value = dot(grad, x_own[2 * slot], (1, 0))
            for half in range(2):
                for eighth in range(2):
                    ref[half, slot, eighth] = value[
                        eighth * tall : (eighth + 1) * tall, half * broad : (half + 1) * broad
                    ].astype(bf16)
    for r in range(4):
        part = slice(r * width, (r + 1) * width)
        gnormed[:, part] += dot(ggate, gates[r], (0, 0)) + dot(gup, ups[r], (0, 0))
    total[...] += dot(hidden, downs[0], (0, 0))

    @pl.when(step == 3)
    def _():
        ffn_end(middle_ref, gain_ref, cot_ref, total, gnormed, inverse, output_ref, gmiddle_ref, branch_ref, ggain_ref)
        for at in range(4):
            for which in range(2):
                tile_copy(at, which).wait_recv()
                if at >= 2:
                    tile_copy(at, which).wait_send()
        first.wait_send()
        second.wait()
        cross.wait()


def ffn_send_call(middle, gain, cot, gates, ups, downs):
    rows, model = middle.shape
    width = gates.shape[2]
    tile = downs.shape[1]
    once = pl.Buffered(1)
    block = (tile // 2, model // 8)

    def whole(*shape, **kw):
        return pl.BlockSpec(shape, lambda s: (0,) * len(shape), **kw)

    columns = pl.BlockSpec((4, tile, width), lambda s: (0, tile_at(s), 0))
    pair = pl.BlockSpec((2, 2, 2, *block), lambda s: (0, 0, tile_at(s), 0, 0))
    grads = jax.ShapeDtypeStruct((2, 2, 8, *block), bf16)
    halves = jax.ShapeDtypeStruct((2, 8, *block), bf16)
    one = jax.ShapeDtypeStruct((8, *block), bf16)
    return pl.pallas_call(
        ffn_send_kernel,
        out_shape=[
            jax.ShapeDtypeStruct((rows, model), bf16),
            jax.ShapeDtypeStruct((rows, model), f32),
            jax.ShapeDtypeStruct((rows, model), bf16),
            jax.ShapeDtypeStruct((8, model), f32),
            grads,
            grads,
            halves,
            one,
            grads,
            grads,
            halves,
            one,
        ],
        grid=(4,),
        in_specs=[
            whole(rows, model, pipeline_mode=once),
            whole(2, model),
            whole(rows, model, pipeline_mode=once),
            columns,
            columns,
            pl.BlockSpec((1, tile, model), lambda s: (tile_at(s), 0, 0)),
        ],
        out_specs=[
            whole(rows, model, pipeline_mode=once),
            whole(rows, model, pipeline_mode=once),
            whole(rows, model, pipeline_mode=once),
            whole(8, model),
            pair,
            pair,
            whole(2, 8, *block, pipeline_mode=once),
            whole(8, *block, pipeline_mode=once),
            HBM,
            HBM,
            HBM,
            HBM,
        ],
        scratch_shapes=[
            pltpu.VMEM((rows, model), bf16),
            pltpu.VMEM((4, rows, width), bf16),
            pltpu.VMEM((model, rows), bf16),
            pltpu.VMEM((model, rows), bf16),
            pltpu.VMEM((rows, model), f32),
            pltpu.VMEM((rows, model), f32),
            pltpu.VMEM((2, 2, 2, 2, 2, *block), bf16),
            pltpu.VMEM((2, 8, *block), bf16),
            pltpu.VMEM((2, 8, *block), bf16),
            pltpu.VMEM((2, 8, *block), bf16),
            pltpu.VMEM((8, *block), bf16),
            sems(11),
            sems(11),
        ],
        compiler_params=pltpu.CompilerParams(collective_id=3, has_side_effects=True, vmem_limit_bytes=60 << 20),
    )(middle, gain, cot, gates, ups, downs)


BY_Y, BY_Z = 1, 2


class Gather:
    def __init__(self, wire, spot, shard, full, held, axis, split, chunks):
        self.wire, self.spot, self.full, self.axis, self.split = wire, spot, full, axis, split
        self.turn, self.neighbour = (spot.z % 2, spot.next) if split == BY_Z else (spot.y, spot.side)
        self.part = shard.shape[axis] // (2 if split else 1)
        self.size = self.part // chunks
        me = spot.me
        self.held, self.loaded = held, wire.keep(shard, full.at[me] if held is None else held)
        here = [self.view(shard, c, self.turn) for c in range(chunks)]
        there = [self.view(full.at[me], c, self.turn) for c in range(chunks)]
        self.cross = [wire.send(a, b, spot.chip) for a, b in zip(here, there)]
        self.near = wire.send(shard, full.at[me], spot.core)
        self.side, self.far = {}, []

    def write(self):
        self.loaded.wait()
        self.own = None if self.held is None else self.wire.keep(self.held, self.full.at[self.spot.me])

    def view(self, ref, chunk, turn):
        start = chunk * self.size + (turn * self.part if self.split else 0)
        index = [slice(None)] * 2
        index[self.axis] = pl.ds(pl.multiple_of(start, self.size), self.size)
        return ref.at[tuple(index)]

    def relay(self, chunk):
        self.cross[chunk].wait_recv()
        part = self.view(self.full.at[self.spot.across], chunk, self.turn)
        if self.split:
            self.side[chunk] = self.wire.send(part, part, self.neighbour)
        self.far.append(self.wire.send(part, part, self.spot.core))

    def relay_other(self, chunk):
        self.side[chunk].wait_recv()
        part = self.view(self.full.at[self.spot.across], chunk, 1 - self.turn)
        self.far.append(self.wire.send(part, part, self.spot.core))

    def end(self):
        if self.own is not None:
            self.own.wait()
        self.near.wait_recv()
        for copy in self.far:
            copy.wait_recv()


class StateSum:
    def __init__(self, wire, spot, places_ref, later, states, beside, outgoing, ring, result):
        self.wire, self.spot, self.states, self.beside = wire, spot, states, beside
        self.outgoing, self.ring, self.result = outgoing, ring, result
        self.sent = {}

        def place(device, block):
            return places_ref[0, 2 * device + block]

        partner = spot.own + 1 - 2 * spot.y
        sources = [place(device, block) for device in (spot.own, partner) for block in range(2)]
        self.masks = {}
        for k in range(4):
            for block in range(2):
                target = place((spot.own + 8 - 2 * k) % 8, block)
                self.masks[k, block] = [
                    jnp.where(source > target if later else source < target, 1.0, 0.0).astype(f32)
                    for source in sources
                ]

    def part(self, k, block, group):
        refs = (self.states.at[0], self.states.at[1], self.beside.at[0], self.beside.at[1])
        terms = [ref[group].astype(f32) * mask for ref, mask in zip(refs, self.masks[k, block])]
        return (terms[0] + terms[1]) + (terms[2] + terms[3])

    def trade(self):
        self.traded = self.wire.send(self.states, self.beside, self.spot.side)

    def first(self, block):
        if block == 0:
            self.traded.wait_recv()
        for group in range(self.states.shape[1]):
            self.outgoing[block, group] = self.part(1, block, group).astype(bf16)
        self.sent[0, block] = self.wire.send(self.outgoing.at[block], self.ring.at[0, block], self.spot.ahead[1])

    def hop(self, step, block):
        self.sent[step, block].wait_recv()
        target = self.result if step == 2 else self.ring.at[step]
        for group in range(self.states.shape[1]):
            value = self.ring[step, block, group].astype(f32) + self.part((step + 2) % 4, block, group)
            target[block, group] = value.astype(bf16)
        if step < 2:
            self.sent[step + 1, block] = self.wire.send(
                self.ring.at[step, block], self.ring.at[step + 1, block], self.spot.ahead[1]
            )


class StateRing:
    def __init__(self, wire, spot, places_ref, later, states, beside, outgoing, ring, result):
        self.wire, self.spot, self.states, self.beside = wire, spot, states, beside
        self.outgoing, self.ring, self.result = outgoing, ring, result
        self.sent, self.traded = {}, {}

        def place(device, block):
            return places_ref[0, 2 * device + block]

        sources = [place((spot.own + 8 - 2 * k) % 8, block) for k in range(4) for block in range(2)]
        self.masks = {}
        for beyond, device in enumerate((spot.own, spot.own + 1 - 2 * spot.y)):
            for block in range(2):
                target = place(device, block)
                self.masks[beyond, block] = [
                    jnp.where(source > target if later else source < target, 1.0, 0.0).astype(f32)
                    for source in sources
                ]

    def part(self, beyond, block, group):
        refs = [ref.at[b] for ref in (self.states, *(self.ring.at[k] for k in range(3))) for b in range(2)]
        total = None
        for ref, mask in zip(refs, self.masks[beyond, block]):
            term = ref[group].astype(f32) * mask
            total = term if total is None else total + term
        return total

    def start(self):
        for block in range(2):
            self.pass_on(0, block, self.states.at[block])

    def pass_on(self, step, block, source):
        self.sent[step, block] = self.wire.send(source, self.ring.at[step, block], self.spot.ahead[1])

    def forward(self, step, block):
        self.sent[step, block].wait_recv()
        if step < 2:
            self.pass_on(step + 1, block, self.ring.at[step, block])

    def partner(self, block):
        for group in range(self.states.shape[1]):
            self.outgoing[block, group] = self.part(1, block, group).astype(bf16)
        self.traded[block] = self.wire.send(self.outgoing.at[block], self.beside.at[block], self.spot.side)

    def finish(self, block):
        self.traded[block].wait_recv()
        for group in range(self.states.shape[1]):
            value = self.part(0, block, group) + self.beside[block, group].astype(f32)
            self.result[block, group] = value.astype(bf16)


def forward_kernel(places_ref, tokens_ref, gains_ref, *refs):
    in_shards, refs = refs[:3], refs[3:]
    weights, (gain_rows, query_ref, key_ref, value_ref, prefix_ref, atten_ref, denom_ref, middle_ref) = refs[:4], refs[4:12]
    in_out, out_out, *fulls = refs[12:17]
    refs = refs[17:]
    gains, in_full, out_full, normed, own_states, rings, outgoing, beside, numer, inner = refs[:10]
    held, (send_sems, recv_sems, local_sems) = refs[10:14], refs[14:]
    spot = Spot()
    wire = Wire(send_sems, recv_sems, local_sems)
    spot.greet([spot.core, spot.chip, spot.side, spot.ahead[1], spot.ahead[3]])
    me = spot.me
    columns, start = [], 0
    for shard in in_shards:
        columns.append(slice(start, start + shard.shape[1]))
        start += shard.shape[1]
    query_w, key_w, value_w = ins = [
        Gather(wire, spot, shard, in_full.at[:, :, at], None, 0, BY_Y, chunks)
        for shard, at, chunks in zip(in_shards, columns, (1, 1, 2))
    ]
    gain_own = wire.keep(gains_ref, gains.at[me])
    gain_near = wire.send(gains_ref, gains.at[me], spot.core)
    gain_cross = wire.send(gains_ref, gains.at[me], spot.chip)
    out_w, gate_w, up_w, down_w = weights
    half = down_w.shape[1] // 2
    left, right = slice(0, half), slice(half, 2 * half)
    out = Gather(wire, spot, out_w, out_full, None, 0, BY_Y, 1)
    gate = Gather(wire, spot, gate_w, fulls[0], held[0], 0, BY_Y, 2)
    up = Gather(wire, spot, up_w, fulls[1], held[1], 0, BY_Y, 2)
    down_left = Gather(wire, spot, down_w.at[:, left], fulls[2].at[:, :, left], held[2], 1, BY_Z, 1)
    down_right = Gather(wire, spot, down_w.at[:, right], fulls[2].at[:, :, right], held[3], 1, 0, 2)
    everything = (*ins, out, gate, up, down_left, down_right)
    kept = {}
    groups = [slice(k, k + 1) for k in range(HEADS // GROUP)]
    views = [
        [ref.at[:, at] for ref in (own_states, beside, outgoing)] + [rings.at[:, :, at], prefix_ref.at[:, at]]
        for at in groups
    ]
    sums = StateSum(wire, spot, places_ref, False, *views[0])
    ring = StateRing(wire, spot, places_ref, False, *views[1])
    intra = list(grid_views((query_ref, FDIM), (key_ref, FDIM), (value_ref, VDIM), (numer, VDIM), (inner, 1)))

    def statistics():
        residual = tokens_ref[...].astype(f32)
        inverse = lax.rsqrt(jnp.mean(residual * residual, axis=-1, keepdims=True) + EPS)
        middle_ref[...] = residual * inverse
        gain_cross.wait_recv()
        across = gains.at[spot.across]
        kept[0] = wire.send(across, across, spot.core)
        for one in everything:
            one.write()

    def project():
        gain_own.wait()
        gain_near.wait_recv()
        kept[0].wait_recv()
        for one in ins:
            one.end()
        kept[1] = wire.keep(in_full, in_out)
        width = in_full.shape[1]
        for row in range(2):
            line = jnp.concatenate([gains[k, row : row + 1, :] for k in range(4)], axis=1)
            gain_rows[row : row + 1, :] = line.astype(f32)
        normed[...] = (middle_ref[...] * gain_rows[0:1, :]).astype(bf16)
        for at, ref in zip(columns, (query_ref, key_ref, value_ref)):
            total = None
            for k in range(4):
                term = dot(normed[:, k * width : (k + 1) * width], in_full[k, :, at], (1, 0))
                total = term if total is None else total + term
            ref[...] = total.astype(bf16).T

    def states():
        for parts in grid_views((key_ref, FDIM), (value_ref, VDIM), (own_states, None)):
            states_kernel(*parts)
        sums.trade()
        ring.start()

    def inter():
        for parts in grid_views(
            (query_ref, FDIM), (prefix_ref, None), (numer, VDIM), (inner, 1), (atten_ref, VDIM), (denom_ref, 1)
        ):
            inter_kernel(*parts)

    def middle():
        out.end()
        kept[2] = wire.keep(out_full, out_out)
        total = tokens_ref[...].astype(f32)
        width = out_w.shape[0]
        for k in range(4):
            total = total + dot(atten_ref[k * width : (k + 1) * width, :], out_full[k], (0, 0))
        middle_ref[...] = total

    query_w.relay(0)
    query_w.relay_other(0)
    value_w.relay(0)
    value_w.relay(1)
    key_w.relay(0)
    statistics()
    value_w.relay_other(1)
    value_w.relay_other(0)
    out.relay(0)
    key_w.relay_other(0)
    project()
    states()
    ring.forward(0, 0)
    gate.relay(1)
    gate.relay(0)
    sums.first(0)
    ring.forward(0, 1)
    up.relay(0)
    ring.forward(1, 0)
    gate.relay_other(1)
    ring.forward(1, 1)
    sums.first(1)
    sums.hop(0, 0)
    intra_kernel(*intra[0])
    ring.forward(2, 1)
    ring.forward(2, 0)
    ring.partner(1)
    intra_kernel(*intra[1])
    sums.hop(0, 1)
    ring.partner(0)
    up.relay(1)
    sums.hop(1, 0)
    sums.hop(1, 1)
    up.relay_other(0)
    down_right.relay(0)
    intra_kernel(*intra[2])
    sums.hop(2, 0)
    ring.finish(0)
    down_left.relay(0)
    intra_kernel(*intra[3])
    sums.hop(2, 1)
    gate.relay_other(0)
    out.relay_other(0)
    ring.finish(1)
    inter()
    down_right.relay(1)
    up.relay_other(1)
    middle()
    down_left.relay_other(0)
    for one in everything[4:]:
        one.end()
    kept[1].wait()
    kept[2].wait()
    wire.end()


def grid_views(*refs):
    for block in range(2):
        for group in range(HEADS // GROUP):
            columns = slice(block * BLOCK, (block + 1) * BLOCK)
            parts = []
            for ref, rows in refs:
                if rows is None:
                    parts.append(ref.at[block : block + 1, group : group + 1])
                else:
                    parts.append(ref.at[group * GROUP * rows : (group + 1) * GROUP * rows, columns])
            yield parts


def add_chunks(total, first, other, count):
    def one(k, carry):
        total[first + k] = (total[first + k].astype(f32) + other[k].astype(f32)).astype(bf16)
        return carry

    lax.fori_loop(0, count, one, 0)


class Flow:
    def __init__(self, wire, spot, kept, sent, crossed, sided, lined, result):
        self.wire, self.spot = wire, spot
        self.kept, self.sent, self.crossed, self.sided, self.lined, self.result = kept, sent, crossed, sided, lined, result
        self.half = spot.y * 4
        self.pair = self.half + 2 * (spot.z % 2)
        self.mine = self.pair + spot.z // 2

    def cross(self):
        self.arrive = self.wire.send(self.sent, self.crossed, self.spot.chip).wait_recv

    def to_side(self):
        self.arrive()
        add_chunks(self.crossed, 0, self.kept, 8)
        there = pl.ds(4 - self.half, 4)
        self.s = self.wire.send(self.crossed.at[there], self.sided, self.spot.side)

    def to_line(self):
        self.s.wait_recv()
        add_chunks(self.crossed, self.half, self.sided, 4)
        there = pl.ds(2 * self.half + 2 - self.pair, 2)
        self.l = self.wire.send(self.crossed.at[there], self.lined.at[0:2], self.spot.next)

    def to_far(self):
        self.l.wait_recv()
        add_chunks(self.crossed, self.pair, self.lined, 2)
        self.f = self.wire.send(self.crossed.at[2 * self.pair + 1 - self.mine], self.lined.at[2], self.spot.ahead[2])

    def from_far(self):
        self.f.wait_recv()
        mine = self.mine
        self.crossed[mine] = (self.crossed[mine].astype(f32) + self.lined[2].astype(f32)).astype(bf16)
        self.own = self.wire.keep(self.crossed.at[mine], self.result.at[mine])
        self.g = self.wire.send(self.crossed.at[mine], self.result.at[mine], self.spot.ahead[2])

    def along_line(self):
        self.own.wait()
        self.g.wait_recv()
        here = self.result.at[pl.ds(self.pair, 2)]
        self.a = self.wire.send(here, here, self.spot.next)

    def along_side(self):
        self.a.wait_recv()
        here = self.result.at[pl.ds(self.half, 4)]
        self.b = self.wire.send(here, here, self.spot.side)

    def end(self):
        self.b.wait_recv()


def backward_kernel(names, *refs):
    r = SimpleNamespace(**dict(zip(names, refs)))
    spot = Spot()
    wire = Wire(r.send_sems, r.recv_sems, r.local_sems)
    me, z = spot.me, spot.z
    spot.greet([spot.core, spot.chip, spot.side, *spot.ahead[1:]])

    def load(*pairs):
        return [wire.keep(a, b) for a, b in pairs]

    def ready(copies):
        for copy in copies:
            copy.wait()

    first = load(
        (r.out_full_hbm, r.out_full),
        (r.branch_hbm, r.branch),
        (r.atten_hbm, r.atten),
        (r.denom_hbm, r.denom),
        (r.query_hbm, r.query),
    )
    arrived = load((r.first_cross, r.crossed.at[0]))
    down_loads = load((r.down_got, r.down_core), (r.down_keep, r.down_stage))
    kept, held = (r.gate_keep, r.up_keep), (r.gate_core, r.up_core)
    bases = (2, 0, 1, 3)
    stage = r.stage
    got = {weight: load((ref, held[weight])) for weight, ref in ((bases[0] // 2, (r.gate_got, r.up_got)[bases[0] // 2]),)}
    staged = {}

    def fetch(index):
        weight, half = bases[index] // 2, bases[index] % 2
        staged[index] = wire.keep(kept[weight].at[half], stage.at[index % 2])

    fetch(0)
    fetch(1)
    second = load((r.key_hbm, r.key), (r.value_hbm, r.value), (r.prefix_hbm, r.prefix))
    other = 1 - bases[0] // 2
    got[other] = load(((r.gate_got, r.up_got)[other], held[other]))
    tokens_load = load((r.tokens_hbm, r.tokens))
    third = load((r.in_full_hbm, r.in_full), (r.gmiddle_hbm, r.gmiddle))

    def base(index):
        weight, half = bases[index] // 2, bases[index] % 2
        ready(got[weight])
        got[weight] = []
        staged[index].wait()
        for slot in range(2):
            add_chunks(held[weight].at[half, slot], 0, stage.at[index % 2, slot], 8)
        if index < 2:
            fetch(index + 2)

    def down_base():
        ready(down_loads)
        for half in range(2):
            add_chunks(r.down_core.at[half], 0, r.down_stage.at[half], 8)

    def flow(index, kept_ref, sent_ref, result):
        return Flow(wire, spot, kept_ref, sent_ref, r.crossed.at[index], r.sided.at[index], r.lined.at[index], result)

    da, db = (flow(half, r.down_core.at[half], r.second_cross, r.down_out.at[half]) for half in range(2))
    da.arrive = arrived[0].wait
    ga, gb = (flow(2 + half, r.gate_core.at[half, 0], r.gate_core.at[half, 1], r.gate_out.at[half]) for half in range(2))
    ua, ub = (flow(4 + half, r.up_core.at[half, 0], r.up_core.at[half, 1], r.up_out.at[half]) for half in range(2))
    out_flow = Flow(
        wire, spot, r.out_base.at[0], r.out_base.at[1], r.out_crossed, r.out_sided, r.out_lined, r.out_out
    )
    in_flow = Flow(wire, spot, r.in_base.at[0], r.in_base.at[1], r.in_crossed, r.in_sided, r.in_lined, r.in_out)
    states, gnumer, gdenom, grad = r.states, r.gnumer, r.gdenom, r.grad
    views = [
        [ref.at[:, k : k + 1] for ref in (states, r.beside, r.outgoing)]
        + [r.ring.at[:, :, k : k + 1], r.later.at[:, k : k + 1]]
        for k in range(HEADS // GROUP)
    ]
    sums = StateSum(wire, spot, r.places, True, *views[0])
    ring = StateRing(wire, spot, r.places, True, *views[1])

    def grad_atten():
        ready(first)
        grad[...] = dot(r.out_full[...], r.branch[...], (1, 1))

    def grad_states():
        for parts in grid_views(
            (r.query, FDIM), (r.atten, VDIM), (r.denom, 1), (grad, VDIM), (gnumer, VDIM), (gdenom, 1), (states, None)
        ):
            grad_states_kernel(*parts)
        sums.trade()
        ring.start()

    core_of = me + 1 - 2 * (me % 2)
    shards = (me, spot.across, core_of, (core_of + 2) % 4)
    width = r.branch.shape[1] // 4

    def out_grads(other):
        for slot in range(2):
            rows = pl.ds(pl.multiple_of(shards[2 * other + slot] * width, width), width)
            value = dot(r.atten[rows, :], r.branch[...], (1, 0))
            ref = r.out_send if other else r.out_base
            for k in range(8):
                ref[slot, k] = value[k * 32 : (k + 1) * 32, :].astype(bf16)
        if other:
            r.out_wait = wire.send(r.out_send, r.out_core, spot.core).wait_recv

    def out_base():
        r.out_wait()
        for slot in range(2):
            add_chunks(r.out_base.at[slot], 0, r.out_core.at[slot], 8)

    narrow = HEADS * FDIM
    gproj = r.gproj
    gquery, gkey = gproj.at[0:narrow], gproj.at[narrow : 2 * narrow]
    gvalue = gproj.at[2 * narrow : 2 * narrow + HEADS * VDIM]
    intra_views = list(
        grid_views(
            (r.query, FDIM),
            (r.key, FDIM),
            (r.value, VDIM),
            (gnumer, VDIM),
            (gdenom, 1),
            (r.prefix, None),
            (gquery, FDIM),
            (r.gkey_in, FDIM),
            (grad, VDIM),
        )
    )

    def intra(index):
        if index == 0:
            ready(second)
        intra_back_kernel(*intra_views[index])

    def inverse(residual):
        return lax.rsqrt(jnp.mean(residual * residual, axis=-1, keepdims=True) + EPS)

    def normalise():
        ready(tokens_load)
        residual = r.tokens[...].astype(f32)
        r.normed[...] = (residual * inverse(residual) * r.gain_one[0:1, :]).astype(bf16)

    turned = r.turned

    def inter_back():
        for parts in grid_views(
            (r.key, FDIM),
            (r.value, VDIM),
            (r.later, None),
            (r.gkey_in, FDIM),
            (grad, VDIM),
            (gkey, FDIM),
            (gvalue, VDIM),
        ):
            inter_back_kernel(*parts)
        turned[...] = gproj[...].T

    def in_grads(other):
        for slot in range(2):
            columns = pl.ds(pl.multiple_of(shards[2 * other + slot] * width, width), width)
            value = dot(r.normed[:, columns], turned[...], (0, 0))
            ref = r.in_send if other else r.in_base
            for k in range(8):
                ref[slot, k] = value[k * 32 : (k + 1) * 32, :].astype(bf16)
        if other:
            r.in_wait = wire.send(r.in_send, r.in_core, spot.core).wait_recv

    def in_base():
        r.in_wait()
        for slot in range(2):
            add_chunks(r.in_base.at[slot], 0, r.in_core.at[slot], 8)

    gains, small, small_in, small_line = r.gains, r.small, r.small_in, r.small_line

    def tokens_grad():
        ready(third)
        gnormed = dot(turned[...], r.in_full[...], (1, 1))
        residual = r.tokens[...].astype(f32)
        inv = inverse(residual)
        gains[0:1, :] = jnp.sum(gnormed * residual * inv, axis=0, keepdims=True)
        weighted = gnormed * r.gain_one[0:1, :]
        slope = jnp.mean(weighted * residual, axis=-1, keepdims=True)
        r.gmiddle[...] += inv * weighted - residual * (inv * inv * inv) * slope
        r.written = wire.keep(r.gmiddle, r.tokens_out)

    def gain_grads():
        gains[1:2, :] = r.ggain_two[0:1, :]
        small[...] = jnp.zeros_like(small)
        for index in range(4):
            for row in range(4):
                start = pl.multiple_of(shards[index] * width + (row % 2) * 128, 128)
                small[index, row : row + 1, :] = gains[row // 2 : row // 2 + 1, pl.ds(start, 128)]
        r.small_wait = wire.send(small.at[2:4], small_in.at[0:2], spot.core).wait_recv

    def gains_cross():
        r.small_wait()
        small[0:2] = small[0:2] + small_in[0:2]
        r.small_wait = wire.send(small.at[1], small_in.at[2], spot.chip).wait_recv

    def gains_side():
        r.small_wait()
        small[0] = small[0] + small_in[2]
        r.small_wait = wire.send(small.at[0], small_in.at[3], spot.side).wait_recv

    def gains_line():
        r.small_wait()
        small_line[z] = small[0] + small_in[3]
        r.small_sent = [wire.send(small_line.at[z], small_line.at[z], spot.ahead[k]) for k in (1, 2, 3)]

    def gains_end():
        for copy in r.small_sent:
            copy.wait_recv()
        r.gains_out[...] = (small_line[0] + small_line[1]) + (small_line[2] + small_line[3])

    db.cross()
    grad_atten()
    grad_states()
    normalise()
    ring.forward(0, 0)
    down_base()
    ring.forward(0, 1)
    base(0)
    ua.cross()
    da.to_side()
    base(1)
    sums.first(0)
    out_grads(1)
    base(2)
    gb.cross()
    ring.forward(1, 1)
    intra(0)
    out_grads(0)
    base(3)
    da.to_line()
    db.to_side()
    ring.forward(1, 0)
    ua.to_side()
    sums.first(1)
    da.to_far()
    intra(1)
    ring.forward(2, 0)
    db.to_line()
    ua.to_line()
    ring.forward(2, 1)
    da.from_far()
    ring.partner(0)
    ring.partner(1)
    ga.cross()
    intra(2)
    sums.hop(0, 0)
    ring.finish(0)
    da.along_line()
    db.to_far()
    out_base()
    ua.to_far()
    out_flow.cross()
    gb.to_side()
    sums.hop(0, 1)
    da.along_side()
    sums.hop(1, 0)
    sums.hop(1, 1)
    intra(3)
    ring.finish(1)
    ga.to_side()
    db.from_far()
    ub.cross()
    gb.to_line()
    sums.hop(2, 0)
    sums.hop(2, 1)
    out_flow.to_side()
    db.along_line()
    ua.from_far()
    inter_back()
    in_grads(1)
    db.along_side()
    out_flow.to_line()
    gb.to_far()
    in_grads(0)
    in_base()
    in_flow.cross()
    out_flow.to_far()
    ua.along_line()
    ub.to_side()
    out_flow.from_far()
    gb.from_far()
    ua.along_side()
    ga.to_line()
    out_flow.along_line()
    tokens_grad()
    ga.to_far()
    ub.to_line()
    out_flow.along_side()
    gb.along_line()
    gain_grads()
    gains_cross()
    in_flow.to_side()
    ga.from_far()
    ub.to_far()
    da.end()
    out_flow.end()
    ga.along_line()
    gb.along_side()
    gains_side()
    ua.end()
    db.end()
    in_flow.to_line()
    ga.along_side()
    ub.from_far()
    in_flow.to_far()
    ub.along_line()
    gb.end()
    in_flow.from_far()
    ub.along_side()
    gains_line()
    in_flow.along_line()
    in_flow.along_side()
    gains_end()
    ga.end()
    ub.end()
    in_flow.end()
    r.written.wait()
    wire.end()


HBM = pl.BlockSpec(memory_space=pltpu.HBM)
VMEM = pl.BlockSpec(memory_space=pltpu.VMEM)
SMEM = pl.BlockSpec(memory_space=pltpu.SMEM)


def sems(count):
    return pltpu.SemaphoreType.DMA((count,))


def forward_call(places, tokens, gains, in_shards, weights):
    rows, model = tokens.shape
    narrow, wide = HEADS * FDIM, HEADS * VDIM
    state = (rows // BLOCK, HEADS // GROUP, STATE, 128)
    in_full = (4, in_shards[0].shape[0], sum(a.shape[1] for a in in_shards))
    tall, model_half = weights[3].shape[0], weights[3].shape[1] // 2

    def low(*shape):
        return jax.ShapeDtypeStruct(shape, bf16)

    return pl.pallas_call(
        forward_kernel,
        out_shape=[
            jax.ShapeDtypeStruct((2, model), f32),
            low(narrow, rows),
            low(narrow, rows),
            low(wide, rows),
            low(*state),
            low(wide, rows),
            jax.ShapeDtypeStruct((HEADS, rows), f32),
            jax.ShapeDtypeStruct((rows, model), f32),
            low(*in_full),
        ]
        + [low(4, *w.shape) for w in weights],
        in_specs=[SMEM, VMEM] + [HBM] * 8,
        out_specs=[VMEM] * 8 + [HBM] * 5,
        scratch_shapes=[
            pltpu.VMEM((4, *gains.shape), bf16),
            pltpu.VMEM(in_full, bf16),
            pltpu.VMEM((4, *weights[0].shape), bf16),
            pltpu.VMEM((rows, model), bf16),
            pltpu.VMEM(state, bf16),
            pltpu.VMEM((3, *state), bf16),
            pltpu.VMEM(state, bf16),
            pltpu.VMEM(state, bf16),
            pltpu.VMEM((wide, rows), f32),
            pltpu.VMEM((HEADS, rows), f32),
            *(pltpu.VMEM(w.shape, bf16) for w in weights[1:3]),
            *[pltpu.VMEM((tall, model_half), bf16)] * 2,
            sems(72),
            sems(72),
            sems(28),
        ],
        compiler_params=pltpu.CompilerParams(collective_id=1, has_side_effects=True, vmem_limit_bytes=58 << 20),
    )(places, tokens, gains, *in_shards, *weights)


def settle_kernel(down_ref, gate_ref, up_ref, out_ref, in_ref, output_ref, tokens_ref, *outs):
    tall, broad = down_ref.shape[2:]
    down_out, gate_out, up_out, out_out = outs[:4]
    for half in range(2):
        down_out[half * tall : (half + 1) * tall, :] = down_ref[half, 0].astype(f32)
        gate_out[:, half * broad : (half + 1) * broad] = gate_ref[half, 0].astype(f32)
        up_out[:, half * broad : (half + 1) * broad] = up_ref[half, 0].astype(f32)
    out_out[...] = out_ref[0].astype(f32)
    start = 0
    for out in outs[4:7]:
        stop = start + out.shape[1]
        out[...] = in_ref[0, :, start:stop].astype(f32)
        start = stop
    outs[7][...] = output_ref[...]
    outs[8][...] = tokens_ref[...]


def settle_call(down, gate, up, out, ins, output, tokens):
    tall, broad = down.shape[2:]
    size, model = out.shape[1:]
    narrow = HEADS * FDIM
    rows = output.shape[0]
    blocks = pl.BlockSpec((2, 1, tall, broad), lambda k: (0, k, 0, 0))

    def line(height, width):
        return pl.BlockSpec((height, width), lambda k: (k, 0))

    def eighths(a):
        return pl.BlockSpec((1, *a.shape[1:]), lambda k: (k, 0, 0))

    shapes = [(2 * tall, 8 * broad), (8 * tall, 2 * broad), (8 * tall, 2 * broad), (8 * size, model)]
    widths = (narrow, narrow, ins.shape[2] - 2 * narrow)
    shapes += [(8 * size, width) for width in widths]
    whole = [line(rows // 8, model)] * 2
    return pl.pallas_call(
        settle_kernel,
        out_shape=[jax.ShapeDtypeStruct(shape, f32) for shape in shapes]
        + [jax.ShapeDtypeStruct(a.shape, a.dtype) for a in (output, tokens)],
        grid=(8,),
        in_specs=[blocks, blocks, blocks, eighths(out), eighths(ins), *whole],
        out_specs=[
            pl.BlockSpec((2 * tall, broad), lambda k: (0, k)),
            line(tall, 2 * broad),
            line(tall, 2 * broad),
            line(size, model),
            *(line(size, width) for width in widths),
            *whole,
        ],
        compiler_params=pltpu.CompilerParams(vmem_limit_bytes=60 << 20),
    )(down, gate, up, out, ins, output, tokens)


def masked_sums(pieces, masks, dtype):
    total = None
    for index, piece in enumerate(pieces):
        for block in range(piece.shape[0]):
            term = masks[:, index, block][:, None, None, None] * piece[block].astype(f32)[None]
            total = term if total is None else total + term
    return total.astype(dtype)


class Exchange:
    def __init__(self, states, positions, own, count, later):
        self.pieces, self.sources, self.own, self.count, self.later = [states], [own], own, count, later
        self.table = positions.reshape(count, states.shape[0])

    def mask(self, target):
        there = self.table[target][:, None, None]
        here = self.table[jnp.stack(self.sources)][None]
        return ((here > there) if self.later else (here < there)).astype(f32)

    def ring(self):
        return self.pieces[-1], "ctx", [(i, (i + 2) % self.count) for i in range(self.count)]

    def passed(self, piece):
        self.sources.append((self.own - 2 * len(self.pieces)) % self.count)
        self.pieces.append(piece)

    def partner(self):
        return trade(masked_sums(self.pieces, self.mask(self.own ^ 1), bf16), 1, self.count)

    def total(self, received):
        return (masked_sums(self.pieces, self.mask(self.own), f32) + received.astype(f32)).astype(bf16)


def backward_call(arrays):
    names, specs, values = [], [], []
    get = SimpleNamespace(**arrays)
    for name, array in arrays.items():
        names.append(name)
        values.append(array)
        specs.append(SMEM if array.dtype == jnp.int32 else VMEM if array.shape[0] <= 8 and array.dtype == f32 else HBM)
    rows, model = get.tokens_hbm.shape
    columns = get.in_full_hbm.shape[1]
    block = get.down_keep.shape[2:]
    narrow, wide = HEADS * FDIM, HEADS * VDIM
    state = get.prefix_hbm.shape
    outs = dict(
        tokens_out=((rows, model), f32, HBM),
        down_out=((2, 8, *block), bf16, HBM),
        gate_out=((2, 8, *block), bf16, HBM),
        up_out=((2, 8, *block), bf16, HBM),
        out_out=((8, 32, model), bf16, HBM),
        in_out=((8, 32, columns), bf16, HBM),
        gains_out=((8, 128), f32, VMEM),
    )
    scratch = dict(
        down_core=((2, 8, *block), bf16),
        down_stage=((2, 8, *block), bf16),
        gate_core=((2, 2, 8, *block), bf16),
        up_core=((2, 2, 8, *block), bf16),
        stage=((2, 2, 8, *block), bf16),
        crossed=((6, 8, *block), bf16),
        sided=((6, 4, *block), bf16),
        lined=((6, 3, *block), bf16),
        out_full=((wide, model), bf16),
        branch=((rows, model), bf16),
        atten=((wide, rows), bf16),
        denom=((HEADS, rows), f32),
        query=((narrow, rows), bf16),
        key=((narrow, rows), bf16),
        value=((wide, rows), bf16),
        prefix=(state, bf16),
        tokens=((rows, model), bf16),
        in_full=((model, columns), bf16),
        gmiddle=((rows, model), f32),
        grad=((wide, rows), f32),
        gnumer=((wide, rows), bf16),
        gdenom=((HEADS, rows), f32),
        states=(state, bf16),
        ring=((3, *state), bf16),
        outgoing=(state, bf16),
        beside=(state, bf16),
        later=(state, bf16),
        gproj=((columns, rows), bf16),
        gkey_in=((narrow, rows), f32),
        normed=((rows, model), bf16),
        turned=((rows, columns), bf16),
        gains=((8, model), f32),
        small=((4, 8, 128), f32),
        small_in=((4, 8, 128), f32),
        small_line=((4, 8, 128), f32),
        out_base=((2, 8, 32, model), bf16),
        out_send=((2, 8, 32, model), bf16),
        out_core=((2, 8, 32, model), bf16),
        out_crossed=((8, 32, model), bf16),
        out_sided=((4, 32, model), bf16),
        out_lined=((3, 32, model), bf16),
        in_base=((2, 8, 32, columns), bf16),
        in_send=((2, 8, 32, columns), bf16),
        in_core=((2, 8, 32, columns), bf16),
        in_crossed=((8, 32, columns), bf16),
        in_sided=((4, 32, columns), bf16),
        in_lined=((3, 32, columns), bf16),
    )
    names += [*outs, *scratch, *dict(send_sems=0, recv_sems=0, local_sems=0)]
    return pl.pallas_call(
        functools.partial(backward_kernel, tuple(names)),
        out_shape=[jax.ShapeDtypeStruct(shape, dtype) for shape, dtype, _ in outs.values()],
        in_specs=specs,
        out_specs=[spec for _, _, spec in outs.values()],
        scratch_shapes=[pltpu.VMEM(shape, dtype) for shape, dtype in scratch.values()]
        + [sems(100), sems(100), sems(48)],
        compiler_params=pltpu.CompilerParams(collective_id=2, has_side_effects=True, vmem_limit_bytes=60 << 20),
    )(*values)


def body(count):
    def layer(
        tokens, block_pos, gain_attn, w_query, w_key, w_value, w_out, gain_ffn, w_gate, w_up, w_down, cotangent
    ):
        own = lax.axis_index("ctx")
        me = lax.axis_index("fsdp").astype(jnp.int32).reshape(1)
        positions = block_pos[0]
        in_shards = (w_query, w_key, w_value)
        gains = jnp.stack([gain_attn, gain_ffn])
        weights = (w_out, w_gate.T, w_up.T, w_down)
        narrow = HEADS * FDIM
        rows = tokens.shape[1]
        unit = 2 * rows * BLOCK * HEADS
        width = sum(a.shape[1] for a in in_shards)
        if count == 8:
            forward = forward_call(block_pos, tokens[0], gains, in_shards, weights)
            gains, query, key, value, prefix, atten, denom, middle, in_full, out_full, gates, ups, downs = forward
        else:
            in_shard = jnp.concatenate(in_shards, axis=1)
            gains, in_full = (lax.all_gather(a, "fsdp", axis=k, tiled=True) for k, a in ((1, gains), (0, in_shard)))
            gains = gains.astype(f32)
        gain_one, gain_two = gains[0], gains[1]
        in_full = in_full.reshape(-1, width)
        if count == 8:
            out_full = out_full.reshape(-1, w_out.shape[1])
        else:
            residual = tokens[0].astype(f32)
            inv_one = lax.rsqrt(jnp.mean(residual * residual, axis=-1, keepdims=True) + EPS)
            normed_one = (residual * inv_one * gain_one).astype(bf16)
            projected = dot(in_full, normed_one, (0, 1)).astype(bf16)
            query, key, value = projected[:narrow], projected[narrow : 2 * narrow], projected[2 * narrow :]
            (own_states,) = attention_call(
                states_kernel, ("narrow", "wide"), (("state", bf16),), rows, unit * FEAT
            )(key, value)
            numer, denom = attention_call(
                intra_kernel, ("narrow", "narrow", "wide"), (("wide", f32), ("head", f32)), rows, unit * 256
            )(query, key, value)
            links = Links()
            states = Exchange(own_states, positions, own, count, False)
            for _ in range(1, count // 2):
                states.passed(links.round([states.ring()])[0])
            prefix = states.total(links.round([states.partner()])[0])
            atten, denom = attention_call(
                inter_kernel,
                ("narrow", "state", "wide", "head"),
                (("wide", bf16), ("head", f32)),
                rows,
                unit * FEAT,
            )(query, prefix, numer, denom)
            out_full, gates, ups, downs = (lax.all_gather(w, "fsdp") for w in weights)
            out_full = out_full.reshape(-1, w_out.shape[1])
            middle = residual + dot(atten, out_full, (0, 0))
        ffn_inputs = (middle, gains, cotangent[0], gates, ups, downs)
        if count == 8:
            results = ffn_send_call(*ffn_inputs)
            output, grad_middle, branch, grad_gain_two = results[:4]
            gate_keep, up_keep, down_keep, second_cross, gate_got, up_got, down_got, first_cross = results[4:]
            arrays = dict(
                places=block_pos,
                gain_one=gains,
                ggain_two=grad_gain_two,
                out_full_hbm=out_full,
                branch_hbm=branch,
                atten_hbm=atten,
                denom_hbm=denom,
                query_hbm=query,
                key_hbm=key,
                value_hbm=value,
                prefix_hbm=prefix,
                tokens_hbm=tokens[0],
                in_full_hbm=in_full,
                gmiddle_hbm=grad_middle,
                down_keep=down_keep,
                down_got=down_got,
                first_cross=first_cross,
                second_cross=second_cross,
                gate_keep=gate_keep,
                gate_got=gate_got,
                up_keep=up_keep,
                up_got=up_got,
            )
            grad_tokens, down_sum, gate_sum, up_sum, out_sum, in_sum, small = backward_call(arrays)
            gain_sums = small[:4].reshape(2, -1)
        else:
            results = ffn_call(me, *ffn_inputs)
            output, grad_middle, branch, grad_gain_two = results[:4]
            pairs = [results[k : k + 2] for k in (8, 4, 6)]
            grad_atten = dot(out_full, branch, (1, 1))
            gnumer, gdenom, grad_states = attention_call(
                grad_states_kernel,
                ("narrow", "wide", "head", "wide"),
                (("wide", bf16), ("head", f32), ("state", bf16)),
                rows,
                unit * FEAT,
            )(query, atten, denom, grad_atten)
            gquery, gkey, gvalue = attention_call(
                intra_back_kernel,
                ("narrow", "narrow", "wide", "wide", "head", "state"),
                (("narrow", bf16), ("narrow", f32), ("wide", f32)),
                rows,
                unit * 512,
            )(query, key, value, gnumer, gdenom, prefix)
            links = Links()
            backward = Exchange(grad_states, positions, own, count, True)
            for _ in range(1, count // 2):
                backward.passed(links.round([backward.ring()])[0])
            later = backward.total(links.round([backward.partner()])[0])
            gkey, gvalue = attention_call(
                inter_back_kernel,
                ("narrow", "wide", "state", "narrow", "wide"),
                (("narrow", bf16), ("wide", bf16)),
                rows,
                unit * 256,
            )(key, value, later, gkey, gvalue)
            gprojected = jnp.concatenate([gquery, gkey, gvalue], axis=0)
            gnormed_one = dot(gprojected, in_full, (0, 1))
            weighted_one = gnormed_one * gain_one
            grad_gain_one = jnp.sum(gnormed_one * residual * inv_one, axis=0)
            grad_tokens = (
                grad_middle
                + inv_one * weighted_one
                - residual
                * (inv_one * inv_one * inv_one)
                * jnp.mean(weighted_one * residual, axis=-1, keepdims=True)
            )

            def summed(keep, send):
                got = lax.ppermute(send, "fsdp", CORE)
                cross = (keep[:, 1].astype(f32) + got[:, 1].astype(f32)).astype(bf16)
                got_cross = lax.ppermute(cross, "fsdp", CHIP)
                total = keep[:, 0].astype(f32) + got[:, 0].astype(f32) + got_cross.astype(f32)
                return lax.psum(total.astype(bf16), "ctx")

            def scattered(grad):
                return lax.psum(lax.psum_scatter(grad, "fsdp", scatter_dimension=0, tiled=True), "ctx")

            down_sum, gate_sum, up_sum = (summed(*pair) for pair in pairs)
            out_sum = scattered(dot(atten, branch, (1, 0)).astype(bf16)).reshape(8, -1, branch.shape[1])
            in_sum = scattered(dot(normed_one, gprojected, (0, 1)).astype(bf16)).reshape(8, -1, width)
            gain_sums = scattered(jnp.stack([grad_gain_one, grad_gain_two[0]], axis=1)).T
        down_grad, gate_grad, up_grad, out_grad, *in_grads, output, grad_tokens = settle_call(
            down_sum, gate_sum, up_sum, out_sum, in_sum, output, grad_tokens
        )
        return (
            output[None],
            grad_tokens[None],
            gain_sums[0],
            *in_grads,
            out_grad,
            gain_sums[1],
            gate_grad.T,
            up_grad.T,
            down_grad,
        )

    return layer


def solution(mesh):
    rows = P("fsdp", None)
    seqs = P("fsdp", "ctx", None)
    vec = P("fsdp")
    in_specs = (seqs, rows, vec, rows, rows, rows, rows, vec, rows, rows, rows, seqs)
    out_specs = (seqs, seqs, vec, rows, rows, rows, rows, vec, rows, rows, rows)
    return jax.shard_map(
        body(mesh.shape["ctx"]), mesh=mesh, in_specs=in_specs, out_specs=out_specs, check_vma=False
    )
```

```python
import functools
from types import SimpleNamespace

import jax
import jax.numpy as jnp
from jax import lax
from jax.experimental import pallas as pl
from jax.experimental.pallas import tpu as pltpu
from jax.sharding import PartitionSpec as P

HEADS = 16
FDIM = 16
VDIM = 64
BLOCK = 256
GROUP = 8
FEAT = 160
STATE = GROUP // 2 * FEAT + 2 * GROUP
EPS = 1e-05
ROOT_HALF = 0.7071067811865476

f32 = jnp.float32
bf16 = jnp.bfloat16


def dims(lhs, rhs):
    return (((lhs,), (rhs,)), ((), ()))


def dot(lhs, rhs, contract):
    return lax.dot_general(lhs, rhs, dims(*contract), preferred_element_type=f32)


def turned(u, shift):
    return pltpu.roll(u, FDIM - shift, 0)


def features(u, pair_weight):
    rows = [u, u * u * ROOT_HALF]
    for shift in range(1, 8):
        rows.append(u * turned(u, shift) * ROOT_HALF)
    rows.append(u[:8] * u[8:] * ROOT_HALF)
    one = (lax.broadcasted_iota(jnp.int32, (8, u.shape[1]), 0) == 0).astype(f32)
    linear = jnp.concatenate(rows[:2], axis=0).astype(bf16)
    pairs = jnp.concatenate(rows[2:], axis=0).astype(bf16) * pair_weight
    del rows
    return jnp.concatenate([linear.astype(f32), pairs.astype(f32), one], axis=0).astype(bf16)


def features_back(u, g):
    total = g[:16] + (2.0 * ROOT_HALF) * (g[16:32] * u)
    for shift in range(1, 8):
        here = (2.0 * ROOT_HALF) * g[16 + 16 * shift : 32 + 16 * shift]
        total = total + here * turned(u, shift) + pltpu.roll(here * u, shift, 0)
    here = (2.0 * ROOT_HALF) * g[144:152]
    return total + jnp.concatenate([here * u[8:], here * u[:8]], axis=0)


def halved(ref, head):
    return ref[head * FDIM : (head + 1) * FDIM, :].astype(f32) * 0.5


def write_states(out_ref, feat, value_pair, weight_row, head):
    pair = head // 2
    product = dot(feat, value_pair, (1, 1))
    half = slice(0, 64) if head % 2 == 0 else slice(64, 128)
    out_ref[0, 0, pair * FEAT : (pair + 1) * FEAT, half] = product[:, half].astype(bf16)
    norm = dot(weight_row, feat, (1, 1))
    base = GROUP // 2 * FEAT + 2 * head
    out_ref[0, 0, base : base + 1, :] = norm[:1, :128].astype(bf16)
    out_ref[0, 0, base + 1 : base + 2, :] = jnp.concatenate([norm[:1, 128:], jnp.zeros((1, 96), f32)], axis=1).astype(bf16)


def norm_row(state_ref, head):
    base = GROUP // 2 * FEAT + 2 * head
    return state_ref[0, 0, base : base + 1, :], state_ref[0, 0, base + 1 : base + 2, :32]


def head_state(state_ref, head):
    pair = head // 2
    return state_ref[0, 0, pair * FEAT : (pair + 1) * FEAT, 64 * (head % 2) : 64 * (head % 2) + 64]


def states_kernel(key_ref, value_ref, out_ref):
    ones = jnp.ones((8, BLOCK), bf16)
    for head in range(GROUP):
        feat = features(halved(key_ref, head), 1.0)
        pair = head // 2
        write_states(out_ref, feat, value_ref[pair * 128 : (pair + 1) * 128, :], ones, head)


def intra_kernel(query_ref, key_ref, value_ref, numer_ref, denom_ref):
    for head in range(GROUP):
        rows = slice(head * FDIM, (head + 1) * FDIM)
        wide = slice(head * VDIM, (head + 1) * VDIM)
        scores = dot(key_ref[rows, :], query_ref[rows, :], (0, 0)) * 0.25
        kernel = 1.0 + scores + 0.5 * scores * scores
        denom_ref[head : head + 1, :] = jnp.sum(kernel, axis=0, keepdims=True)
        numer_ref[wide, :] = dot(value_ref[wide, :], kernel.astype(bf16), (1, 0))


def inter_kernel(query_ref, prefix_ref, numer_ref, denom_in_ref, atten_ref, denom_ref):
    for head in range(GROUP):
        wide = slice(head * VDIM, (head + 1) * VDIM)
        feat = features(halved(query_ref, head), 2.0)
        numer = numer_ref[wide, :] + dot(head_state(prefix_ref, head), feat, (0, 0))
        first, second = norm_row(prefix_ref, head)
        denom = denom_in_ref[head : head + 1, :] + dot(first, feat[:128], (1, 0)) + dot(second, feat[128:], (1, 0))
        denom_ref[head : head + 1, :] = denom
        atten_ref[wide, :] = (numer / denom).astype(bf16)


def grad_states_kernel(query_ref, atten_ref, denom_ref, grad_ref, gnumer_ref, gdenom_ref, out_ref):
    for pair in range(GROUP // 2):
        for head in (2 * pair, 2 * pair + 1):
            wide = slice(head * VDIM, (head + 1) * VDIM)
            denom = denom_ref[head : head + 1, :]
            grad = grad_ref[wide, :]
            gnumer_ref[wide, :] = (grad / denom).astype(bf16)
            gdenom = -jnp.sum(grad * atten_ref[wide, :].astype(f32), axis=0, keepdims=True) / denom
            gdenom_ref[head : head + 1, :] = gdenom.astype(bf16).astype(f32)
        for head in (2 * pair, 2 * pair + 1):
            feat = features(halved(query_ref, head), 1.0)
            weights = jnp.broadcast_to(gdenom_ref[head : head + 1, :], (8, BLOCK)).astype(bf16)
            write_states(out_ref, feat, gnumer_ref[pair * 128 : (pair + 1) * 128, :], weights, head)


def intra_back_kernel(
    query_ref, key_ref, value_ref, gnumer_ref, gdenom_ref, prefix_ref, gquery_ref, gkey_ref, gvalue_ref
):
    for head in range(GROUP):
        rows = slice(head * FDIM, (head + 1) * FDIM)
        wide = slice(head * VDIM, (head + 1) * VDIM)
        query, key = query_ref[rows, :], key_ref[rows, :]
        gnumer = gnumer_ref[wide, :]
        gdenom = gdenom_ref[head : head + 1, :]
        scores = dot(key, query, (0, 0)) * 0.25
        kernel = (1.0 + scores + 0.5 * scores * scores).astype(bf16)
        gkernel = dot(value_ref[wide, :], gnumer, (0, 0)) + gdenom
        gscores = ((1.0 + scores) * gkernel).astype(bf16)
        gvalue_ref[wide, :] = dot(gnumer, kernel, (1, 1))
        gkey_ref[rows, :] = dot(query, gscores, (1, 1)) * 0.25
        first, second = norm_row(prefix_ref, head)
        gdenom_low = gdenom.astype(bf16)
        outer_prod = jnp.concatenate([dot(first, gdenom_low, (0, 0)), dot(second, gdenom_low, (0, 0))], axis=0)
        gfeat = dot(head_state(prefix_ref, head), gnumer, (1, 0)) + outer_prod
        gquery = dot(key, gscores, (1, 0)) * 0.25 + 0.5 * features_back(halved(query_ref, head), gfeat)
        gquery_ref[rows, :] = gquery.astype(bf16)


def inter_back_kernel(key_ref, value_ref, later_ref, gkey_in_ref, gvalue_in_ref, gkey_ref, gvalue_ref):
    ones = jnp.ones((1, BLOCK), bf16)
    for head in range(GROUP):
        rows = slice(head * FDIM, (head + 1) * FDIM)
        wide = slice(head * VDIM, (head + 1) * VDIM)
        u = halved(key_ref, head)
        state = head_state(later_ref, head)
        first, second = norm_row(later_ref, head)
        outer_prod = jnp.concatenate([dot(first, ones, (0, 0)), dot(second, ones, (0, 0))], axis=0)
        gfeat = dot(state, value_ref[wide, :], (1, 0)) + outer_prod
        gkey_ref[rows, :] = (gkey_in_ref[rows, :] + 0.5 * features_back(u, gfeat)).astype(bf16)
        feat = features(u, 2.0)
        gvalue_ref[wide, :] = (gvalue_in_ref[wide, :] + dot(state, feat, (0, 0))).astype(bf16)


def attention_call(kernel, ins, outs, tokens, flops):
    blocks = tokens // BLOCK
    groups = HEADS // GROUP
    forms = {
        "narrow": ((GROUP * FDIM, BLOCK), lambda b, g: (g, b), (HEADS * FDIM, tokens)),
        "wide": ((GROUP * VDIM, BLOCK), lambda b, g: (g, b), (HEADS * VDIM, tokens)),
        "head": ((GROUP, BLOCK), lambda b, g: (g, b), (HEADS, tokens)),
        "state": ((1, 1, STATE, 128), lambda b, g: (b, g, 0, 0), (blocks, groups, STATE, 128)),
    }

    def spec(name):
        return pl.BlockSpec(forms[name][0], forms[name][1])

    def call(*arrays):
        moved = sum(a.size * a.dtype.itemsize for a in arrays)
        return pl.pallas_call(
            kernel,
            out_shape=[jax.ShapeDtypeStruct(forms[name][2], dtype) for name, dtype in outs],
            grid=(blocks, groups),
            in_specs=[spec(name) for name in ins],
            out_specs=[spec(name) for name, _ in outs],
            compiler_params=pltpu.CompilerParams(vmem_limit_bytes=40 << 20),
            cost_estimate=pl.CostEstimate(flops=flops, bytes_accessed=2 * moved, transcendentals=0),
        )(*arrays)

    return call


ORDER = (0, 2, 1, 3)


def place(step):
    return (step % 2) * 2 + step // 2


def ffn_begin(me, middle_ref, gain_ref, cot_ref, normed, x_own, x_turned, cot_turned, total, gnormed, inverse):
    width = x_own.shape[2]
    core = me + 1 - 2 * (me % 2)
    normed[...] = (middle_ref[...] * inverse() * gain_ref[1:2, :]).astype(bf16)
    for r, shard in enumerate((me, core, (me + 2) % 4, (core + 2) % 4)):
        x_own[r] = normed[:, pl.ds(pl.multiple_of(shard * width, width), width)]
    x_turned[...] = normed[...].T
    cot_turned[...] = cot_ref[...].T
    total[...] = jnp.zeros_like(total)
    gnormed[...] = jnp.zeros_like(gnormed)


def ffn_tile(gates, ups, down, x_turned, cot_turned):
    gate = dot(gates[...], x_turned[...], (1, 0))
    up = dot(ups[...], x_turned[...], (1, 0))
    ghidden = dot(down, cot_turned[...], (1, 0))
    sigmoid = jax.nn.sigmoid(gate)
    silu = gate * sigmoid
    hidden = (silu * up).astype(bf16)
    ggate = (ghidden * up * (sigmoid * (1.0 + gate * (1.0 - sigmoid)))).astype(bf16)
    return hidden, ggate, (ghidden * silu).astype(bf16)


def ffn_end(middle_ref, gain_ref, cot_ref, total, gnormed, inverse, output_ref, gmiddle_ref, branch_ref, ggain_ref):
    middle, inv, cot = middle_ref[...], inverse(), cot_ref[...].astype(f32)
    grad = gnormed[...]
    output_ref[...] = (middle + total[...]).astype(bf16)
    ggain_ref[...] = jnp.broadcast_to(jnp.sum(grad * middle * inv, axis=0, keepdims=True), ggain_ref.shape)
    weighted = grad * gain_ref[1:2, :]
    slope = jnp.mean(weighted * middle, axis=-1, keepdims=True)
    gmiddle = cot + inv * weighted - middle * (inv * inv * inv) * slope
    gmiddle_ref[...] = gmiddle
    branch_ref[...] = gmiddle.astype(bf16)


def ffn_kernel(me_ref, middle_ref, gain_ref, cot_ref, gates, ups, downs, *refs):
    output_ref, gmiddle_ref, branch_ref, ggain_ref = refs[:4]
    gate_keep, gate_send, up_keep, up_send, down_keep, down_send = refs[4:10]
    normed, x_own, x_turned, cot_turned, total, gnormed = refs[10:]
    step = pl.program_id(0)

    def inverse():
        middle = middle_ref[...]
        return lax.rsqrt(jnp.mean(middle * middle, axis=-1, keepdims=True) + EPS)

    @pl.when(step == 0)
    def _():
        ffn_begin(
            me_ref[0], middle_ref, gain_ref, cot_ref, normed, x_own, x_turned, cot_turned, total, gnormed, inverse
        )

    hidden, ggate, gup = ffn_tile(gates, ups, downs[0], x_turned, cot_turned)
    down = downs[0]
    total[...] += dot(hidden, down, (0, 0))
    gdown = dot(hidden, cot_ref[...], (1, 0))
    tall, broad = down_keep.shape[3:]

    def store(ref, slot, grad):
        for half in range(2):
            for eighth in range(8):
                ref[half, slot, eighth] = grad[
                    half * tall : (half + 1) * tall, eighth * broad : (eighth + 1) * broad
                ].astype(bf16)

    @pl.when(step < 2)
    def _():
        store(down_keep, 0, gdown)

    @pl.when(step >= 2)
    def _():
        store(down_send, 0, gdown)

    def store_turned(keep, send, r, grad):
        ref = send if r % 2 else keep
        for half in range(2):
            for eighth in range(2):
                ref[half, r // 2, eighth] = grad[
                    eighth * tall : (eighth + 1) * tall, half * broad : (half + 1) * broad
                ].astype(bf16)

    gnormed[...] += dot(ggate, gates[...], (0, 0)) + dot(gup, ups[...], (0, 0))
    for r in range(4):
        store_turned(gate_keep, gate_send, r, dot(ggate, x_own[r], (1, 0)))
        store_turned(up_keep, up_send, r, dot(gup, x_own[r], (1, 0)))

    @pl.when(step == 3)
    def _():
        ffn_end(middle_ref, gain_ref, cot_ref, total, gnormed, inverse, output_ref, gmiddle_ref, branch_ref, ggain_ref)


def ffn_call(me, middle, gain, cot, gates, ups, downs):
    rows, model = middle.shape
    hidden = gates.shape[0]
    width = model // 4
    tile = downs.shape[1]
    once = pl.Buffered(1)

    def whole(shape, **kw):
        return pl.BlockSpec(shape, lambda s, me: (0,) * len(shape), **kw)

    columns = pl.BlockSpec((tile, model), lambda s, me: (me[0] ^ place(s), 0))
    block = (tile // 2, model // 8)
    pair = pl.BlockSpec((2, 2, 2, *block), lambda s, me: (0, 0, me[0] ^ place(s), 0, 0))
    grads = jax.ShapeDtypeStruct((2, 2, 8, *block), bf16)
    return pl.pallas_call(
        ffn_kernel,
        out_shape=[
            jax.ShapeDtypeStruct((rows, model), bf16),
            jax.ShapeDtypeStruct((rows, model), f32),
            jax.ShapeDtypeStruct((rows, model), bf16),
            jax.ShapeDtypeStruct((8, model), f32),
            grads,
            grads,
            grads,
            grads,
            grads,
            grads,
        ],
        grid_spec=pltpu.PrefetchScalarGridSpec(
            num_scalar_prefetch=1,
            grid=(4,),
            in_specs=[
                whole((rows, model), pipeline_mode=once),
                whole((2, model)),
                whole((rows, model), pipeline_mode=once),
                columns,
                columns,
                pl.BlockSpec((1, tile, model), lambda s, me: (me[0] ^ place(s), 0, 0)),
            ],
            out_specs=[
                whole((rows, model), pipeline_mode=once),
                whole((rows, model), pipeline_mode=once),
                whole((rows, model), pipeline_mode=once),
                whole((8, model)),
                pair,
                pair,
                pair,
                pair,
                pl.BlockSpec((2, 1, 8, *block), lambda s, me: (0, jnp.minimum(s, 1), 0, 0, 0)),
                pl.BlockSpec((2, 1, 8, *block), lambda s, me: (0, jnp.maximum(s - 2, 0), 0, 0, 0)),
            ],
            scratch_shapes=[
                pltpu.VMEM((rows, model), bf16),
                pltpu.VMEM((4, rows, width), bf16),
                pltpu.VMEM((model, rows), bf16),
                pltpu.VMEM((model, rows), bf16),
                pltpu.VMEM((rows, model), f32),
                pltpu.VMEM((rows, model), f32),
            ],
        ),
        compiler_params=pltpu.CompilerParams(vmem_limit_bytes=58 << 20),
        cost_estimate=pl.CostEstimate(
            flops=18 * rows * model * hidden, bytes_accessed=14 * hidden * model, transcendentals=0
        ),
    )(me, middle, gain, cot, gates, ups, downs)


CORE = [(0, 1), (1, 0), (2, 3), (3, 2)]
CHIP = [(0, 2), (2, 0), (1, 3), (3, 1)]


class Links:
    def __init__(self):
        self.last = ()

    def round(self, sends, beside=()):
        arrays = [send[0] for send in sends]
        if self.last:
            arrays = lax.optimization_barrier((*arrays, *self.last))[: len(arrays)]
        results = [lax.ppermute(a, axis, perm) for a, (_, axis, perm) in zip(arrays, sends)]
        self.last = (*results, *beside)
        return results


def trade(array, bits, count):
    return array, "ctx", [(i, i ^ bits) for i in range(count)]


MESH = pl.DeviceIdType.MESH


class Spot:
    def __init__(self):
        self.me = lax.axis_index("fsdp")
        self.own = lax.axis_index("ctx")
        self.core = {"fsdp": self.me + 1 - 2 * (self.me % 2)}
        self.across = (self.me + 2) % 4
        self.chip = {"fsdp": self.across}
        self.y = self.own % 2
        self.z = self.own // 2
        self.side = {"ctx": self.own + 1 - 2 * self.y}
        self.next = {"ctx": self.own + 2 - 4 * (self.z % 2)}
        self.ahead = [None] + [{"ctx": (self.own + 2 * k) % 8} for k in (1, 2, 3)]

    def greet(self, neighbours):
        barrier = pltpu.get_barrier_semaphore()
        for neighbour in neighbours:
            pl.semaphore_signal(barrier, inc=1, device_id=neighbour, device_id_type=MESH)
        pl.semaphore_wait(barrier, len(neighbours))


class Wire:
    def __init__(self, send_sems, recv_sems, local_sems):
        self.send_sems, self.recv_sems, self.local_sems = send_sems, recv_sems, local_sems
        self.sent, self.local, self.count = [], [], 0

    def send(self, source, target, device):
        k = self.count
        self.count += 1
        copy = pltpu.make_async_remote_copy(
            src_ref=source,
            dst_ref=target,
            send_sem=self.send_sems.at[k],
            recv_sem=self.recv_sems.at[k],
            device_id=device,
            device_id_type=MESH,
        )
        copy.start()
        self.sent.append(copy)
        return copy

    def keep(self, source, target):
        copy = pltpu.make_async_copy(source, target, self.local_sems.at[len(self.local)])
        copy.start()
        self.local.append(copy)
        return copy

    def left(self, copy):
        copy.wait_send()
        self.sent = [other for other in self.sent if other is not copy]

    def end(self):
        for copy in self.sent:
            copy.wait_send()


def tile_at(step):
    me = lax.axis_index("fsdp")
    place = 3 - step
    return 2 * ((me // 2 + place // 2) % 2) + (me % 2 + place) % 2


def ffn_send_kernel(middle_ref, gain_ref, cot_ref, gates, ups, downs, *refs):
    output_ref, gmiddle_ref, branch_ref, ggain_ref = refs[:4]
    gate_keep, up_keep, down_keep, down_cross, gate_got, up_got, down_got, crossed = refs[4:12]
    normed, x_own, x_turned, cot_turned, total, gnormed = refs[12:18]
    sending, down_first, down_second, down_in, crossing, send_sems, recv_sems = refs[18:]
    step = pl.program_id(0)
    spot = Spot()
    tall, broad = down_keep.shape[2:]

    def copy(k, source, target, device):
        return pltpu.make_async_remote_copy(
            src_ref=source,
            dst_ref=target,
            send_sem=send_sems.at[k],
            recv_sem=recv_sems.at[k],
            device_id=device,
            device_id_type=MESH,
        )

    def tile_copy(at, which):
        got = (gate_got, up_got)[which].at[:, :, pl.ds(2 * tile_at(at), 2)]
        return copy(2 * at + which, sending.at[at % 2, which], got, spot.core)

    first = copy(8, down_first, down_in, spot.core)
    second = copy(9, down_second, down_got, spot.core)
    cross = copy(10, crossing, crossed, spot.chip)

    def inverse():
        middle = middle_ref[...]
        return lax.rsqrt(jnp.mean(middle * middle, axis=-1, keepdims=True) + EPS)

    @pl.when(step == 0)
    def _():
        spot.greet([spot.core, spot.chip])
        ffn_begin(
            spot.me, middle_ref, gain_ref, cot_ref, normed, x_own, x_turned, cot_turned, total, gnormed, inverse
        )

    hidden, ggate, gup = ffn_tile(gates, ups, downs[0], x_turned, cot_turned)
    gdown = dot(hidden, cot_ref[...], (1, 0))

    def down_block(half, eighth):
        return gdown[half * tall : (half + 1) * tall, eighth * broad : (eighth + 1) * broad]

    def store(ref):
        for half in range(2):
            for eighth in range(8):
                ref[half, eighth] = down_block(half, eighth).astype(bf16)

    @pl.when(step == 0)
    def _():
        store(down_first)
        first.start()

    @pl.when(step == 1)
    def _():
        first.wait_recv()
        for half, ref in enumerate((crossing, down_cross)):
            for eighth in range(8):
                ref[eighth] = (down_block(half, eighth) + down_in[half, eighth].astype(f32)).astype(bf16)
        cross.start()

    @pl.when(step == 2)
    def _():
        store(down_second)
        second.start()

    @pl.when(step == 3)
    def _():
        store(down_keep)

    for at in range(4):

        @pl.when(step == at)
        def _(at=at):
            if at >= 2:
                tile_copy(at - 2, 0).wait_send()
                tile_copy(at - 2, 1).wait_send()
            for which, grad in enumerate((ggate, gup)):
                for slot in range(2):
                    value = dot(grad, x_own[2 * slot + 1], (1, 0))
                    for half in range(2):
                        for eighth in range(2):
                            sending[at % 2, which, half, slot, eighth] = value[
                                eighth * tall : (eighth + 1) * tall, half * broad : (half + 1) * broad
                            ].astype(bf16)
                tile_copy(at, which).start()

    for grad, ref in ((ggate, gate_keep), (gup, up_keep)):
        for slot in range(2):
            value = dot(grad, x_own[2 * slot], (1, 0))
            for half in range(2):
                for eighth in range(2):
                    ref[half, slot, eighth] = value[
                        eighth * tall : (eighth + 1) * tall, half * broad : (half + 1) * broad
                    ].astype(bf16)
    gnormed[...] += dot(ggate, gates[...], (0, 0)) + dot(gup, ups[...], (0, 0))
    total[...] += dot(hidden, downs[0], (0, 0))

    @pl.when(step == 3)
    def _():
        ffn_end(middle_ref, gain_ref, cot_ref, total, gnormed, inverse, output_ref, gmiddle_ref, branch_ref, ggain_ref)
        for at in range(4):
            for which in range(2):
                tile_copy(at, which).wait_recv()
                if at >= 2:
                    tile_copy(at, which).wait_send()
        first.wait_send()
        second.wait()
        cross.wait()


def ffn_send_call(middle, gain, cot, gates, ups, downs):
    rows, model = middle.shape
    width = model // 4
    tile = downs.shape[1]
    once = pl.Buffered(1)
    block = (tile // 2, model // 8)

    def whole(*shape, **kw):
        return pl.BlockSpec(shape, lambda s: (0,) * len(shape), **kw)

    columns = pl.BlockSpec((tile, model), lambda s: (tile_at(s), 0))
    pair = pl.BlockSpec((2, 2, 2, *block), lambda s: (0, 0, tile_at(s), 0, 0))
    grads = jax.ShapeDtypeStruct((2, 2, 8, *block), bf16)
    halves = jax.ShapeDtypeStruct((2, 8, *block), bf16)
    one = jax.ShapeDtypeStruct((8, *block), bf16)
    return pl.pallas_call(
        ffn_send_kernel,
        out_shape=[
            jax.ShapeDtypeStruct((rows, model), bf16),
            jax.ShapeDtypeStruct((rows, model), f32),
            jax.ShapeDtypeStruct((rows, model), bf16),
            jax.ShapeDtypeStruct((8, model), f32),
            grads,
            grads,
            halves,
            one,
            grads,
            grads,
            halves,
            one,
        ],
        grid=(4,),
        in_specs=[
            whole(rows, model, pipeline_mode=once),
            whole(2, model),
            whole(rows, model, pipeline_mode=once),
            columns,
            columns,
            pl.BlockSpec((1, tile, model), lambda s: (tile_at(s), 0, 0)),
        ],
        out_specs=[
            whole(rows, model, pipeline_mode=once),
            whole(rows, model, pipeline_mode=once),
            whole(rows, model, pipeline_mode=once),
            whole(8, model),
            pair,
            pair,
            whole(2, 8, *block, pipeline_mode=once),
            whole(8, *block, pipeline_mode=once),
            HBM,
            HBM,
            HBM,
            HBM,
        ],
        scratch_shapes=[
            pltpu.VMEM((rows, model), bf16),
            pltpu.VMEM((4, rows, width), bf16),
            pltpu.VMEM((model, rows), bf16),
            pltpu.VMEM((model, rows), bf16),
            pltpu.VMEM((rows, model), f32),
            pltpu.VMEM((rows, model), f32),
            pltpu.VMEM((2, 2, 2, 2, 2, *block), bf16),
            pltpu.VMEM((2, 8, *block), bf16),
            pltpu.VMEM((2, 8, *block), bf16),
            pltpu.VMEM((2, 8, *block), bf16),
            pltpu.VMEM((8, *block), bf16),
            sems(11),
            sems(11),
        ],
        compiler_params=pltpu.CompilerParams(collective_id=3, has_side_effects=True, vmem_limit_bytes=60 << 20),
    )(middle, gain, cot, gates, ups, downs)


BY_Y, BY_Z = 1, 2


class Gather:
    def __init__(self, wire, spot, shard, full, held, axis, split, chunks):
        self.stacked = len(full.shape) == 3
        self.wire, self.spot, self.full, self.axis, self.split = wire, spot, full, axis, split
        self.turn, self.neighbour = (spot.z % 2, spot.next) if split == BY_Z else (spot.y, spot.side)
        self.part = shard.shape[axis] // (2 if split else 1)
        self.size = self.part // chunks
        me = spot.me
        self.held, self.loaded = held, wire.keep(shard, self.place(me) if held is None else held)
        here = [self.view(shard, c, self.turn) for c in range(chunks)]
        there = [self.view(self.place(me), c, self.turn) for c in range(chunks)]
        self.cross = [wire.send(a, b, spot.chip) for a, b in zip(here, there)]
        self.near = wire.send(shard, self.place(me), spot.core)
        self.side, self.far = {}, []

    def place(self, shard):
        if self.stacked:
            return self.full.at[shard]
        width = self.full.shape[1] // 4
        return self.full.at[:, pl.ds(pl.multiple_of(shard * width, width), width)]

    def write(self):
        self.loaded.wait()
        self.own = None if self.held is None else self.wire.keep(self.held, self.place(self.spot.me))

    def view(self, ref, chunk, turn):
        start = chunk * self.size + (turn * self.part if self.split else 0)
        index = [slice(None)] * 2
        index[self.axis] = pl.ds(pl.multiple_of(start, self.size), self.size)
        return ref.at[tuple(index)]

    def relay(self, chunk):
        self.cross[chunk].wait_recv()
        part = self.view(self.place(self.spot.across), chunk, self.turn)
        if self.split:
            self.side[chunk] = self.wire.send(part, part, self.neighbour)
        self.far.append(self.wire.send(part, part, self.spot.core))

    def relay_other(self, chunk):
        self.side[chunk].wait_recv()
        part = self.view(self.place(self.spot.across), chunk, 1 - self.turn)
        self.far.append(self.wire.send(part, part, self.spot.core))

    def end(self):
        if self.own is not None:
            self.own.wait()
        self.near.wait_recv()
        for copy in self.far:
            copy.wait_recv()


class StateSum:
    def __init__(self, wire, spot, places_ref, later, states, beside, outgoing, ring, result):
        self.wire, self.spot, self.states, self.beside = wire, spot, states, beside
        self.outgoing, self.ring, self.result = outgoing, ring, result
        self.sent = {}

        def place(device, block):
            return places_ref[0, 2 * device + block]

        partner = spot.own + 1 - 2 * spot.y
        sources = [place(device, block) for device in (spot.own, partner) for block in range(2)]
        self.masks = {}
        for k in range(4):
            for block in range(2):
                target = place((spot.own + 8 - 2 * k) % 8, block)
                self.masks[k, block] = [
                    jnp.where(source > target if later else source < target, 1.0, 0.0).astype(f32)
                    for source in sources
                ]

    def part(self, k, block, group):
        refs = (self.states.at[0], self.states.at[1], self.beside.at[0], self.beside.at[1])
        terms = [ref[group].astype(f32) * mask for ref, mask in zip(refs, self.masks[k, block])]
        return (terms[0] + terms[1]) + (terms[2] + terms[3])

    def trade(self):
        self.traded = self.wire.send(self.states, self.beside, self.spot.side)

    def first(self, block):
        if block == 0:
            self.traded.wait_recv()
        for group in range(self.states.shape[1]):
            self.outgoing[block, group] = self.part(1, block, group).astype(bf16)
        self.sent[0, block] = self.wire.send(self.outgoing.at[block], self.ring.at[0, block], self.spot.ahead[1])

    def hop(self, step, block):
        self.sent[step, block].wait_recv()
        target = self.result if step == 2 else self.ring.at[step]
        for group in range(self.states.shape[1]):
            value = self.ring[step, block, group].astype(f32) + self.part((step + 2) % 4, block, group)
            target[block, group] = value.astype(bf16)
        if step < 2:
            self.sent[step + 1, block] = self.wire.send(
                self.ring.at[step, block], self.ring.at[step + 1, block], self.spot.ahead[1]
            )


class StateRing:
    def __init__(self, wire, spot, places_ref, later, states, beside, outgoing, ring, result):
        self.wire, self.spot, self.states, self.beside = wire, spot, states, beside
        self.outgoing, self.ring, self.result = outgoing, ring, result
        self.sent, self.traded = {}, {}

        def place(device, block):
            return places_ref[0, 2 * device + block]

        sources = [place((spot.own + 8 - 2 * k) % 8, block) for k in range(4) for block in range(2)]
        self.masks = {}
        for beyond, device in enumerate((spot.own, spot.own + 1 - 2 * spot.y)):
            for block in range(2):
                target = place(device, block)
                self.masks[beyond, block] = [
                    jnp.where(source > target if later else source < target, 1.0, 0.0).astype(f32)
                    for source in sources
                ]

    def part(self, beyond, block, group):
        refs = [ref.at[b] for ref in (self.states, *(self.ring.at[k] for k in range(3))) for b in range(2)]
        total = None
        for ref, mask in zip(refs, self.masks[beyond, block]):
            term = ref[group].astype(f32) * mask
            total = term if total is None else total + term
        return total

    def start(self):
        for block in range(2):
            self.pass_on(0, block, self.states.at[block])

    def pass_on(self, step, block, source):
        self.sent[step, block] = self.wire.send(source, self.ring.at[step, block], self.spot.ahead[1])

    def forward(self, step, block):
        self.sent[step, block].wait_recv()
        if step < 2:
            self.pass_on(step + 1, block, self.ring.at[step, block])

    def partner(self, block):
        for group in range(self.states.shape[1]):
            self.outgoing[block, group] = self.part(1, block, group).astype(bf16)
        self.traded[block] = self.wire.send(self.outgoing.at[block], self.beside.at[block], self.spot.side)

    def finish(self, block):
        self.traded[block].wait_recv()
        for group in range(self.states.shape[1]):
            value = self.part(0, block, group) + self.beside[block, group].astype(f32)
            self.result[block, group] = value.astype(bf16)


def forward_kernel(places_ref, tokens_ref, gains_ref, *refs):
    in_shards, refs = refs[:3], refs[3:]
    weights, (gain_rows, query_ref, key_ref, value_ref, prefix_ref, atten_ref, denom_ref, middle_ref) = refs[:4], refs[4:12]
    in_out, out_out, *fulls = refs[12:17]
    refs = refs[17:]
    gains, in_full, out_full, normed, own_states, rings, outgoing, beside, numer, inner = refs[:10]
    held, (send_sems, recv_sems, local_sems) = refs[10:14], refs[14:]
    spot = Spot()
    wire = Wire(send_sems, recv_sems, local_sems)
    spot.greet([spot.core, spot.chip, spot.side, spot.ahead[1], spot.ahead[3]])
    me = spot.me
    columns, start = [], 0
    for shard in in_shards:
        columns.append(slice(start, start + shard.shape[1]))
        start += shard.shape[1]
    query_w, key_w, value_w = ins = [
        Gather(wire, spot, shard, in_full.at[:, :, at], None, 0, BY_Y, chunks)
        for shard, at, chunks in zip(in_shards, columns, (1, 1, 2))
    ]
    gain_own = wire.keep(gains_ref, gains.at[me])
    gain_near = wire.send(gains_ref, gains.at[me], spot.core)
    gain_cross = wire.send(gains_ref, gains.at[me], spot.chip)
    out_w, gate_w, up_w, down_w = weights
    half = down_w.shape[1] // 2
    left, right = slice(0, half), slice(half, 2 * half)
    out = Gather(wire, spot, out_w, out_full, None, 0, BY_Y, 1)
    gate = Gather(wire, spot, gate_w, fulls[0], held[0], 0, BY_Y, 2)
    up = Gather(wire, spot, up_w, fulls[1], held[1], 0, BY_Y, 2)
    down_left = Gather(wire, spot, down_w.at[:, left], fulls[2].at[:, :, left], held[2], 1, BY_Z, 1)
    down_right = Gather(wire, spot, down_w.at[:, right], fulls[2].at[:, :, right], held[3], 1, 0, 2)
    everything = (*ins, out, gate, up, down_left, down_right)
    kept = {}
    groups = [slice(k, k + 1) for k in range(HEADS // GROUP)]
    views = [
        [ref.at[:, at] for ref in (own_states, beside, outgoing)] + [rings.at[:, :, at], prefix_ref.at[:, at]]
        for at in groups
    ]
    sums = StateSum(wire, spot, places_ref, False, *views[0])
    ring = StateRing(wire, spot, places_ref, False, *views[1])
    intra = list(grid_views((query_ref, FDIM), (key_ref, FDIM), (value_ref, VDIM), (numer, VDIM), (inner, 1)))

    def statistics():
        residual = tokens_ref[...].astype(f32)
        inverse = lax.rsqrt(jnp.mean(residual * residual, axis=-1, keepdims=True) + EPS)
        middle_ref[...] = residual * inverse
        gain_cross.wait_recv()
        across = gains.at[spot.across]
        kept[0] = wire.send(across, across, spot.core)
        for one in everything:
            one.write()

    def project():
        gain_own.wait()
        gain_near.wait_recv()
        kept[0].wait_recv()
        for one in ins:
            one.end()
        kept[1] = wire.keep(in_full, in_out)
        width = in_full.shape[1]
        for row in range(2):
            line = jnp.concatenate([gains[k, row : row + 1, :] for k in range(4)], axis=1)
            gain_rows[row : row + 1, :] = line.astype(f32)
        normed[...] = (middle_ref[...] * gain_rows[0:1, :]).astype(bf16)
        for at, ref in zip(columns, (query_ref, key_ref, value_ref)):
            total = None
            for k in range(4):
                term = dot(normed[:, k * width : (k + 1) * width], in_full[k, :, at], (1, 0))
                total = term if total is None else total + term
            ref[...] = total.astype(bf16).T

    def states():
        for parts in grid_views((key_ref, FDIM), (value_ref, VDIM), (own_states, None)):
            states_kernel(*parts)
        sums.trade()
        ring.start()

    def inter():
        for parts in grid_views(
            (query_ref, FDIM), (prefix_ref, None), (numer, VDIM), (inner, 1), (atten_ref, VDIM), (denom_ref, 1)
        ):
            inter_kernel(*parts)

    def middle():
        out.end()
        kept[2] = wire.keep(out_full, out_out)
        total = tokens_ref[...].astype(f32)
        width = out_w.shape[0]
        for k in range(4):
            total = total + dot(atten_ref[k * width : (k + 1) * width, :], out_full[k], (0, 0))
        middle_ref[...] = total

    query_w.relay(0)
    query_w.relay_other(0)
    value_w.relay(0)
    value_w.relay(1)
    key_w.relay(0)
    statistics()
    value_w.relay_other(1)
    value_w.relay_other(0)
    out.relay(0)
    key_w.relay_other(0)
    project()
    states()
    ring.forward(0, 0)
    gate.relay(1)
    gate.relay(0)
    sums.first(0)
    ring.forward(0, 1)
    up.relay(0)
    ring.forward(1, 0)
    gate.relay_other(1)
    ring.forward(1, 1)
    sums.first(1)
    sums.hop(0, 0)
    intra_kernel(*intra[0])
    ring.forward(2, 1)
    ring.forward(2, 0)
    ring.partner(1)
    intra_kernel(*intra[1])
    sums.hop(0, 1)
    ring.partner(0)
    up.relay(1)
    sums.hop(1, 0)
    sums.hop(1, 1)
    up.relay_other(0)
    down_right.relay(0)
    intra_kernel(*intra[2])
    sums.hop(2, 0)
    ring.finish(0)
    down_left.relay(0)
    intra_kernel(*intra[3])
    sums.hop(2, 1)
    gate.relay_other(0)
    out.relay_other(0)
    ring.finish(1)
    inter()
    down_right.relay(1)
    up.relay_other(1)
    middle()
    down_left.relay_other(0)
    for one in everything[4:]:
        one.end()
    kept[1].wait()
    kept[2].wait()
    wire.end()


def grid_views(*refs):
    for block in range(2):
        for group in range(HEADS // GROUP):
            columns = slice(block * BLOCK, (block + 1) * BLOCK)
            parts = []
            for ref, rows in refs:
                if rows is None:
                    parts.append(ref.at[block : block + 1, group : group + 1])
                else:
                    parts.append(ref.at[group * GROUP * rows : (group + 1) * GROUP * rows, columns])
            yield parts


def add_chunks(total, first, other, count):
    def one(k, carry):
        total[first + k] = (total[first + k].astype(f32) + other[k].astype(f32)).astype(bf16)
        return carry

    lax.fori_loop(0, count, one, 0)


class Flow:
    def __init__(self, wire, spot, kept, sent, crossed, sided, lined, result):
        self.wire, self.spot = wire, spot
        self.kept, self.sent, self.crossed, self.sided, self.lined, self.result = kept, sent, crossed, sided, lined, result
        self.half = spot.y * 4
        self.pair = self.half + 2 * (spot.z % 2)
        self.mine = self.pair + spot.z // 2

    def cross(self):
        self.arrive = self.wire.send(self.sent, self.crossed, self.spot.chip).wait_recv

    def to_side(self):
        self.arrive()
        add_chunks(self.crossed, 0, self.kept, 8)
        there = pl.ds(4 - self.half, 4)
        self.s = self.wire.send(self.crossed.at[there], self.sided, self.spot.side)

    def to_line(self):
        self.s.wait_recv()
        add_chunks(self.crossed, self.half, self.sided, 4)
        there = pl.ds(2 * self.half + 2 - self.pair, 2)
        self.l = self.wire.send(self.crossed.at[there], self.lined.at[0:2], self.spot.next)

    def to_far(self):
        self.l.wait_recv()
        add_chunks(self.crossed, self.pair, self.lined, 2)
        self.f = self.wire.send(self.crossed.at[2 * self.pair + 1 - self.mine], self.lined.at[2], self.spot.ahead[2])

    def from_far(self):
        self.f.wait_recv()
        mine = self.mine
        self.crossed[mine] = (self.crossed[mine].astype(f32) + self.lined[2].astype(f32)).astype(bf16)
        self.own = self.wire.keep(self.crossed.at[mine], self.result.at[mine])
        self.g = self.wire.send(self.crossed.at[mine], self.result.at[mine], self.spot.ahead[2])

    def along_line(self):
        self.own.wait()
        self.g.wait_recv()
        here = self.result.at[pl.ds(self.pair, 2)]
        self.a = self.wire.send(here, here, self.spot.next)

    def along_side(self):
        self.a.wait_recv()
        here = self.result.at[pl.ds(self.half, 4)]
        self.b = self.wire.send(here, here, self.spot.side)

    def end(self):
        self.b.wait_recv()


def backward_kernel(names, *refs):
    r = SimpleNamespace(**dict(zip(names, refs)))
    spot = Spot()
    wire = Wire(r.send_sems, r.recv_sems, r.local_sems)
    me, z = spot.me, spot.z
    spot.greet([spot.core, spot.chip, spot.side, *spot.ahead[1:]])

    def load(*pairs):
        return [wire.keep(a, b) for a, b in pairs]

    def ready(copies):
        for copy in copies:
            copy.wait()

    first = load(
        (r.out_full_hbm, r.out_full),
        (r.branch_hbm, r.branch),
        (r.atten_hbm, r.atten),
        (r.denom_hbm, r.denom),
        (r.query_hbm, r.query),
    )
    arrived = load((r.first_cross, r.crossed.at[0]))
    down_loads = load((r.down_got, r.down_core), (r.down_keep, r.down_stage))
    kept, held = (r.gate_keep, r.up_keep), (r.gate_core, r.up_core)
    bases = (2, 0, 1, 3)
    stage = r.stage
    got = {weight: load((ref, held[weight])) for weight, ref in ((bases[0] // 2, (r.gate_got, r.up_got)[bases[0] // 2]),)}
    staged = {}

    def fetch(index):
        weight, half = bases[index] // 2, bases[index] % 2
        staged[index] = wire.keep(kept[weight].at[half], stage.at[index % 2])

    fetch(0)
    fetch(1)
    second = load((r.key_hbm, r.key), (r.value_hbm, r.value), (r.prefix_hbm, r.prefix))
    other = 1 - bases[0] // 2
    got[other] = load(((r.gate_got, r.up_got)[other], held[other]))
    tokens_load = load((r.tokens_hbm, r.tokens))
    third = load((r.in_full_hbm, r.in_full), (r.gmiddle_hbm, r.gmiddle))

    def base(index):
        weight, half = bases[index] // 2, bases[index] % 2
        ready(got[weight])
        got[weight] = []
        staged[index].wait()
        for slot in range(2):
            add_chunks(held[weight].at[half, slot], 0, stage.at[index % 2, slot], 8)
        if index < 2:
            fetch(index + 2)

    def down_base():
        ready(down_loads)
        for half in range(2):
            add_chunks(r.down_core.at[half], 0, r.down_stage.at[half], 8)

    def flow(index, kept_ref, sent_ref, result):
        return Flow(wire, spot, kept_ref, sent_ref, r.crossed.at[index], r.sided.at[index], r.lined.at[index], result)

    da, db = (flow(half, r.down_core.at[half], r.second_cross, r.down_out.at[half]) for half in range(2))
    da.arrive = arrived[0].wait
    ga, gb = (flow(2 + half, r.gate_core.at[half, 0], r.gate_core.at[half, 1], r.gate_out.at[half]) for half in range(2))
    ua, ub = (flow(4 + half, r.up_core.at[half, 0], r.up_core.at[half, 1], r.up_out.at[half]) for half in range(2))
    out_flow = Flow(
        wire, spot, r.out_base.at[0], r.out_base.at[1], r.out_crossed, r.out_sided, r.out_lined, r.out_out
    )
    in_flow = Flow(wire, spot, r.in_base.at[0], r.in_base.at[1], r.in_crossed, r.in_sided, r.in_lined, r.in_out)
    states, gnumer, gdenom, grad = r.states, r.gnumer, r.gdenom, r.grad
    views = [
        [ref.at[:, k : k + 1] for ref in (states, r.beside, r.outgoing)]
        + [r.ring.at[:, :, k : k + 1], r.later.at[:, k : k + 1]]
        for k in range(HEADS // GROUP)
    ]
    sums = StateSum(wire, spot, r.places, True, *views[0])
    ring = StateRing(wire, spot, r.places, True, *views[1])

    def grad_atten():
        ready(first)
        grad[...] = dot(r.out_full[...], r.branch[...], (1, 1))

    def grad_states():
        for parts in grid_views(
            (r.query, FDIM), (r.atten, VDIM), (r.denom, 1), (grad, VDIM), (gnumer, VDIM), (gdenom, 1), (states, None)
        ):
            grad_states_kernel(*parts)
        sums.trade()
        ring.start()

    core_of = me + 1 - 2 * (me % 2)
    shards = (me, spot.across, core_of, (core_of + 2) % 4)
    width = r.branch.shape[1] // 4

    def out_grads(other):
        for slot in range(2):
            rows = pl.ds(pl.multiple_of(shards[2 * other + slot] * width, width), width)
            value = dot(r.atten[rows, :], r.branch[...], (1, 0))
            ref = r.out_send if other else r.out_base
            for k in range(8):
                ref[slot, k] = value[k * 32 : (k + 1) * 32, :].astype(bf16)
        if other:
            r.out_wait = wire.send(r.out_send, r.out_core, spot.core).wait_recv

    def out_base():
        r.out_wait()
        for slot in range(2):
            add_chunks(r.out_base.at[slot], 0, r.out_core.at[slot], 8)

    narrow = HEADS * FDIM
    gproj = r.gproj
    gquery, gkey = gproj.at[0:narrow], gproj.at[narrow : 2 * narrow]
    gvalue = gproj.at[2 * narrow : 2 * narrow + HEADS * VDIM]
    intra_views = list(
        grid_views(
            (r.query, FDIM),
            (r.key, FDIM),
            (r.value, VDIM),
            (gnumer, VDIM),
            (gdenom, 1),
            (r.prefix, None),
            (gquery, FDIM),
            (r.gkey_in, FDIM),
            (grad, VDIM),
        )
    )

    def intra(index):
        if index == 0:
            ready(second)
        intra_back_kernel(*intra_views[index])

    def inverse(residual):
        return lax.rsqrt(jnp.mean(residual * residual, axis=-1, keepdims=True) + EPS)

    def normalise():
        ready(tokens_load)
        residual = r.tokens[...].astype(f32)
        r.normed[...] = (residual * inverse(residual) * r.gain_one[0:1, :]).astype(bf16)

    turned = r.turned

    def inter_back():
        for parts in grid_views(
            (r.key, FDIM),
            (r.value, VDIM),
            (r.later, None),
            (r.gkey_in, FDIM),
            (grad, VDIM),
            (gkey, FDIM),
            (gvalue, VDIM),
        ):
            inter_back_kernel(*parts)
        turned[...] = gproj[...].T

    def in_grads(other):
        for slot in range(2):
            columns = pl.ds(pl.multiple_of(shards[2 * other + slot] * width, width), width)
            value = dot(r.normed[:, columns], turned[...], (0, 0))
            ref = r.in_send if other else r.in_base
            for k in range(8):
                ref[slot, k] = value[k * 32 : (k + 1) * 32, :].astype(bf16)
        if other:
            r.in_wait = wire.send(r.in_send, r.in_core, spot.core).wait_recv

    def in_base():
        r.in_wait()
        for slot in range(2):
            add_chunks(r.in_base.at[slot], 0, r.in_core.at[slot], 8)

    gains, small, small_in, small_line = r.gains, r.small, r.small_in, r.small_line

    def tokens_grad():
        ready(third)
        gnormed = dot(turned[...], r.in_full[...], (1, 1))
        residual = r.tokens[...].astype(f32)
        inv = inverse(residual)
        gains[0:1, :] = jnp.sum(gnormed * residual * inv, axis=0, keepdims=True)
        weighted = gnormed * r.gain_one[0:1, :]
        slope = jnp.mean(weighted * residual, axis=-1, keepdims=True)
        r.gmiddle[...] += inv * weighted - residual * (inv * inv * inv) * slope
        r.written = wire.keep(r.gmiddle, r.tokens_out)

    def gain_grads():
        gains[1:2, :] = r.ggain_two[0:1, :]
        small[...] = jnp.zeros_like(small)
        for index in range(4):
            for row in range(4):
                start = pl.multiple_of(shards[index] * width + (row % 2) * 128, 128)
                small[index, row : row + 1, :] = gains[row // 2 : row // 2 + 1, pl.ds(start, 128)]
        r.small_wait = wire.send(small.at[2:4], small_in.at[0:2], spot.core).wait_recv

    def gains_cross():
        r.small_wait()
        small[0:2] = small[0:2] + small_in[0:2]
        r.small_wait = wire.send(small.at[1], small_in.at[2], spot.chip).wait_recv

    def gains_side():
        r.small_wait()
        small[0] = small[0] + small_in[2]
        r.small_wait = wire.send(small.at[0], small_in.at[3], spot.side).wait_recv

    def gains_line():
        r.small_wait()
        small_line[z] = small[0] + small_in[3]
        r.small_sent = [wire.send(small_line.at[z], small_line.at[z], spot.ahead[k]) for k in (1, 2, 3)]

    def gains_end():
        for copy in r.small_sent:
            copy.wait_recv()
        r.gains_out[...] = (small_line[0] + small_line[1]) + (small_line[2] + small_line[3])

    db.cross()
    grad_atten()
    grad_states()
    normalise()
    ring.forward(0, 0)
    down_base()
    ring.forward(0, 1)
    base(0)
    ua.cross()
    da.to_side()
    base(1)
    sums.first(0)
    out_grads(1)
    base(2)
    gb.cross()
    ring.forward(1, 1)
    intra(0)
    out_grads(0)
    base(3)
    da.to_line()
    db.to_side()
    ring.forward(1, 0)
    ua.to_side()
    sums.first(1)
    da.to_far()
    intra(1)
    ring.forward(2, 0)
    db.to_line()
    ua.to_line()
    ring.forward(2, 1)
    da.from_far()
    ring.partner(0)
    ring.partner(1)
    ga.cross()
    intra(2)
    sums.hop(0, 0)
    ring.finish(0)
    da.along_line()
    db.to_far()
    out_base()
    ua.to_far()
    out_flow.cross()
    gb.to_side()
    sums.hop(0, 1)
    da.along_side()
    sums.hop(1, 0)
    sums.hop(1, 1)
    intra(3)
    ring.finish(1)
    ga.to_side()
    db.from_far()
    ub.cross()
    gb.to_line()
    sums.hop(2, 0)
    sums.hop(2, 1)
    out_flow.to_side()
    db.along_line()
    ua.from_far()
    inter_back()
    in_grads(1)
    db.along_side()
    out_flow.to_line()
    gb.to_far()
    in_grads(0)
    in_base()
    in_flow.cross()
    out_flow.to_far()
    ua.along_line()
    ub.to_side()
    out_flow.from_far()
    gb.from_far()
    ua.along_side()
    ga.to_line()
    out_flow.along_line()
    tokens_grad()
    ga.to_far()
    ub.to_line()
    out_flow.along_side()
    gb.along_line()
    gain_grads()
    gains_cross()
    in_flow.to_side()
    ga.from_far()
    ub.to_far()
    da.end()
    out_flow.end()
    ga.along_line()
    gb.along_side()
    gains_side()
    ua.end()
    db.end()
    in_flow.to_line()
    ga.along_side()
    ub.from_far()
    in_flow.to_far()
    ub.along_line()
    gb.end()
    in_flow.from_far()
    ub.along_side()
    gains_line()
    in_flow.along_line()
    in_flow.along_side()
    gains_end()
    ga.end()
    ub.end()
    in_flow.end()
    r.written.wait()
    wire.end()


HBM = pl.BlockSpec(memory_space=pltpu.HBM)
VMEM = pl.BlockSpec(memory_space=pltpu.VMEM)
SMEM = pl.BlockSpec(memory_space=pltpu.SMEM)


def sems(count):
    return pltpu.SemaphoreType.DMA((count,))


def forward_call(places, tokens, gains, in_shards, weights):
    rows, model = tokens.shape
    narrow, wide = HEADS * FDIM, HEADS * VDIM
    state = (rows // BLOCK, HEADS // GROUP, STATE, 128)
    in_full = (4, in_shards[0].shape[0], sum(a.shape[1] for a in in_shards))
    tall, model_half = weights[3].shape[0], weights[3].shape[1] // 2

    def low(*shape):
        return jax.ShapeDtypeStruct(shape, bf16)

    return pl.pallas_call(
        forward_kernel,
        out_shape=[
            jax.ShapeDtypeStruct((2, model), f32),
            low(narrow, rows),
            low(narrow, rows),
            low(wide, rows),
            low(*state),
            low(wide, rows),
            jax.ShapeDtypeStruct((HEADS, rows), f32),
            jax.ShapeDtypeStruct((rows, model), f32),
            low(*in_full),
        ]
        + [low(4, *weights[0].shape)]
        + [low(w.shape[0], 4 * w.shape[1]) for w in weights[1:3]]
        + [low(4, *weights[3].shape)],
        in_specs=[SMEM, VMEM] + [HBM] * 8,
        out_specs=[VMEM] * 8 + [HBM] * 5,
        scratch_shapes=[
            pltpu.VMEM((4, *gains.shape), bf16),
            pltpu.VMEM(in_full, bf16),
            pltpu.VMEM((4, *weights[0].shape), bf16),
            pltpu.VMEM((rows, model), bf16),
            pltpu.VMEM(state, bf16),
            pltpu.VMEM((3, *state), bf16),
            pltpu.VMEM(state, bf16),
            pltpu.VMEM(state, bf16),
            pltpu.VMEM((wide, rows), f32),
            pltpu.VMEM((HEADS, rows), f32),
            *(pltpu.VMEM(w.shape, bf16) for w in weights[1:3]),
            *[pltpu.VMEM((tall, model_half), bf16)] * 2,
            sems(72),
            sems(72),
            sems(28),
        ],
        compiler_params=pltpu.CompilerParams(collective_id=1, has_side_effects=True, vmem_limit_bytes=58 << 20),
    )(places, tokens, gains, *in_shards, *weights)


def settle_kernel(down_ref, gate_ref, up_ref, out_ref, in_ref, output_ref, tokens_ref, *outs):
    tall, broad = down_ref.shape[2:]
    down_out, gate_out, up_out, out_out = outs[:4]
    size = out_ref.shape[1]
    for k in range(2):
        tiles, lanes, lines = (slice(k * n, (k + 1) * n) for n in (tall, broad, size))
        for half in range(2):
            down_out[half * tall : (half + 1) * tall, lanes] = down_ref[half, k].astype(f32)
            gate_out[tiles, half * broad : (half + 1) * broad] = gate_ref[half, k].astype(f32)
            up_out[tiles, half * broad : (half + 1) * broad] = up_ref[half, k].astype(f32)
        out_out[lines, :] = out_ref[k].astype(f32)
        start = 0
        for out in outs[4:7]:
            stop = start + out.shape[1]
            out[lines, :] = in_ref[k, :, start:stop].astype(f32)
            start = stop
    outs[7][...] = output_ref[...]
    outs[8][...] = tokens_ref[...]


def settle_call(down, gate, up, out, ins, output, tokens):
    tall, broad = down.shape[2:]
    size, model = out.shape[1:]
    narrow = HEADS * FDIM
    rows = output.shape[0]
    blocks = pl.BlockSpec((2, 2, tall, broad), lambda k: (0, k, 0, 0))

    def line(height, width):
        return pl.BlockSpec((height, width), lambda k: (k, 0))

    def eighths(a):
        return pl.BlockSpec((2, *a.shape[1:]), lambda k: (k, 0, 0))

    shapes = [(2 * tall, 8 * broad), (8 * tall, 2 * broad), (8 * tall, 2 * broad), (8 * size, model)]
    widths = (narrow, narrow, ins.shape[2] - 2 * narrow)
    shapes += [(8 * size, width) for width in widths]
    whole = [line(rows // 4, model)] * 2
    return pl.pallas_call(
        settle_kernel,
        out_shape=[jax.ShapeDtypeStruct(shape, f32) for shape in shapes]
        + [jax.ShapeDtypeStruct(a.shape, a.dtype) for a in (output, tokens)],
        grid=(4,),
        in_specs=[blocks, blocks, blocks, eighths(out), eighths(ins), *whole],
        out_specs=[
            pl.BlockSpec((2 * tall, 2 * broad), lambda k: (0, k)),
            line(2 * tall, 2 * broad),
            line(2 * tall, 2 * broad),
            line(2 * size, model),
            *(line(2 * size, width) for width in widths),
            *whole,
        ],
        compiler_params=pltpu.CompilerParams(vmem_limit_bytes=60 << 20),
    )(down, gate, up, out, ins, output, tokens)


def masked_sums(pieces, masks, dtype):
    total = None
    for index, piece in enumerate(pieces):
        for block in range(piece.shape[0]):
            term = masks[:, index, block][:, None, None, None] * piece[block].astype(f32)[None]
            total = term if total is None else total + term
    return total.astype(dtype)


class Exchange:
    def __init__(self, states, positions, own, count, later):
        self.pieces, self.sources, self.own, self.count, self.later = [states], [own], own, count, later
        self.table = positions.reshape(count, states.shape[0])

    def mask(self, target):
        there = self.table[target][:, None, None]
        here = self.table[jnp.stack(self.sources)][None]
        return ((here > there) if self.later else (here < there)).astype(f32)

    def ring(self):
        return self.pieces[-1], "ctx", [(i, (i + 2) % self.count) for i in range(self.count)]

    def passed(self, piece):
        self.sources.append((self.own - 2 * len(self.pieces)) % self.count)
        self.pieces.append(piece)

    def partner(self):
        return trade(masked_sums(self.pieces, self.mask(self.own ^ 1), bf16), 1, self.count)

    def total(self, received):
        return (masked_sums(self.pieces, self.mask(self.own), f32) + received.astype(f32)).astype(bf16)


def backward_call(arrays):
    names, specs, values = [], [], []
    get = SimpleNamespace(**arrays)
    for name, array in arrays.items():
        names.append(name)
        values.append(array)
        specs.append(SMEM if array.dtype == jnp.int32 else VMEM if array.shape[0] <= 8 and array.dtype == f32 else HBM)
    rows, model = get.tokens_hbm.shape
    columns = get.in_full_hbm.shape[1]
    block = get.down_keep.shape[2:]
    narrow, wide = HEADS * FDIM, HEADS * VDIM
    state = get.prefix_hbm.shape
    outs = dict(
        tokens_out=((rows, model), f32, HBM),
        down_out=((2, 8, *block), bf16, HBM),
        gate_out=((2, 8, *block), bf16, HBM),
        up_out=((2, 8, *block), bf16, HBM),
        out_out=((8, 32, model), bf16, HBM),
        in_out=((8, 32, columns), bf16, HBM),
        gains_out=((8, 128), f32, VMEM),
    )
    scratch = dict(
        down_core=((2, 8, *block), bf16),
        down_stage=((2, 8, *block), bf16),
        gate_core=((2, 2, 8, *block), bf16),
        up_core=((2, 2, 8, *block), bf16),
        stage=((2, 2, 8, *block), bf16),
        crossed=((6, 8, *block), bf16),
        sided=((6, 4, *block), bf16),
        lined=((6, 3, *block), bf16),
        out_full=((wide, model), bf16),
        branch=((rows, model), bf16),
        atten=((wide, rows), bf16),
        denom=((HEADS, rows), f32),
        query=((narrow, rows), bf16),
        key=((narrow, rows), bf16),
        value=((wide, rows), bf16),
        prefix=(state, bf16),
        tokens=((rows, model), bf16),
        in_full=((model, columns), bf16),
        gmiddle=((rows, model), f32),
        grad=((wide, rows), f32),
        gnumer=((wide, rows), bf16),
        gdenom=((HEADS, rows), f32),
        states=(state, bf16),
        ring=((3, *state), bf16),
        outgoing=(state, bf16),
        beside=(state, bf16),
        later=(state, bf16),
        gproj=((columns, rows), bf16),
        gkey_in=((narrow, rows), f32),
        normed=((rows, model), bf16),
        turned=((rows, columns), bf16),
        gains=((8, model), f32),
        small=((4, 8, 128), f32),
        small_in=((4, 8, 128), f32),
        small_line=((4, 8, 128), f32),
        out_base=((2, 8, 32, model), bf16),
        out_send=((2, 8, 32, model), bf16),
        out_core=((2, 8, 32, model), bf16),
        out_crossed=((8, 32, model), bf16),
        out_sided=((4, 32, model), bf16),
        out_lined=((3, 32, model), bf16),
        in_base=((2, 8, 32, columns), bf16),
        in_send=((2, 8, 32, columns), bf16),
        in_core=((2, 8, 32, columns), bf16),
        in_crossed=((8, 32, columns), bf16),
        in_sided=((4, 32, columns), bf16),
        in_lined=((3, 32, columns), bf16),
    )
    names += [*outs, *scratch, *dict(send_sems=0, recv_sems=0, local_sems=0)]
    return pl.pallas_call(
        functools.partial(backward_kernel, tuple(names)),
        out_shape=[jax.ShapeDtypeStruct(shape, dtype) for shape, dtype, _ in outs.values()],
        in_specs=specs,
        out_specs=[spec for _, _, spec in outs.values()],
        scratch_shapes=[pltpu.VMEM(shape, dtype) for shape, dtype in scratch.values()]
        + [sems(100), sems(100), sems(48)],
        compiler_params=pltpu.CompilerParams(collective_id=2, has_side_effects=True, vmem_limit_bytes=60 << 20),
    )(*values)


def body(count):
    def layer(
        tokens, block_pos, gain_attn, w_query, w_key, w_value, w_out, gain_ffn, w_gate, w_up, w_down, cotangent
    ):
        own = lax.axis_index("ctx")
        me = lax.axis_index("fsdp").astype(jnp.int32).reshape(1)
        positions = block_pos[0]
        in_shards = (w_query, w_key, w_value)
        gains = jnp.stack([gain_attn, gain_ffn])
        weights = (w_out, w_gate.T, w_up.T, w_down)
        narrow = HEADS * FDIM
        rows = tokens.shape[1]
        unit = 2 * rows * BLOCK * HEADS
        width = sum(a.shape[1] for a in in_shards)
        if count == 8:
            forward = forward_call(block_pos, tokens[0], gains, in_shards, weights)
            gains, query, key, value, prefix, atten, denom, middle, in_full, out_full, gates, ups, downs = forward
        else:
            in_shard = jnp.concatenate(in_shards, axis=1)
            gains, in_full = (lax.all_gather(a, "fsdp", axis=k, tiled=True) for k, a in ((1, gains), (0, in_shard)))
            gains = gains.astype(f32)
        gain_one, gain_two = gains[0], gains[1]
        in_full = in_full.reshape(-1, width)
        if count == 8:
            out_full = out_full.reshape(-1, w_out.shape[1])
        else:
            residual = tokens[0].astype(f32)
            inv_one = lax.rsqrt(jnp.mean(residual * residual, axis=-1, keepdims=True) + EPS)
            normed_one = (residual * inv_one * gain_one).astype(bf16)
            projected = dot(in_full, normed_one, (0, 1)).astype(bf16)
            query, key, value = projected[:narrow], projected[narrow : 2 * narrow], projected[2 * narrow :]
            (own_states,) = attention_call(
                states_kernel, ("narrow", "wide"), (("state", bf16),), rows, unit * FEAT
            )(key, value)
            numer, denom = attention_call(
                intra_kernel, ("narrow", "narrow", "wide"), (("wide", f32), ("head", f32)), rows, unit * 256
            )(query, key, value)
            links = Links()
            states = Exchange(own_states, positions, own, count, False)
            for _ in range(1, count // 2):
                states.passed(links.round([states.ring()])[0])
            prefix = states.total(links.round([states.partner()])[0])
            atten, denom = attention_call(
                inter_kernel,
                ("narrow", "state", "wide", "head"),
                (("wide", bf16), ("head", f32)),
                rows,
                unit * FEAT,
            )(query, prefix, numer, denom)
            out_full, downs = (lax.all_gather(w, "fsdp") for w in (w_out, w_down))
            gates, ups = (lax.all_gather(w, "fsdp", axis=1, tiled=True) for w in weights[1:3])
            out_full = out_full.reshape(-1, w_out.shape[1])
            middle = residual + dot(atten, out_full, (0, 0))
        ffn_inputs = (middle, gains, cotangent[0], gates, ups, downs)
        if count == 8:
            results = ffn_send_call(*ffn_inputs)
            output, grad_middle, branch, grad_gain_two = results[:4]
            gate_keep, up_keep, down_keep, second_cross, gate_got, up_got, down_got, first_cross = results[4:]
            arrays = dict(
                places=block_pos,
                gain_one=gains,
                ggain_two=grad_gain_two,
                out_full_hbm=out_full,
                branch_hbm=branch,
                atten_hbm=atten,
                denom_hbm=denom,
                query_hbm=query,
                key_hbm=key,
                value_hbm=value,
                prefix_hbm=prefix,
                tokens_hbm=tokens[0],
                in_full_hbm=in_full,
                gmiddle_hbm=grad_middle,
                down_keep=down_keep,
                down_got=down_got,
                first_cross=first_cross,
                second_cross=second_cross,
                gate_keep=gate_keep,
                gate_got=gate_got,
                up_keep=up_keep,
                up_got=up_got,
            )
            grad_tokens, down_sum, gate_sum, up_sum, out_sum, in_sum, small = backward_call(arrays)
            gain_sums = small[:4].reshape(2, -1)
        else:
            results = ffn_call(me, *ffn_inputs)
            output, grad_middle, branch, grad_gain_two = results[:4]
            pairs = [results[k : k + 2] for k in (8, 4, 6)]
            grad_atten = dot(out_full, branch, (1, 1))
            gnumer, gdenom, grad_states = attention_call(
                grad_states_kernel,
                ("narrow", "wide", "head", "wide"),
                (("wide", bf16), ("head", f32), ("state", bf16)),
                rows,
                unit * FEAT,
            )(query, atten, denom, grad_atten)
            gquery, gkey, gvalue = attention_call(
                intra_back_kernel,
                ("narrow", "narrow", "wide", "wide", "head", "state"),
                (("narrow", bf16), ("narrow", f32), ("wide", f32)),
                rows,
                unit * 512,
            )(query, key, value, gnumer, gdenom, prefix)
            links = Links()
            backward = Exchange(grad_states, positions, own, count, True)
            for _ in range(1, count // 2):
                backward.passed(links.round([backward.ring()])[0])
            later = backward.total(links.round([backward.partner()])[0])
            gkey, gvalue = attention_call(
                inter_back_kernel,
                ("narrow", "wide", "state", "narrow", "wide"),
                (("narrow", bf16), ("wide", bf16)),
                rows,
                unit * 256,
            )(key, value, later, gkey, gvalue)
            gprojected = jnp.concatenate([gquery, gkey, gvalue], axis=0)
            gnormed_one = dot(gprojected, in_full, (0, 1))
            weighted_one = gnormed_one * gain_one
            grad_gain_one = jnp.sum(gnormed_one * residual * inv_one, axis=0)
            grad_tokens = (
                grad_middle
                + inv_one * weighted_one
                - residual
                * (inv_one * inv_one * inv_one)
                * jnp.mean(weighted_one * residual, axis=-1, keepdims=True)
            )

            def summed(keep, send):
                got = lax.ppermute(send, "fsdp", CORE)
                cross = (keep[:, 1].astype(f32) + got[:, 1].astype(f32)).astype(bf16)
                got_cross = lax.ppermute(cross, "fsdp", CHIP)
                total = keep[:, 0].astype(f32) + got[:, 0].astype(f32) + got_cross.astype(f32)
                return lax.psum(total.astype(bf16), "ctx")

            def scattered(grad):
                return lax.psum(lax.psum_scatter(grad, "fsdp", scatter_dimension=0, tiled=True), "ctx")

            down_sum, gate_sum, up_sum = (summed(*pair) for pair in pairs)
            out_sum = scattered(dot(atten, branch, (1, 0)).astype(bf16)).reshape(8, -1, branch.shape[1])
            in_sum = scattered(dot(normed_one, gprojected, (0, 1)).astype(bf16)).reshape(8, -1, width)
            gain_sums = scattered(jnp.stack([grad_gain_one, grad_gain_two[0]], axis=1)).T
        down_grad, gate_grad, up_grad, out_grad, *in_grads, output, grad_tokens = settle_call(
            down_sum, gate_sum, up_sum, out_sum, in_sum, output, grad_tokens
        )
        return (
            output[None],
            grad_tokens[None],
            gain_sums[0],
            *in_grads,
            out_grad,
            gain_sums[1],
            gate_grad.T,
            up_grad.T,
            down_grad,
        )

    return layer


def solution(mesh):
    rows = P("fsdp", None)
    seqs = P("fsdp", "ctx", None)
    vec = P("fsdp")
    in_specs = (seqs, rows, vec, rows, rows, rows, rows, vec, rows, rows, rows, seqs)
    out_specs = (seqs, seqs, vec, rows, rows, rows, rows, vec, rows, rows, rows)
    return jax.shard_map(
        body(mesh.shape["ctx"]), mesh=mesh, in_specs=in_specs, out_specs=out_specs, check_vma=False
    )
```
